512 devices in a mesh: seq: 128 (over z, y_lo, x), col: 4 (over y_hi, core).
Axes of the slice: x: 4, y: 8 (y_hi: 2, y_lo: 4; y = y_hi * 4 + y_lo), z: 8, core: 2. Of those that a mesh axis runs over, the one named last changes fastest.
Arguments:
- atom_inputs: bfloat16 [24576, 128], P('seq'), may hold values from -6 to 6
- atom_token: int32 [24576], P('seq'), may hold values from -1 to 2047, as said below
- counts: int32 [2048], P('seq'), may hold values from 1 to 12, as said below
- window_start: int32 [768], P('seq'), may hold values from -64 to 24512, as said below
- pair_features: bfloat16 [2048, 2048, 128], P('seq', 'col'), may hold values from -6 to 6
- w_query: bfloat16 [128, 128], P(None, 'col'), may hold values from -0.5 to 0.5
- w_key: bfloat16 [128, 128], P(None, 'col'), may hold values from -0.5 to 0.5
- w_value: bfloat16 [128, 128], P(None, 'col'), may hold values from -0.5 to 0.5
- w_out: bfloat16 [128, 128], P('col'), may hold values from -0.5 to 0.5
- w_bias: bfloat16 [128, 4], replicated, as said below
- atom_cotangent: bfloat16 [24576, 128], P('seq'), may hold values from -6 to 6
- token_cotangent: bfloat16 [2048, 128], P('seq'), may hold values from -24 to 24
Outputs:
- grad_atoms: bfloat16 [24576, 128], P('seq', 'col')
- grad_pair: bfloat16 [2048, 2048, 128], P('seq', 'col')
- grad_w_query: float32 [128, 128], P(None, 'col')
- grad_w_key: float32 [128, 128], P(None, 'col')
- grad_w_value: float32 [128, 128], P(None, 'col')
- grad_w_out: float32 [128, 128], P('col')
- grad_w_bias: float32 [128, 4], P(None, 'col')
The draws below stay inside these ranges and needn't reach their ends.
Inputs may be any that keep to these rules, and one draw needn't show every extreme that they name: `counts`: each token has 1 to 12 atoms; in every draw all 16 tokens of some range d (tokens d * 16 to (d + 1) * 16 - 1) have 12 atoms. `atom_token`: slots d * 192 to (d + 1) * 192 - 1 hold, from the first on, counts[t] consecutive slots for each token t of range d in order; the remaining slots of the range are -1. window_start[j] = j * 32 - 64 + r with r from 0 to 32; both ends of r occur in every draw. `w_bias`: every entry lies between -0.25 and 0.25.
All inputs are finite; a program needn't handle non-finite values.
Results may differ from the reference program's by a relative error of at most 0.015.
Values may be sent and summed in bfloat16 or wider, within the bound.
No kernel may reach another device: no remote copies, remote signals or barrier semaphores. Data moves between devices by JAX's collectives and lax.ppermute only.
A program may use at most 64 MiB of HBM per device.

```python
import math
import jax
import jax.numpy as jnp
from jax import lax

ATOM_WIDTH = 128
PAIR_WIDTH = 128
HEADS = 4
HEAD_DIM = 32
QUERY_BLOCK = 32
KEY_WINDOW = 128
REACH = 64
MAX_ATOMS = 12
TOK_DEV = 16
ATOM_DEV = 192
TOKENS = 2048
ATOMS = 24576
BLOCKS = 768


def layout_counts(key):
    base_key = jax.random.fold_in(key, 11)
    group_count = TOKENS // TOK_DEV
    high_key, busy_key, count_key = jax.random.split(base_key, 3)
    high_counts = jax.random.randint(high_key, (group_count, 1), 4, MAX_ATOMS + 1)
    busiest = jax.random.randint(busy_key, (), 0, group_count)
    spread_bits = jax.random.randint(count_key, (group_count, TOK_DEV), 0, 1 << 20)
    per_token = 1 + spread_bits % high_counts
    per_token = jnp.where(jnp.arange(group_count)[:, None] == busiest, MAX_ATOMS, per_token)
    return per_token.astype(jnp.int32)


def draw_counts(key, part):
    return layout_counts(key).reshape(TOKENS).astype(jnp.int32)


def draw_atom_token(key, part):
    per_token = layout_counts(key)
    group_count = per_token.shape[0]
    token_ends = jnp.cumsum(per_token, axis=1)
    slot_iota = jnp.arange(ATOM_DEV, dtype=jnp.int32)
    local_token = jnp.sum((token_ends[:, None, :] <= slot_iota[None, :, None]).astype(jnp.int32), axis=2)
    token_base = (jnp.arange(group_count, dtype=jnp.int32) * TOK_DEV)[:, None]
    result = jnp.where(local_token < TOK_DEV, local_token + token_base, -1)
    return result.reshape(ATOMS).astype(jnp.int32)


def draw_window_start(key, part):
    base_key = jax.random.fold_in(key, 29)
    shift_key, first_key, second_key = jax.random.split(base_key, 3)
    spare = 2 * REACH + QUERY_BLOCK - KEY_WINDOW
    shifts = jax.random.randint(shift_key, (BLOCKS,), 0, spare + 1)
    first_pick = jax.random.randint(first_key, (), 0, BLOCKS)
    second_pick = (first_pick + 1 + jax.random.randint(second_key, (), 0, BLOCKS - 1)) % BLOCKS
    block_iota = jnp.arange(BLOCKS, dtype=jnp.int32)
    shifts = jnp.where(block_iota == first_pick, 0, shifts)
    shifts = jnp.where(block_iota == second_pick, spare, shifts)
    shifts = jnp.where(block_iota == 0, 0, shifts)
    shifts = jnp.where(block_iota == BLOCKS - 1, spare, shifts)
    return (block_iota * QUERY_BLOCK - REACH + shifts).astype(jnp.int32)


def bias_weight_values(key):
    base_key = jax.random.fold_in(key, 41)
    normal_key = jax.random.fold_in(base_key, 2)
    spread = min(PAIR_WIDTH ** (-0.5), 0.1)
    values = jax.random.normal(normal_key, (PAIR_WIDTH, HEADS), jnp.float32) * spread
    return jnp.clip(values, -0.25, 0.25)


def draw_w_bias(key, part):
    return bias_weight_values(key).astype(jnp.bfloat16)


def draw_pair_features(key, part):
    base_key = jax.random.fold_in(key, 53)
    value_key = jax.random.fold_in(base_key, 0)
    result = jnp.clip(jax.random.normal(value_key, (TOKENS, TOKENS, PAIR_WIDTH), jnp.float32), -6.0, 6.0)
    return result.astype(jnp.bfloat16)


def levels(rng, extent, pieces, smallest, high):
    def one(position, parts):
        steps = jax.random.uniform(jax.random.fold_in(jax.random.fold_in(rng, 6), position), (parts,), jnp.float32, smallest / len(pieces), high / len(pieces))
        return jnp.repeat(jnp.exp(steps), extent[position] // parts).reshape((-1,) + (1,) * (len(extent) - position - 1))

    loudness = one(*pieces[0])
    for cut in pieces[1:]:
        loudness = loudness * one(*cut)
    return loudness


def scatter_about(key, shape, scale, bound, cuts=(), held_as=jnp.bfloat16):
    values = jax.random.normal(key, shape, jnp.float32) * scale
    if len(cuts) > 0:
        values = levels(key, shape, cuts, -0.22, 0.18) * values
    return jnp.clip(values, min=-bound, max=bound).astype(held_as)


def setup_inputs(seed: int = 0) -> dict:
    splits = jax.random.split(jax.random.key(seed), 13)
    atom_inputs = scatter_about(splits[0], (ATOMS, ATOM_WIDTH), 1.0, 6.0, ((0, 128),))
    atom_token = draw_atom_token(jax.random.fold_in(splits[12], 71), 0)
    counts = draw_counts(jax.random.fold_in(splits[12], 71), 0)
    window_start = draw_window_start(jax.random.fold_in(splits[12], 71), 0)
    pair_features = draw_pair_features(jax.random.fold_in(splits[12], 71), 0)
    w_query = scatter_about(splits[5], (ATOM_WIDTH, ATOM_WIDTH), ATOM_WIDTH ** -0.5, 0.5, ((1, 4),))
    w_key = scatter_about(splits[6], (ATOM_WIDTH, ATOM_WIDTH), ATOM_WIDTH ** -0.5, 0.5, ((1, 4),))
    w_value = scatter_about(splits[7], (ATOM_WIDTH, ATOM_WIDTH), ATOM_WIDTH ** -0.5, 0.5, ((1, 4),))
    w_out = scatter_about(splits[8], (ATOM_WIDTH, ATOM_WIDTH), ATOM_WIDTH ** -0.5, 0.5, ((0, 4),))
    w_bias = draw_w_bias(jax.random.fold_in(splits[12], 71), 0)
    atom_cotangent = scatter_about(splits[10], (ATOMS, ATOM_WIDTH), 1.0, 6.0, ((0, 128),))
    token_cotangent = scatter_about(splits[11], (TOKENS, ATOM_WIDTH), 4.0, 24.0, ((0, 128),))
    return {"atom_inputs": atom_inputs, "atom_token": atom_token, "counts": counts, "window_start": window_start, "pair_features": pair_features, "w_query": w_query, "w_key": w_key, "w_value": w_value, "w_out": w_out, "w_bias": w_bias, "atom_cotangent": atom_cotangent, "token_cotangent": token_cotangent}


def reference(atom_inputs, atom_token, counts, window_start, pair_features, w_query, w_key, w_value, w_out, w_bias, atom_cotangent, token_cotangent):
    top_precision = lax.Precision.HIGHEST
    inv_root = 1.0 / math.sqrt(HEAD_DIM)
    queries = jnp.dot(atom_inputs, w_query, preferred_element_type=jnp.float32).astype(jnp.bfloat16)
    keys_all = jnp.dot(atom_inputs, w_key, preferred_element_type=jnp.float32).astype(jnp.bfloat16)
    values_all = jnp.dot(atom_inputs, w_value, preferred_element_type=jnp.float32).astype(jnp.bfloat16)
    slot_live = atom_token >= 0
    safe_token = jnp.maximum(atom_token, 0)
    count_per_atom = counts[safe_token].astype(jnp.float32)
    pooled_back = token_cotangent[safe_token].astype(jnp.float32) / count_per_atom[:, None]
    upstream = jnp.where(slot_live[:, None], atom_cotangent.astype(jnp.float32) + pooled_back, 0.0).astype(jnp.bfloat16)
    grad_attended = jnp.dot(upstream, w_out.T, preferred_element_type=jnp.float32).astype(jnp.bfloat16)
    bias_weight = w_bias.astype(jnp.float32)
    window_iota = jnp.arange(KEY_WINDOW, dtype=jnp.int32)
    query_iota = jnp.arange(QUERY_BLOCK, dtype=jnp.int32)

    def one_block(block_index):
        query_rows = block_index * QUERY_BLOCK + query_iota
        key_rows = window_start[block_index] + window_iota
        inside = (key_rows >= 0) & (key_rows < ATOMS)
        safe_rows = jnp.clip(key_rows, 0, ATOMS - 1).astype(jnp.int32)
        key_token = jnp.where(inside, atom_token[safe_rows], -1)
        query_token = atom_token[query_rows]
        key_live = key_token >= 0
        query_live = query_token >= 0
        allowed = key_live[None, :] | jnp.logical_not(query_live)[:, None]
        both_live = query_live[:, None] & key_live[None, :]
        pair_rows = pair_features[jnp.maximum(query_token, 0)[:, None], jnp.maximum(key_token, 0)[None, :]]
        bias_per_block = jnp.einsum('qkc,ch->hqk', pair_rows.astype(jnp.float32), bias_weight, precision=top_precision)
        bias_per_block = jnp.where(both_live[None], bias_per_block, 0.0)
        queries_per_block = queries[query_rows].astype(jnp.float32).reshape(QUERY_BLOCK, HEADS, HEAD_DIM)
        keys_per_block = jnp.where(inside[:, None], keys_all[safe_rows].astype(jnp.float32), 0.0).reshape(KEY_WINDOW, HEADS, HEAD_DIM)
        values_per_block = jnp.where(inside[:, None], values_all[safe_rows].astype(jnp.float32), 0.0).reshape(KEY_WINDOW, HEADS, HEAD_DIM)
        scores = jnp.einsum('qhd,khd->hqk', queries_per_block, keys_per_block, precision=top_precision) * inv_root + bias_per_block
        masked = jnp.where(allowed[None], scores, -1e+30)
        row_max = lax.optimization_barrier(jnp.max(masked, axis=-1, keepdims=True))
        raw_weights = jnp.where(allowed[None], jnp.exp(masked - row_max), 0.0)
        weights = raw_weights / lax.optimization_barrier(jnp.sum(raw_weights, axis=-1, keepdims=True))
        reduced_weights = lax.optimization_barrier(weights.astype(jnp.bfloat16)).astype(jnp.float32)
        attended = jnp.einsum('hqk,khd->qhd', reduced_weights, values_per_block, precision=top_precision).astype(jnp.bfloat16)
        gradient_per_block = grad_attended[query_rows].astype(jnp.float32).reshape(QUERY_BLOCK, HEADS, HEAD_DIM)
        grad_weights = jnp.einsum('qhd,khd->hqk', gradient_per_block, values_per_block, precision=top_precision)
        score_gradient = weights * (grad_weights - lax.optimization_barrier(jnp.sum(weights * grad_weights, axis=-1, keepdims=True)))
        reduced_scores = lax.optimization_barrier(score_gradient.astype(jnp.bfloat16)).astype(jnp.float32)
        grad_queries = jnp.einsum('hqk,khd->qhd', reduced_scores, keys_per_block, precision=top_precision) * inv_root
        key_terms = jnp.einsum('hqk,qhd->khd', reduced_scores, queries_per_block, precision=top_precision) * inv_root
        value_terms = jnp.einsum('hqk,qhd->khd', reduced_weights, gradient_per_block, precision=top_precision)
        kept_scores = jnp.where(both_live[None], score_gradient, 0.0)
        return (attended.reshape(QUERY_BLOCK, ATOM_WIDTH), grad_queries.reshape(QUERY_BLOCK, ATOM_WIDTH), key_terms.reshape(KEY_WINDOW, ATOM_WIDTH), value_terms.reshape(KEY_WINDOW, ATOM_WIDTH), jnp.transpose(kept_scores, (1, 2, 0)), jnp.maximum(query_token, 0), jnp.maximum(key_token, 0), safe_rows, inside)
    outputs = lax.map(one_block, jnp.arange(BLOCKS, dtype=jnp.int32))
    attended_blocks, query_grads, key_blocks, value_blocks, score_blocks, query_tokens, key_tokens, row_blocks, inside_blocks = outputs
    attended = attended_blocks.reshape(ATOMS, ATOM_WIDTH)
    grad_queries = query_grads.reshape(ATOMS, ATOM_WIDTH)
    flat_rows = row_blocks.reshape(-1)
    keep_rows = inside_blocks.reshape(-1)[:, None]
    grad_keys = jnp.zeros((ATOMS, ATOM_WIDTH), jnp.float32).at[flat_rows].add(jnp.where(keep_rows, key_blocks.reshape(-1, ATOM_WIDTH), 0.0))
    grad_values = jnp.zeros((ATOMS, ATOM_WIDTH), jnp.float32).at[flat_rows].add(jnp.where(keep_rows, value_blocks.reshape(-1, ATOM_WIDTH), 0.0))
    flat_pairs = (query_tokens[:, :, None] * TOKENS + key_tokens[:, None, :]).reshape(-1)
    token_bias_grad = jnp.zeros((TOKENS * TOKENS, HEADS), jnp.float32).at[flat_pairs].add(score_blocks.reshape(-1, HEADS))
    token_bias_grad = token_bias_grad.reshape(TOKENS, TOKENS, HEADS)

    def pair_rows_block(group_index):
        row_start = group_index * TOK_DEV
        grad_rows = lax.dynamic_slice_in_dim(token_bias_grad, row_start, TOK_DEV, 0)
        pair_rows = lax.dynamic_slice_in_dim(pair_features, row_start, TOK_DEV, 0).astype(jnp.float32)
        pair_grad = jnp.einsum('tsh,ch->tsc', grad_rows, bias_weight, precision=top_precision).astype(jnp.bfloat16)
        weight_part = jnp.einsum('tsc,tsh->ch', pair_rows, grad_rows, precision=top_precision)
        return (pair_grad, weight_part)
    pair_blocks, weight_parts = lax.map(pair_rows_block, jnp.arange(TOKENS // TOK_DEV, dtype=jnp.int32))
    grad_pair = pair_blocks.reshape(TOKENS, TOKENS, PAIR_WIDTH)
    grad_w_bias = lax.optimization_barrier(jnp.sum(weight_parts, axis=0))
    inputs_wide = atom_inputs.astype(jnp.float32)
    grad_w_query = jnp.dot(inputs_wide.T, grad_queries, precision=top_precision)
    grad_w_key = jnp.dot(inputs_wide.T, grad_keys, precision=top_precision)
    grad_w_value = jnp.dot(inputs_wide.T, grad_values, precision=top_precision)
    grad_w_out = jnp.dot(attended.T, upstream, preferred_element_type=jnp.float32)
    grad_atoms = (upstream.astype(jnp.float32) + jnp.dot(grad_queries, w_query.astype(jnp.float32).T, precision=top_precision) + jnp.dot(grad_keys, w_key.astype(jnp.float32).T, precision=top_precision) + jnp.dot(grad_values, w_value.astype(jnp.float32).T, precision=top_precision)).astype(jnp.bfloat16)
    return (grad_atoms, grad_pair, grad_w_query, grad_w_key, grad_w_value, grad_w_out, grad_w_bias)
```

```python
import math

import jax
import jax.numpy as jnp
from jax import lax
from jax.experimental import pallas as pl
from jax.experimental.pallas import tpu as pltpu
from jax.sharding import PartitionSpec as P

QUERY_BLOCK = 32
KEY_WINDOW = 128
REACH = 64
SUB = 16
BAND = 64
GROUP = 96
SPAN = GROUP + 2 * REACH
HEADS = 4
HALO_ROWS = REACH + 16
VMEM_LIMIT = 32 * 1024 * 1024
F32 = jnp.float32
BF16 = jnp.bfloat16

NN = (((1,), (0,)), ((), ()))
NT = (((1,), (1,)), ((), ()))
TN = (((0,), (0,)), ((), ()))


def mm(a, b, dims=NN):
    return lax.dot_general(a, b, dims, preferred_element_type=F32)


def halves(x):
    high = x.astype(BF16)
    return high, (x - high.astype(F32)).astype(BF16)


def mm2(a, b, dims=NN):
    high, low = halves(a)
    return mm(high, b, dims) + mm(low, b, dims)


def band_copies(index_ref, pair_ref, band, sems):
    width = pair_ref.shape[1]
    copies = []
    for part in range(3):
        start = (index_ref[0] + part - 1) * SUB - index_ref[1] * width
        own = jnp.logical_and(start >= 0, start < width)
        safe = pl.multiple_of(jnp.clip(start, 0, width - SUB), SUB)
        copy = pltpu.make_async_copy(
            pair_ref.at[:, pl.ds(safe, SUB), :],
            band.at[:, pl.ds(part * SUB, SUB), :],
            sems.at[part],
        )
        copies.append((own, safe, copy))
    return copies


def start_band(copies, band):
    tokens = band.shape[0]
    band[:, 3 * SUB :, :] = jnp.zeros((tokens, BAND - 3 * SUB, band.shape[2]), BF16)
    for part, (own, _, copy) in enumerate(copies):

        @pl.when(own)
        def _(copy=copy):
            copy.start()

        @pl.when(jnp.logical_not(own))
        def _(part=part):
            band[:, part * SUB : (part + 1) * SUB, :] = jnp.zeros((tokens, SUB, band.shape[2]), BF16)


def wait_all(copies):
    for own, _, copy in copies:

        @pl.when(own)
        def _(copy=copy):
            copy.wait()


def bias_rows(w_bias):
    wide = jnp.concatenate([w_bias.astype(F32), jnp.zeros((w_bias.shape[0], 124), F32)], axis=1)
    return wide.T[:8]


def pack_kernel(
    index_ref,
    pair_ref,
    wq_ref,
    wk_ref,
    wv_ref,
    wo_ref,
    wb_ref,
    pack_ref,
    grad_pair_ref,
    band,
    zeros,
    bias,
    band_sems,
    zero_sems,
):
    copies = band_copies(index_ref, pair_ref, band, band_sems)
    start_band(copies, band)
    zeros[...] = jnp.zeros(zeros.shape, BF16)
    tokens = band.shape[0]
    fills = [
        pltpu.make_async_copy(zeros, grad_pair_ref.at[t], zero_sems.at[t]) for t in range(tokens)
    ]
    for fill in fills:
        fill.start()
    head = wq_ref.shape[1]
    joined = jnp.concatenate(
        [wq_ref[...].astype(F32), wk_ref[...].astype(F32), wv_ref[...].astype(F32)]
        + [jnp.zeros((wq_ref.shape[0], head), F32)],
        axis=1,
    ).T
    weights = jnp.concatenate([joined[: 3 * head].astype(BF16), wo_ref[...]], axis=0)
    rows = bias_rows(wb_ref[...]).astype(BF16)
    wait_all(copies)
    for t in range(tokens):
        part = mm(rows, band[t], NT)
        high = part.astype(BF16).astype(F32)
        bias[8 * t : 8 * t + 8, :] = jnp.concatenate([high, part - high], axis=1)
    packed = jnp.concatenate([weights, bias[...].astype(BF16)], axis=0)
    for c in range(HEADS):
        pack_ref[c] = packed
    for fill in fills:
        fill.wait()


def attention_kernel(
    index_ref,
    window_ref,
    pair_ref,
    grad_in_ref,
    recv_ref,
    below_ref,
    own_ref,
    above_ref,
    token_row_ref,
    token_col_ref,
    counts_ref,
    atom_cot_ref,
    token_cot_ref,
    wb_ref,
    pay_ref,
    rim_down_ref,
    rim_up_ref,
    own_out_ref,
    grad_pair_ref,
    band,
    main,
    grad_band,
    band_sems,
    out_sems,
):
    del grad_in_ref
    copies = band_copies(index_ref, pair_ref, band, band_sems)
    start_band(copies, band)
    seq, col = index_ref[0], index_ref[1]
    atoms = own_ref.shape[0]
    width = own_ref.shape[1]
    tokens = band.shape[0]
    head = width // HEADS
    inv_root = 1.0 / math.sqrt(head)
    slot_base = seq * atoms
    token_base = seq * tokens

    def gathered(first, count):
        return jnp.concatenate([recv_ref[c, first : first + count, :] for c in range(HEADS)], axis=0)

    wq_t, wk_t, wv_t, wo = (gathered(i * head, head) for i in range(4))
    bias = recv_ref[0, 4 * head :, :].astype(F32)
    for c in range(1, HEADS):
        bias = bias + recv_ref[c, 4 * head :, :].astype(F32)
    bias = bias.astype(BF16)

    own = own_ref[...]
    ext = jnp.concatenate([below_ref[:REACH, :], own, above_ref[:REACH, :]], axis=0)
    queries = mm(own, wq_t, NT).astype(BF16)
    keys = mm(ext, wk_t, NT).astype(BF16)
    values = mm(ext, wv_t, NT).astype(BF16)

    token_col = token_col_ref[...]
    live_col = token_col >= 0
    local_col = token_col - token_base
    token_lanes = lax.broadcasted_iota(jnp.int32, (atoms, tokens), 1)
    onehot = (local_col == token_lanes).astype(F32)
    pooled = mm(onehot.astype(BF16), token_cot_ref[...])
    count = jnp.sum(onehot * counts_ref[...].astype(F32), axis=1, keepdims=True)
    safe_count = jnp.where(live_col, count, 1.0)
    upstream = jnp.where(live_col, atom_cot_ref[...].astype(F32) + pooled / safe_count, 0.0)
    upstream = upstream.astype(BF16)
    grad_attended = mm(upstream, wo, NT).astype(BF16)

    def halo_tokens(ref):
        row = ref[REACH : REACH + 16, :].astype(F32)[:1]
        return (row[:, :REACH] * 64.0 + row[:, REACH:]).astype(jnp.int32) - 1

    own_row = token_row_ref[...]
    key_rows = (
        jnp.concatenate([halo_tokens(below_ref), own_row[:, : SPAN - REACH]], axis=1),
        jnp.concatenate([own_row[:, atoms - (SPAN - REACH) :], halo_tokens(above_ref)], axis=1),
    )
    head_lanes = lax.broadcasted_iota(jnp.int32, (GROUP, width), 1) // head
    head_masks = [head_lanes == h for h in range(HEADS)]

    def stacked(x):
        return jnp.concatenate(
            [jnp.where(mask, x, jnp.zeros_like(x)) for mask in head_masks], axis=0
        )

    def folded(x):
        total = jnp.where(head_masks[0], x[:GROUP], 0.0)
        for h in range(1, HEADS):
            total = total + jnp.where(head_masks[h], x[h * GROUP : (h + 1) * GROUP], 0.0)
        return total

    attended, grad_queries, key_terms, value_terms = [], [], [], []
    token_grad = jnp.zeros((tokens * 8, width), F32)
    for g in range(atoms // GROUP):
        rows = slice(g * GROUP, (g + 1) * GROUP)
        span = slice(g * GROUP, g * GROUP + SPAN)
        k_g, v_g = keys[span], values[span]
        q_m = stacked(queries[rows].astype(F32)).astype(BF16)
        a_m = stacked(grad_attended[rows].astype(F32)).astype(BF16)
        key_token = key_rows[g]
        key_live = key_token >= 0
        key_band = jnp.where(key_live, key_token - (token_base - tokens), -1000)
        lane_band = lax.broadcasted_iota(jnp.int32, (width, SPAN), 0)
        key_onehot = ((lane_band & (REACH - 1)) == key_band).astype(F32).astype(BF16)
        local = local_col[rows]
        slot = lax.broadcasted_iota(jnp.int32, (GROUP, tokens * 8), 1)
        query_onehot = jnp.concatenate(
            [(slot == local * 8 + h).astype(F32) for h in range(HEADS)], axis=0
        ).astype(BF16)
        picked = mm(query_onehot, bias).astype(BF16)
        scores = mm(q_m, k_g, NT) * inv_root + mm(picked, key_onehot)
        scores = scores.reshape(HEADS, GROUP, SPAN)
        block = lax.broadcasted_iota(jnp.int32, (GROUP, 1), 0) // QUERY_BLOCK
        base = slot_base - REACH + g * GROUP
        first = g * (GROUP // QUERY_BLOCK)
        start = jnp.where(
            block == 0,
            window_ref[first] - base,
            jnp.where(block == 1, window_ref[first + 1] - base, window_ref[first + 2] - base),
        )
        position = lax.broadcasted_iota(jnp.int32, (GROUP, SPAN), 1)
        inside = (position >= start) & (position < start + KEY_WINDOW)
        dead_query = local < 0
        allowed = inside & (key_live | dead_query)
        masked = jnp.where(allowed[None], scores, -1e30)
        row_max = jnp.max(masked, axis=-1, keepdims=True)
        raw = jnp.where(allowed[None], jnp.exp(masked - row_max), 0.0)
        weights = raw / jnp.sum(raw, axis=-1, keepdims=True)
        grad_weights = mm(a_m, v_g, NT).reshape(HEADS, GROUP, SPAN)
        inner = jnp.sum(weights * grad_weights, axis=-1, keepdims=True)
        grad_scores = (weights * (grad_weights - inner)).reshape(HEADS * GROUP, SPAN)
        w_low = weights.reshape(HEADS * GROUP, SPAN).astype(BF16)
        s_high, s_low = halves(grad_scores)
        attended.append(folded(mm(w_low, v_g)))
        grad_queries.append(folded(mm(s_high, k_g)) * inv_root)
        key_terms.append(mm(s_high, q_m, TN) * inv_root)
        value_terms.append(mm(w_low, a_m, TN))
        by_token = mm(query_onehot, s_high, TN) + mm(query_onehot, s_low, TN)
        token_grad = token_grad + mm2(by_token, key_onehot, NT)

    attended = jnp.concatenate(attended, axis=0).astype(BF16)
    grad_q = jnp.concatenate(grad_queries, axis=0)

    def overlapped(terms):
        lap = SPAN - GROUP
        return jnp.concatenate(
            [terms[0][:GROUP], terms[0][GROUP:] + terms[1][:lap], terms[1][lap:]], axis=0
        )

    grad_k = overlapped(key_terms)
    grad_v = overlapped(value_terms)

    rows = bias_rows(wb_ref[...])
    turned = token_grad.T[: 3 * SUB]
    for t in range(tokens):
        total = turned[:, 8 * t : 8 * t + 1] * rows[0:1]
        for h in range(1, HEADS):
            total = total + turned[:, 8 * t + h : 8 * t + h + 1] * rows[h : h + 1]
        grad_band[t] = total.astype(BF16)
    outs = []
    for part, (own_part, safe, _) in enumerate(copies):
        copy = pltpu.make_async_copy(
            grad_band.at[:, pl.ds(part * SUB, SUB), :],
            grad_pair_ref.at[:, pl.ds(safe, SUB), :],
            out_sems.at[part],
        )
        outs.append((own_part, safe, copy))

        @pl.when(own_part)
        def _(copy=copy):
            copy.start()

    plane = pay_ref.shape[0] // HEADS
    chunk = width // plane
    products = (
        mm2(grad_q, own, TN),
        mm2(grad_k, ext, TN),
        mm2(grad_v, ext, TN),
        mm(attended, upstream, TN),
    )
    per_product = head // chunk
    for i, product in enumerate(products):
        for c in range(HEADS):
            for j in range(per_product):
                to = ((i * per_product + j) * HEADS + c) * chunk
                at = c * head + j * chunk
                main[to : to + chunk, :] = product[at : at + chunk]
    wait_all(copies)
    w_bias_grad = jnp.zeros((8, width), F32)
    for t in range(tokens):
        w_bias_grad = w_bias_grad + mm2(token_grad[8 * t : 8 * t + 8, :BAND], band[t])
    spread = w_bias_grad + pltpu.roll(w_bias_grad, 4, 0)
    share = chunk // HEADS
    for j in range(share):
        pay_ref[:, j * width : (j + 1) * width] = main[
            pl.ds(col * share + j, plane * HEADS, stride=chunk), :
        ]
    pay_ref[:, share * width :] = jnp.concatenate([spread] * (plane * HEADS // 8), axis=0)

    key_part = mm2(grad_k, wk_t) + mm2(grad_v, wv_t)
    query_part = mm2(grad_q, wq_t) + upstream.astype(F32)
    shift = lax.rem(width - col * head, width)
    own_part = pltpu.roll(key_part[REACH : REACH + atoms] + query_part, shift, 1)
    own_out_ref[...] = own_part[:, :head]
    rim_down_ref[...] = pltpu.roll(key_part[:REACH], shift, 1)[:, :head].astype(BF16)
    rim_up_ref[...] = pltpu.roll(key_part[REACH + atoms :], shift, 1)[:, :head].astype(BF16)
    wait_all(outs)


def final_kernel(
    main_ref,
    bias_ref,
    own_ref,
    below_ref,
    above_ref,
    atoms_ref,
    gq_ref,
    gk_ref,
    gv_ref,
    go_ref,
    gb_ref,
):
    head = atoms_ref.shape[1]
    rows = atoms_ref.shape[0]
    edge = below_ref.shape[0]
    own = own_ref[...]
    atoms_ref[...] = jnp.concatenate(
        [
            own[:edge] + below_ref[...].astype(F32),
            own[edge : rows - edge],
            own[rows - edge :] + above_ref[...].astype(F32),
        ],
        axis=0,
    ).astype(BF16)
    turned = main_ref[...].T
    gq_ref[...] = turned[:, :head]
    gk_ref[...] = turned[:, head : 2 * head]
    gv_ref[...] = turned[:, 2 * head : 3 * head]
    go_ref[...] = main_ref[3 * head :, :]
    gb_ref[...] = jnp.broadcast_to(bias_ref[...], (8, bias_ref.shape[1])).T[:, :1]


def vmem():
    return pl.BlockSpec(memory_space=pltpu.VMEM)


def smem():
    return pl.BlockSpec(memory_space=pltpu.SMEM)


def anywhere():
    return pl.BlockSpec(memory_space=pl.ANY)


def shape(dims, dtype):
    return jax.ShapeDtypeStruct(dims, dtype)


PARAMS = pltpu.CompilerParams(vmem_limit_bytes=VMEM_LIMIT)


def per_device(
    atom_inputs,
    atom_token,
    counts,
    window_start,
    pair_features,
    w_query,
    w_key,
    w_value,
    w_out,
    w_bias,
    atom_cotangent,
    token_cotangent,
):
    atoms, width = atom_inputs.shape
    tokens, columns, _ = pair_features.shape
    head = w_query.shape[1]
    seqs = lax.axis_size("seq")
    plane = 16 if seqs % 16 == 0 else 4
    planes = seqs // plane
    index = jnp.stack([lax.axis_index("seq"), lax.axis_index("col")]).astype(jnp.int32)
    up = [(i, i + 1) for i in range(seqs - 1)]
    down = [(i + 1, i) for i in range(seqs - 1)]

    def edge(rows, token):
        code = token + 1
        line = jnp.concatenate([code // 64, code % 64]).astype(BF16)[None]
        return jnp.concatenate([rows, line, jnp.zeros((15, width), BF16)], axis=0)

    below = lax.ppermute(edge(atom_inputs[atoms - REACH :], atom_token[atoms - REACH :]), "seq", up)
    above = lax.ppermute(edge(atom_inputs[:REACH], atom_token[:REACH]), "seq", down)

    pack, grad_pair = pl.pallas_call(
        pack_kernel,
        out_shape=(shape((HEADS, 2 * width, width), BF16), shape(pair_features.shape, BF16)),
        in_specs=[smem(), anywhere()] + [vmem()] * 5,
        out_specs=(vmem(), anywhere()),
        scratch_shapes=[
            pltpu.VMEM((tokens, BAND, width), BF16),
            pltpu.VMEM((columns, width), BF16),
            pltpu.VMEM((tokens * 8, width), F32),
            pltpu.SemaphoreType.DMA((3,)),
            pltpu.SemaphoreType.DMA((tokens,)),
        ],
        compiler_params=PARAMS,
        name="pack",
    )(index, pair_features, w_query, w_key, w_value, w_out, w_bias)
    recv = lax.all_to_all(pack, "col", 0, 0, tiled=True)

    chunk = width // plane
    share = chunk // HEADS
    pay, rim_down, rim_up, own_part, grad_pair = pl.pallas_call(
        attention_kernel,
        out_shape=(
            shape((plane * HEADS, (share + 1) * width), F32),
            shape((REACH, head), BF16),
            shape((REACH, head), BF16),
            shape((atoms, head), F32),
            shape(pair_features.shape, BF16),
        ),
        in_specs=[smem(), smem(), anywhere(), anywhere()] + [vmem()] * 10,
        out_specs=(vmem(), vmem(), vmem(), vmem(), anywhere()),
        scratch_shapes=[
            pltpu.VMEM((tokens, BAND, width), BF16),
            pltpu.VMEM((HEADS * width, width), F32),
            pltpu.VMEM((tokens, 3 * SUB, width), BF16),
            pltpu.SemaphoreType.DMA((3,)),
            pltpu.SemaphoreType.DMA((3,)),
        ],
        input_output_aliases={3: 4},
        compiler_params=PARAMS,
        name="attention",
    )(
        index,
        window_start,
        pair_features,
        grad_pair,
        recv,
        below,
        atom_inputs,
        above,
        atom_token[None, :],
        atom_token[:, None],
        counts[None, :],
        atom_cotangent,
        token_cotangent,
        w_bias,
    )
    from_above = lax.ppermute(rim_down, "seq", down)
    from_below = lax.ppermute(rim_up, "seq", up)

    cols = lax.axis_size("col")
    whole_planes = [
        [(z * plane + i) * cols + c for i in range(plane) for c in range(cols)]
        for z in range(planes)
    ]
    across = [[z * plane + i for z in range(planes)] for i in range(plane)]
    within = [[z * plane + i for i in range(plane)] for z in range(planes)]
    first = lax.all_to_all(
        pay[:, None, :], ("seq", "col"), 0, 0, tiled=True, axis_index_groups=whole_planes
    )
    summed = first.reshape(plane, HEADS, (share + 1) * width).sum(axis=0)
    mains = summed[:, : share * width].reshape(1, chunk * width)
    tail = summed[:, share * width :].sum(axis=0, keepdims=True)
    joined = jnp.concatenate([mains, tail], axis=1)
    second = lax.all_to_all(
        jnp.broadcast_to(joined[None], (planes, 1, joined.shape[1])),
        "seq",
        0,
        0,
        tiled=True,
        axis_index_groups=across,
    ).sum(axis=0)
    third = lax.all_to_all(
        jnp.broadcast_to(second[None, :, : chunk * width], (plane, 1, chunk * width)),
        "seq",
        0,
        0,
        tiled=True,
        axis_index_groups=within,
    )
    return pl.pallas_call(
        final_kernel,
        out_shape=(
            shape((atoms, head), BF16),
            shape((width, head), F32),
            shape((width, head), F32),
            shape((width, head), F32),
            shape((head, width), F32),
            shape((width, 1), F32),
        ),
        in_specs=[vmem()] * 5,
        out_specs=(vmem(),) * 6,
        compiler_params=PARAMS,
        name="final",
    )(
        third.reshape(width, width),
        second[:, chunk * width :],
        own_part,
        from_below,
        from_above,
    ), grad_pair


def ordered(*args):
    (grad_atoms, *weights), grad_pair = per_device(*args)
    return (grad_atoms, grad_pair, *weights)


def solution(mesh):
    placed = (
        P("seq", None),
        P("seq"),
        P("seq"),
        P("seq"),
        P("seq", "col", None),
        P(None, "col"),
        P(None, "col"),
        P(None, "col"),
        P("col", None),
        P(),
        P("seq", None),
        P("seq", None),
    )
    return jax.shard_map(
        ordered,
        mesh=mesh,
        in_specs=placed,
        out_specs=(
            P("seq", "col"),
            P("seq", "col", None),
            P(None, "col"),
            P(None, "col"),
            P(None, "col"),
            P("col", None),
            P(None, "col"),
        ),
        check_vma=False,
    )
```

```python
import functools
import math

import jax
import jax.numpy as jnp
from jax import lax
from jax.experimental import pallas as pl
from jax.experimental.pallas import tpu as pltpu
from jax.sharding import PartitionSpec as P

QUERY_BLOCK = 32
KEY_WINDOW = 128
REACH = 64
SUB = 16
BAND = 64
GROUP = 96
SPAN = GROUP + 2 * REACH
HEADS = 4
F32 = jnp.float32
BF16 = jnp.bfloat16

NN = (((1,), (0,)), ((), ()))
NT = (((1,), (1,)), ((), ()))
TN = (((0,), (0,)), ((), ()))


def mm(a, b, dims=NN):
    return lax.dot_general(a, b, dims, preferred_element_type=F32)


def halves(x):
    high = x.astype(BF16)
    return high, (x - high.astype(F32)).astype(BF16)


def mm2(a, b, dims=NN):
    high, low = halves(a)
    return mm(high, b, dims) + mm(low, b, dims)


def band_copies(index_ref, pair_ref, band, sems):
    width = pair_ref.shape[1]
    copies = []
    for part in range(3):
        start = (index_ref[0] + part - 1) * SUB - index_ref[1] * width
        own = jnp.logical_and(start >= 0, start < width)
        safe = pl.multiple_of(jnp.clip(start, 0, width - SUB), SUB)
        copy = pltpu.make_async_copy(
            pair_ref.at[:, pl.ds(safe, SUB), :],
            band.at[:, pl.ds(part * SUB, SUB), :],
            sems.at[part],
        )
        copies.append((own, safe, copy))
    return copies


def start_band(copies, band):
    tokens = band.shape[0]
    band[:, 3 * SUB :, :] = jnp.zeros((tokens, BAND - 3 * SUB, band.shape[2]), BF16)
    for part, (own, _, copy) in enumerate(copies):

        @pl.when(own)
        def _(copy=copy):
            copy.start()

        @pl.when(jnp.logical_not(own))
        def _(part=part):
            band[:, part * SUB : (part + 1) * SUB, :] = jnp.zeros((tokens, SUB, band.shape[2]), BF16)


def wait_all(copies):
    for own, _, copy in copies:

        @pl.when(own)
        def _(copy=copy):
            copy.wait()


def pad_rows(x, rows):
    return jnp.concatenate([x, jnp.zeros((rows - x.shape[0],) + x.shape[1:], x.dtype)], axis=0)


def pick(condition, one, other):
    return jnp.where(condition, one.astype(F32), other.astype(F32))


def pack_kernel(
    index_ref,
    pair_ref,
    wq_ref,
    wk_ref,
    wv_ref,
    wo_ref,
    wb_ref,
    atoms_ref,
    token_row_ref,
    pack_ref,
    band,
    bias,
    band_sems,
):
    copies = band_copies(index_ref, pair_ref, band, band_sems)
    start_band(copies, band)
    odd = lax.rem(index_ref[0], 2) == 1
    tokens = band.shape[0]
    atoms = atoms_ref.shape[0]
    weights = pick(
        odd,
        jnp.concatenate([wq_ref[...], wk_ref[...]], axis=0),
        jnp.concatenate([wv_ref[...], wo_ref[...]], axis=0),
    ).astype(BF16)
    share = REACH // HEADS
    first = jnp.where(odd, atoms - REACH, 0) + index_ref[1] * share
    edge = atoms_ref[pl.ds(pl.multiple_of(first, share), share), :]
    row = token_row_ref[...]
    code = jnp.where(odd, row[:, atoms - REACH :], row[:, :REACH]) + 1
    line = jnp.concatenate([code >> 6, code & 63], axis=1).astype(F32)
    line = jnp.broadcast_to(line, (share, line.shape[1])).astype(BF16)
    other = jnp.concatenate(
        [edge, line, jnp.zeros((REACH - 2 * share, edge.shape[1]), BF16)], axis=0
    )
    rows = pad_rows(wb_ref[...].astype(F32), 8).astype(BF16)
    wait_all(copies)
    for t in range(0, tokens, 2):
        part = mm(rows, band[t], NT) + pltpu.roll(mm(rows, band[t + 1], NT), 4, 0)
        high = part.astype(BF16).astype(F32)
        bias[4 * t : 4 * t + 8, :] = jnp.concatenate([high, part - high], axis=1)
    low_tail = pick(odd, bias[...], other).astype(BF16)
    high_tail = pick(odd, other, bias[...]).astype(BF16)
    for c in range(HEADS):
        pack_ref[c] = jnp.concatenate([weights, low_tail], axis=0)
        pack_ref[HEADS + c] = jnp.concatenate([weights, high_tail], axis=0)


def attention_kernel(
    index_ref,
    window_ref,
    pair_ref,
    recv_ref,
    near_ref,
    own_ref,
    token_row_ref,
    token_col_ref,
    counts_ref,
    atom_cot_ref,
    token_cot_ref,
    wb_ref,
    pay_ref,
    rim_far_ref,
    rim_near_ref,
    own_out_ref,
    grad_pair_ref,
    band,
    zeros,
    main,
    grad_band,
    band_sems,
    zero_sems,
    out_sems,
    *,
    seqs,
):
    copies = band_copies(index_ref, pair_ref, band, band_sems)
    start_band(copies, band)
    tokens = band.shape[0]
    zeros[...] = jnp.zeros(zeros.shape, BF16)
    fills = [
        pltpu.make_async_copy(zeros, grad_pair_ref.at[t], zero_sems.at[t]) for t in range(tokens)
    ]
    for fill in fills:
        fill.start()
    seq, col = index_ref[0], index_ref[1]
    odd = lax.rem(seq, 2) == 1
    atoms = own_ref.shape[0]
    width = own_ref.shape[1]
    head = width // HEADS
    inv_root = 1.0 / math.sqrt(head)
    slot_base = seq * atoms
    token_base = seq * tokens
    same = jnp.where(odd, 0, HEADS)
    paired = HEADS - same
    share = REACH // HEADS

    def gathered(member, first):
        return jnp.concatenate(
            [recv_ref[member + c, first : first + head, :] for c in range(HEADS)], axis=0
        )

    wq_t, wk_t = gathered(0, 0), gathered(0, head)
    wv_t, wo = gathered(HEADS, 0), gathered(HEADS, head)
    bias = recv_ref[same, 2 * head :, :].astype(F32)
    for c in range(1, HEADS):
        bias = bias + recv_ref[same + c, 2 * head :, :].astype(F32)
    bias = bias.astype(BF16)

    own = own_ref[...]
    far_rows = jnp.concatenate(
        [recv_ref[paired + c, 2 * head : 2 * head + share, :] for c in range(HEADS)], axis=0
    )
    near_rows = near_ref[:REACH, :]
    has_below, has_above = seq > 0, seq < seqs - 1
    below = jnp.where(has_below, pick(odd, near_rows, far_rows), 0.0).astype(BF16)
    above = jnp.where(has_above, pick(odd, far_rows, near_rows), 0.0).astype(BF16)
    ext = jnp.concatenate([below, own, above], axis=0)
    queries = mm(own, wq_t, NT).astype(BF16)
    keys = mm(ext, wk_t, NT).astype(BF16)
    values = mm(ext, wv_t, NT).astype(BF16)

    token_col = token_col_ref[...]
    live_col = token_col >= 0
    local_col = token_col - token_base
    token_lanes = lax.broadcasted_iota(jnp.int32, (atoms, tokens), 1)
    onehot = (local_col == token_lanes).astype(F32)
    pooled = mm(onehot.astype(BF16), token_cot_ref[...])
    count = jnp.sum(onehot * counts_ref[...].astype(F32), axis=1, keepdims=True)
    safe_count = jnp.where(live_col, count, 1.0)
    upstream = jnp.where(live_col, atom_cot_ref[...].astype(F32) + pooled / safe_count, 0.0)
    upstream = upstream.astype(BF16)
    grad_attended = mm(upstream, wo, NT).astype(BF16)

    def decoded(line):
        row = line.astype(F32)[:1]
        return (row[:, :REACH] * 64.0 + row[:, REACH:]).astype(jnp.int32) - 1

    far_token = decoded(recv_ref[paired, 2 * head + share : 2 * head + 2 * share, :])
    near_token = decoded(near_ref[REACH : REACH + 16, :])
    below_token = jnp.where(has_below, jnp.where(odd, near_token, far_token), -1)
    above_token = jnp.where(has_above, jnp.where(odd, far_token, near_token), -1)
    own_row = token_row_ref[...]
    key_rows = (
        jnp.concatenate([below_token, own_row[:, : SPAN - REACH]], axis=1),
        jnp.concatenate([own_row[:, atoms - (SPAN - REACH) :], above_token], axis=1),
    )
    head_lanes = lax.broadcasted_iota(jnp.int32, (GROUP, width), 1) // head
    head_masks = [head_lanes == h for h in range(HEADS)]

    def stacked(x):
        return jnp.concatenate(
            [jnp.where(mask, x, jnp.zeros_like(x)) for mask in head_masks], axis=0
        )

    def folded(x):
        total = jnp.where(head_masks[0], x[:GROUP], 0.0)
        for h in range(1, HEADS):
            total = total + jnp.where(head_masks[h], x[h * GROUP : (h + 1) * GROUP], 0.0)
        return total

    attended, grad_queries, key_terms, value_terms = [], [], [], []
    token_grad = jnp.zeros((tokens * HEADS, width), F32)
    for g in range(atoms // GROUP):
        rows = slice(g * GROUP, (g + 1) * GROUP)
        span = slice(g * GROUP, g * GROUP + SPAN)
        k_g, v_g = keys[span], values[span]
        q_m = stacked(queries[rows].astype(F32)).astype(BF16)
        a_m = stacked(grad_attended[rows].astype(F32)).astype(BF16)
        key_token = key_rows[g]
        key_live = key_token >= 0
        key_band = jnp.where(key_live, key_token - (token_base - tokens), -1000)
        lane_band = lax.broadcasted_iota(jnp.int32, (width, SPAN), 0)
        key_onehot = ((lane_band & (BAND - 1)) == key_band).astype(F32).astype(BF16)
        local = local_col[rows]
        slot = lax.broadcasted_iota(jnp.int32, (GROUP, tokens * HEADS), 1)
        query_onehot = jnp.concatenate(
            [(slot == local * HEADS + h).astype(F32) for h in range(HEADS)], axis=0
        )
        query_onehot = query_onehot.astype(BF16)
        picked = mm(query_onehot, bias).astype(BF16)
        scores = mm(q_m, k_g, NT) * inv_root + mm(picked, key_onehot)
        scores = scores.reshape(HEADS, GROUP, SPAN)
        block = lax.broadcasted_iota(jnp.int32, (GROUP, 1), 0) // QUERY_BLOCK
        base = slot_base - REACH + g * GROUP
        first = g * (GROUP // QUERY_BLOCK)
        start = jnp.where(
            block == 0,
            window_ref[first] - base,
            jnp.where(block == 1, window_ref[first + 1] - base, window_ref[first + 2] - base),
        )
        position = lax.broadcasted_iota(jnp.int32, (GROUP, SPAN), 1)
        inside = (position >= start) & (position < start + KEY_WINDOW)
        dead_query = local < 0
        allowed = inside & (key_live | dead_query)
        masked = jnp.where(allowed[None], scores, -1e30)
        row_max = jnp.max(masked, axis=-1, keepdims=True)
        raw = jnp.where(allowed[None], jnp.exp(masked - row_max), 0.0)
        weights = raw / jnp.sum(raw, axis=-1, keepdims=True)
        grad_weights = mm(a_m, v_g, NT).reshape(HEADS, GROUP, SPAN)
        inner = jnp.sum(weights * grad_weights, axis=-1, keepdims=True)
        grad_scores = (weights * (grad_weights - inner)).reshape(HEADS * GROUP, SPAN)
        w_low = weights.reshape(HEADS * GROUP, SPAN).astype(BF16)
        s_high, s_low = halves(grad_scores)
        attended.append(folded(mm(w_low, v_g)))
        grad_queries.append(folded(mm(s_high, k_g)) * inv_root)
        key_terms.append(mm(s_high, q_m, TN) * inv_root)
        value_terms.append(mm(w_low, a_m, TN))
        by_token = mm(query_onehot, s_high, TN) + mm(query_onehot, s_low, TN)
        token_grad = token_grad + mm2(by_token, key_onehot, NT)

    attended = jnp.concatenate(attended, axis=0).astype(BF16)
    grad_q = jnp.concatenate(grad_queries, axis=0)

    def overlapped(terms):
        lap = SPAN - GROUP
        return jnp.concatenate(
            [terms[0][:GROUP], terms[0][GROUP:] + terms[1][:lap], terms[1][lap:]], axis=0
        )

    grad_k = overlapped(key_terms)
    grad_v = overlapped(value_terms)

    rows = pad_rows(wb_ref[...].astype(F32), 8)
    turned = pad_rows(token_grad, width).T[: 3 * SUB]
    for t in range(tokens):
        at = HEADS * t
        total = turned[:, at : at + 1] * rows[0:1]
        for h in range(1, HEADS):
            total = total + turned[:, at + h : at + h + 1] * rows[h : h + 1]
        grad_band[t] = total.astype(BF16)
    for fill in fills:
        fill.wait()
    outs = []
    for part, (own_part, safe, _) in enumerate(copies):
        copy = pltpu.make_async_copy(
            grad_band.at[:, pl.ds(part * SUB, SUB), :],
            grad_pair_ref.at[:, pl.ds(safe, SUB), :],
            out_sems.at[part],
        )
        outs.append((own_part, safe, copy))

        @pl.when(own_part)
        def _(copy=copy):
            copy.start()

    plane = pay_ref.shape[0] // HEADS
    chunk = width // plane
    products = (
        mm2(grad_q, own, TN),
        mm2(grad_k, ext, TN),
        mm2(grad_v, ext, TN),
        mm(attended, upstream, TN),
    )
    per_product = head // chunk
    for i, product in enumerate(products):
        for c in range(HEADS):
            for j in range(per_product):
                to = ((i * per_product + j) * HEADS + c) * chunk
                at = c * head + j * chunk
                main[to : to + chunk, :] = product[at : at + chunk]
    wait_all(copies)
    w_bias_grad = jnp.zeros((8, width), F32)
    left = lax.broadcasted_iota(jnp.int32, (8, width), 1) < BAND
    for t in range(0, tokens, 2):
        two = token_grad[HEADS * t : HEADS * t + 8]
        two = jnp.where(left, two, pltpu.roll(two, 4, 0))
        stack = jnp.concatenate([band[t], band[t + 1]], axis=0)
        w_bias_grad = w_bias_grad + mm2(two, stack)
    upper = lax.broadcasted_iota(jnp.int32, (8, width), 0) < HEADS
    spread = jnp.where(upper, w_bias_grad, pltpu.roll(w_bias_grad, 4, 0))
    share = chunk // HEADS
    for j in range(share):
        pay_ref[:, j * width : (j + 1) * width] = main[
            pl.ds(col * share + j, plane * HEADS, stride=chunk), :
        ]
    pay_ref[:, share * width :] = jnp.concatenate([spread] * (plane * HEADS // 8), axis=0)

    key_part = mm2(grad_k, wk_t) + mm2(grad_v, wv_t)
    query_part = mm2(grad_q, wq_t) + upstream.astype(F32)
    shift = lax.rem(width - col * head, width)
    whole = jnp.concatenate(
        [key_part[REACH : REACH + atoms] + query_part, key_part[:REACH]]
        + [key_part[REACH + atoms :], jnp.zeros((REACH, width), F32)],
        axis=0,
    )
    whole = pltpu.roll(whole, shift, 1).T[:head]
    own_out_ref[...] = whole[:, :atoms]
    rim_down = whole[:, atoms : atoms + REACH]
    rim_up = whole[:, atoms + REACH : atoms + 2 * REACH]
    rim_far_ref[...] = jnp.where(odd, rim_up, rim_down).astype(BF16)
    rim_near_ref[...] = jnp.where(odd, rim_down, rim_up).astype(BF16)
    wait_all(outs)


def final_kernel(
    index_ref,
    main_ref,
    bias_ref,
    own_ref,
    far_ref,
    near_ref,
    atoms_ref,
    gq_ref,
    gk_ref,
    gv_ref,
    go_ref,
    gb_ref,
):
    head, atoms = atoms_ref.shape
    odd = lax.rem(index_ref[0], 2) == 1
    below = pick(odd, near_ref[...], far_ref[...])
    above = pick(odd, far_ref[...], near_ref[...])
    middle = jnp.zeros((head, atoms - 2 * REACH), F32)
    atoms_ref[...] = (own_ref[...] + jnp.concatenate([below, middle, above], axis=1)).astype(BF16)
    for i, ref in enumerate((gq_ref, gk_ref, gv_ref, go_ref)):
        ref[...] = main_ref[i * head : (i + 1) * head, :]
    gb_ref[...] = bias_ref[...]


def vmem():
    return pl.BlockSpec(memory_space=pltpu.VMEM)


def smem():
    return pl.BlockSpec(memory_space=pltpu.SMEM)


def in_hbm():
    return pl.BlockSpec(memory_space=pltpu.MemorySpace.HBM)


def shape(dims, dtype):
    return jax.ShapeDtypeStruct(dims, dtype)


def params(mebibytes):
    return pltpu.CompilerParams(vmem_limit_bytes=mebibytes * 1024 * 1024)


def per_device(
    atom_inputs,
    atom_token,
    counts,
    window_start,
    pair_features,
    w_query,
    w_key,
    w_value,
    w_out,
    w_bias,
    atom_cotangent,
    token_cotangent,
):
    atoms, width = atom_inputs.shape
    tokens, columns, _ = pair_features.shape
    head = w_query.shape[1]
    seqs = lax.axis_size("seq")
    plane = 16 if seqs % 16 == 0 else 4
    planes = seqs // plane
    cols = lax.axis_size("col")
    seq = lax.axis_index("seq")
    index = jnp.stack([seq, lax.axis_index("col")]).astype(jnp.int32)
    odd = seq % 2 == 1
    token_row = atom_token[None, :]

    near = [(i, i ^ 1) for i in range(seqs)]
    far = [(i, i + 1) for i in range(1, seqs - 1, 2)]
    far = far + [(j, i) for i, j in far]
    far_groups = [
        [n * cols + c for n in (i, (i + 1) % seqs) for c in range(cols)] for i in range(1, seqs, 2)
    ]
    edge_start = jnp.where(odd, 0, atoms - REACH)
    code = lax.dynamic_slice(atom_token, (edge_start,), (REACH,)) + 1
    line = jnp.concatenate([code // 64, code % 64]).astype(BF16)[None]
    edge = lax.dynamic_slice(atom_inputs, (edge_start, 0), (REACH, width))
    near_edge = lax.ppermute(
        jnp.concatenate([edge, line, jnp.zeros((15, width), BF16)], axis=0), "seq", near
    )
    w_bias_t = w_bias.T
    pack = pl.pallas_call(
        pack_kernel,
        out_shape=shape((2 * HEADS, width, width), BF16),
        in_specs=[smem(), in_hbm()] + [vmem()] * 7,
        out_specs=vmem(),
        scratch_shapes=[
            pltpu.VMEM((tokens, BAND, width), BF16),
            pltpu.VMEM((tokens * HEADS, width), F32),
            pltpu.SemaphoreType.DMA((3,)),
        ],
        compiler_params=params(60),
        name="pack",
    )(
        index,
        pair_features,
        w_query.T,
        w_key.T,
        w_value.T,
        w_out,
        w_bias_t,
        atom_inputs,
        token_row,
    )
    recv = lax.all_to_all(
        pack, ("seq", "col"), 0, 0, tiled=True, axis_index_groups=far_groups
    )

    chunk = width // plane
    share = chunk // HEADS
    pay, rim_far, rim_near, own_part, grad_pair = pl.pallas_call(
        functools.partial(attention_kernel, seqs=seqs),
        out_shape=(
            shape((plane * HEADS, (share + 1) * width), F32),
            shape((head, REACH), BF16),
            shape((head, REACH), BF16),
            shape((head, atoms), F32),
            shape(pair_features.shape, BF16),
        ),
        in_specs=[smem(), smem(), in_hbm()] + [vmem()] * 9,
        out_specs=(vmem(), vmem(), vmem(), vmem(), in_hbm()),
        scratch_shapes=[
            pltpu.VMEM((tokens, BAND, width), BF16),
            pltpu.VMEM((columns, width), BF16),
            pltpu.VMEM((HEADS * width, width), F32),
            pltpu.VMEM((tokens, 3 * SUB, width), BF16),
            pltpu.SemaphoreType.DMA((3,)),
            pltpu.SemaphoreType.DMA((tokens,)),
            pltpu.SemaphoreType.DMA((3,)),
        ],
        compiler_params=params(32),
        name="attention",
    )(
        index,
        window_start,
        pair_features,
        recv,
        near_edge,
        atom_inputs,
        token_row,
        atom_token[:, None],
        counts[None, :],
        atom_cotangent,
        token_cotangent,
        w_bias_t,
    )
    rim_far = lax.ppermute(rim_far, "seq", far)
    rim_near = lax.ppermute(rim_near, "seq", near)

    whole_planes = [
        [(z * plane + i) * cols + c for i in range(plane) for c in range(cols)]
        for z in range(planes)
    ]
    across = [[z * plane + i for z in range(planes)] for i in range(plane)]
    within = [[z * plane + i for i in range(plane)] for z in range(planes)]
    first = lax.all_to_all(
        pay[:, None, :], ("seq", "col"), 0, 0, tiled=True, axis_index_groups=whole_planes
    )
    summed = first.reshape(plane, HEADS, (share + 1) * width).sum(axis=0)
    mains = summed[:, : share * width].reshape(1, chunk * width)
    tail = summed[:, share * width :].sum(axis=0, keepdims=True)
    joined = jnp.concatenate([mains, tail], axis=1)
    second = lax.all_to_all(
        jnp.broadcast_to(joined[None], (planes, 1, joined.shape[1])),
        "seq",
        0,
        0,
        tiled=True,
        axis_index_groups=across,
    ).sum(axis=0)
    third = lax.all_to_all(
        jnp.broadcast_to(second[None, :, : chunk * width], (plane, 1, chunk * width)),
        "seq",
        0,
        0,
        tiled=True,
        axis_index_groups=within,
    )
    grad_atoms, gq, gk, gv, go, gb = pl.pallas_call(
        final_kernel,
        out_shape=(
            shape((head, atoms), BF16),
            shape((head, width), F32),
            shape((head, width), F32),
            shape((head, width), F32),
            shape((head, width), F32),
            shape((1, width), F32),
        ),
        in_specs=[smem()] + [vmem()] * 5,
        out_specs=(vmem(),) * 6,
        compiler_params=params(16),
        name="final",
    )(
        index,
        third.reshape(width, width),
        second[:, chunk * width :],
        own_part,
        rim_far,
        rim_near,
    )
    return (grad_atoms.T, grad_pair, gq.T, gk.T, gv.T, go, gb.T)


def solution(mesh):
    placed = (
        P("seq", None),
        P("seq"),
        P("seq"),
        P("seq"),
        P("seq", "col", None),
        P(None, "col"),
        P(None, "col"),
        P(None, "col"),
        P("col", None),
        P(),
        P("seq", None),
        P("seq", None),
    )
    return jax.shard_map(
        per_device,
        mesh=mesh,
        in_specs=placed,
        out_specs=(
            P("seq", "col"),
            P("seq", "col", None),
            P(None, "col"),
            P(None, "col"),
            P(None, "col"),
            P("col", None),
            P(None, "col"),
        ),
        check_vma=False,
    )
```

```python
import functools
import math

import jax
import jax.numpy as jnp
from jax import lax
from jax.experimental import pallas as pl
from jax.experimental.pallas import tpu as pltpu
from jax.sharding import PartitionSpec as P

QUERY_BLOCK = 32
KEY_WINDOW = 128
REACH = 64
SUB = 16
BAND = 64
GROUP = 96
SPAN = GROUP + 2 * REACH
HEADS = 4
F32 = jnp.float32
BF16 = jnp.bfloat16

NN = (((1,), (0,)), ((), ()))
NT = (((1,), (1,)), ((), ()))
TN = (((0,), (0,)), ((), ()))


def mm(a, b, dims=NN):
    return lax.dot_general(a, b, dims, preferred_element_type=F32)


def halves(x):
    high = x.astype(BF16)
    return high, (x - high.astype(F32)).astype(BF16)


def mm2(a, b, dims=NN):
    high, low = halves(a)
    return mm(high, b, dims) + mm(low, b, dims)


def band_copies(seq, col, pair_ref, band, sems):
    width = pair_ref.shape[1]
    copies = []
    for part in range(3):
        start = (seq + part - 1) * SUB - col * width
        own = jnp.logical_and(start >= 0, start < width)
        safe = pl.multiple_of(jnp.clip(start, 0, width - SUB), SUB)
        copy = pltpu.make_async_copy(
            pair_ref.at[:, pl.ds(safe, SUB), :],
            band.at[:, pl.ds(part * SUB, SUB), :],
            sems.at[part],
        )
        copies.append((own, safe, copy))
    return copies


def start_band(copies, band):
    tokens = band.shape[0]
    band[:, 3 * SUB :, :] = jnp.zeros((tokens, BAND - 3 * SUB, band.shape[2]), BF16)
    for part, (own, _, copy) in enumerate(copies):

        @pl.when(own)
        def _(copy=copy):
            copy.start()

        @pl.when(jnp.logical_not(own))
        def _(part=part):
            band[:, part * SUB : (part + 1) * SUB, :] = jnp.zeros((tokens, SUB, band.shape[2]), BF16)


def wait_all(copies):
    for own, _, copy in copies:

        @pl.when(own)
        def _(copy=copy):
            copy.wait()


def pad_rows(x, rows):
    return jnp.concatenate([x, jnp.zeros((rows - x.shape[0],) + x.shape[1:], x.dtype)], axis=0)


def pick(condition, one, other):
    return jnp.where(condition, one.astype(F32), other.astype(F32))


def pack_kernel(
    pair_ref,
    wq_ref,
    wk_ref,
    wv_ref,
    wo_ref,
    atoms_ref,
    wb_ref,
    token_row_ref,
    pack_ref,
    band,
    half,
    edge,
    bias,
    band_sems,
    sems,
):
    seq, col = lax.axis_index("seq"), lax.axis_index("col")
    odd = lax.rem(seq, 2) == 1
    copies = band_copies(seq, col, pair_ref, band, band_sems)
    start_band(copies, band)
    tokens = band.shape[0]
    atoms = atoms_ref.shape[0]
    head = wq_ref.shape[0]
    share = REACH // HEADS
    first = jnp.where(odd, atoms - REACH, 0) + col * share
    others = [
        pltpu.make_async_copy(
            atoms_ref.at[pl.ds(pl.multiple_of(first, share), share), :], edge, sems.at[0]
        )
    ] + [
        pltpu.make_async_copy(ref, half.at[i * head : (i + 1) * head, :], sems.at[i + 1])
        for i, ref in enumerate((wq_ref, wk_ref, wv_ref, wo_ref))
    ]
    for copy in others:
        copy.start()
    row = token_row_ref[...]
    code = jnp.where(odd, row[:, atoms - REACH :], row[:, :REACH]) + 1
    line = jnp.concatenate([code >> 6, code & 63], axis=1).astype(F32)
    line = jnp.broadcast_to(line, (share, line.shape[1])).astype(BF16)
    rows = pad_rows(wb_ref[...].astype(F32), 8).astype(BF16)
    for copy in others:
        copy.wait()
    weights = pick(odd, half[: 2 * head, :], half[2 * head :, :]).astype(BF16)
    other = jnp.concatenate(
        [edge[...], line, jnp.zeros((REACH - 2 * share, edge.shape[1]), BF16)], axis=0
    )
    wait_all(copies)
    for t in range(0, tokens, 2):
        part = mm(rows, band[t], NT) + pltpu.roll(mm(rows, band[t + 1], NT), 4, 0)
        high = part.astype(BF16).astype(F32)
        bias[4 * t : 4 * t + 8, :] = jnp.concatenate([high, part - high], axis=1)
    low_tail = pick(odd, bias[...], other).astype(BF16)
    high_tail = pick(odd, other, bias[...]).astype(BF16)
    for c in range(HEADS):
        pack_ref[c] = jnp.concatenate([weights, low_tail], axis=0)
        pack_ref[HEADS + c] = jnp.concatenate([weights, high_tail], axis=0)


def attention_kernel(
    window_ref,
    pair_ref,
    recv_ref,
    near_ref,
    own_ref,
    token_row_ref,
    token_col_ref,
    counts_ref,
    atom_cot_ref,
    token_cot_ref,
    wb_ref,
    pay_ref,
    rim_far_ref,
    rim_near_ref,
    own_out_ref,
    grad_pair_ref,
    band,
    zeros,
    main,
    grad_band,
    band_sems,
    zero_sems,
    out_sems,
    *,
    seqs,
    plane,
):
    seq, col = lax.axis_index("seq"), lax.axis_index("col")
    copies = band_copies(seq, col, pair_ref, band, band_sems)
    start_band(copies, band)
    tokens = band.shape[0]
    zeros[...] = jnp.zeros(zeros.shape, BF16)
    fills = [
        pltpu.make_async_copy(zeros, grad_pair_ref.at[t], zero_sems.at[t]) for t in range(tokens)
    ]
    for fill in fills:
        fill.start()
    odd = lax.rem(seq, 2) == 1
    atoms = own_ref.shape[0]
    width = own_ref.shape[1]
    head = width // HEADS
    inv_root = 1.0 / math.sqrt(head)
    slot_base = seq * atoms
    token_base = seq * tokens
    same = jnp.where(odd, 0, HEADS)
    paired = HEADS - same
    share = REACH // HEADS

    def gathered(member, first):
        return jnp.concatenate(
            [recv_ref[member + c, first : first + head, :] for c in range(HEADS)], axis=0
        )

    wq_t, wk_t = gathered(0, 0), gathered(0, head)
    wv_t, wo = gathered(HEADS, 0), gathered(HEADS, head)
    bias = recv_ref[same, 2 * head :, :].astype(F32)
    for c in range(1, HEADS):
        bias = bias + recv_ref[same + c, 2 * head :, :].astype(F32)
    bias = bias.astype(BF16)

    own = own_ref[...]
    far_rows = jnp.concatenate(
        [recv_ref[paired + c, 2 * head : 2 * head + share, :] for c in range(HEADS)], axis=0
    )
    near_rows = near_ref[:REACH, :]
    has_below, has_above = seq > 0, seq < seqs - 1
    below = jnp.where(has_below, pick(odd, near_rows, far_rows), 0.0).astype(BF16)
    above = jnp.where(has_above, pick(odd, far_rows, near_rows), 0.0).astype(BF16)
    ext = jnp.concatenate([below, own, above], axis=0)
    queries = mm(own, wq_t, NT).astype(BF16)
    keys = mm(ext, wk_t, NT).astype(BF16)
    values = mm(ext, wv_t, NT).astype(BF16)

    token_col = token_col_ref[...]
    live_col = token_col >= 0
    local_col = token_col - token_base
    token_lanes = lax.broadcasted_iota(jnp.int32, (atoms, tokens), 1)
    onehot = (local_col == token_lanes).astype(F32)
    pooled = mm(onehot.astype(BF16), token_cot_ref[...])
    count = jnp.sum(onehot * counts_ref[...].astype(F32), axis=1, keepdims=True)
    safe_count = jnp.where(live_col, count, 1.0)
    upstream = jnp.where(live_col, atom_cot_ref[...].astype(F32) + pooled / safe_count, 0.0)
    upstream = upstream.astype(BF16)
    grad_attended = mm(upstream, wo, NT).astype(BF16)

    def decoded(line):
        row = line.astype(F32)[:1]
        return (row[:, :REACH] * 64.0 + row[:, REACH:]).astype(jnp.int32) - 1

    far_token = decoded(recv_ref[paired, 2 * head + share : 2 * head + 2 * share, :])
    near_token = decoded(near_ref[REACH : REACH + 16, :])
    below_token = jnp.where(has_below, jnp.where(odd, near_token, far_token), -1)
    above_token = jnp.where(has_above, jnp.where(odd, far_token, near_token), -1)
    own_row = token_row_ref[...]
    key_rows = (
        jnp.concatenate([below_token, own_row[:, : SPAN - REACH]], axis=1),
        jnp.concatenate([own_row[:, atoms - (SPAN - REACH) :], above_token], axis=1),
    )
    head_lanes = lax.broadcasted_iota(jnp.int32, (GROUP, width), 1) // head
    head_masks = [head_lanes == h for h in range(HEADS)]

    def stacked(x):
        return jnp.concatenate(
            [jnp.where(mask, x, jnp.zeros_like(x)) for mask in head_masks], axis=0
        )

    def folded(x):
        total = jnp.where(head_masks[0], x[:GROUP], 0.0)
        for h in range(1, HEADS):
            total = total + jnp.where(head_masks[h], x[h * GROUP : (h + 1) * GROUP], 0.0)
        return total

    attended, grad_queries, key_terms, value_terms = [], [], [], []
    token_grad = jnp.zeros((tokens * HEADS, width), F32)
    for g in range(atoms // GROUP):
        rows = slice(g * GROUP, (g + 1) * GROUP)
        span = slice(g * GROUP, g * GROUP + SPAN)
        k_g, v_g = keys[span], values[span]
        q_m = stacked(queries[rows].astype(F32)).astype(BF16)
        a_m = stacked(grad_attended[rows].astype(F32)).astype(BF16)
        key_token = key_rows[g]
        key_live = key_token >= 0
        key_band = jnp.where(key_live, key_token - (token_base - tokens), -1000)
        lane_band = lax.broadcasted_iota(jnp.int32, (width, SPAN), 0)
        key_onehot = ((lane_band & (BAND - 1)) == key_band).astype(F32).astype(BF16)
        local = local_col[rows]
        slot = lax.broadcasted_iota(jnp.int32, (GROUP, tokens * HEADS), 1)
        query_onehot = jnp.concatenate(
            [(slot == local * HEADS + h).astype(F32) for h in range(HEADS)], axis=0
        )
        query_onehot = query_onehot.astype(BF16)
        picked = mm(query_onehot, bias).astype(BF16)
        scores = mm(q_m, k_g, NT) * inv_root + mm(picked, key_onehot)
        scores = scores.reshape(HEADS, GROUP, SPAN)
        block = lax.broadcasted_iota(jnp.int32, (GROUP, 1), 0) // QUERY_BLOCK
        base = slot_base - REACH + g * GROUP
        first = g * (GROUP // QUERY_BLOCK)
        start = jnp.where(
            block == 0,
            window_ref[first] - base,
            jnp.where(block == 1, window_ref[first + 1] - base, window_ref[first + 2] - base),
        )
        position = lax.broadcasted_iota(jnp.int32, (GROUP, SPAN), 1)
        inside = (position >= start) & (position < start + KEY_WINDOW)
        dead_query = local < 0
        allowed = inside & (key_live | dead_query)
        masked = jnp.where(allowed[None], scores, -1e30)
        row_max = jnp.max(masked, axis=-1, keepdims=True)
        raw = jnp.where(allowed[None], jnp.exp(masked - row_max), 0.0)
        weights = raw / jnp.sum(raw, axis=-1, keepdims=True)
        grad_weights = mm(a_m, v_g, NT).reshape(HEADS, GROUP, SPAN)
        inner = jnp.sum(weights * grad_weights, axis=-1, keepdims=True)
        grad_scores = (weights * (grad_weights - inner)).reshape(HEADS * GROUP, SPAN)
        w_low = weights.reshape(HEADS * GROUP, SPAN).astype(BF16)
        s_high, s_low = halves(grad_scores)
        attended.append(folded(mm(w_low, v_g)))
        grad_queries.append(folded(mm(s_high, k_g)) * inv_root)
        key_terms.append(mm(s_high, q_m, TN) * inv_root)
        value_terms.append(mm(w_low, a_m, TN))
        by_token = mm(query_onehot, s_high, TN) + mm(query_onehot, s_low, TN)
        token_grad = token_grad + mm2(by_token, key_onehot, NT)

    attended = jnp.concatenate(attended, axis=0).astype(BF16)
    grad_q = jnp.concatenate(grad_queries, axis=0)

    def overlapped(terms):
        lap = SPAN - GROUP
        return jnp.concatenate(
            [terms[0][:GROUP], terms[0][GROUP:] + terms[1][:lap], terms[1][lap:]], axis=0
        )

    grad_k = overlapped(key_terms)
    grad_v = overlapped(value_terms)

    rows = pad_rows(wb_ref[...].astype(F32), 8)
    turned = pad_rows(token_grad, width).T[: 3 * SUB]
    for t in range(tokens):
        at = HEADS * t
        total = turned[:, at : at + 1] * rows[0:1]
        for h in range(1, HEADS):
            total = total + turned[:, at + h : at + h + 1] * rows[h : h + 1]
        grad_band[t] = total.astype(BF16)
    for fill in fills:
        fill.wait()
    outs = []
    for part, (own_part, safe, _) in enumerate(copies):
        copy = pltpu.make_async_copy(
            grad_band.at[:, pl.ds(part * SUB, SUB), :],
            grad_pair_ref.at[:, pl.ds(safe, SUB), :],
            out_sems.at[part],
        )
        outs.append((own_part, safe, copy))

        @pl.when(own_part)
        def _(copy=copy):
            copy.start()

    chunk = width // plane
    products = (
        mm2(grad_q, own, TN),
        mm2(grad_k, ext, TN),
        mm2(grad_v, ext, TN),
        mm(attended, upstream, TN),
    )
    per_product = head // chunk
    for i, product in enumerate(products):
        for c in range(HEADS):
            for j in range(per_product):
                to = ((i * per_product + j) * HEADS + c) * chunk
                at = c * head + j * chunk
                main[to : to + chunk, :] = product[at : at + chunk]
    wait_all(copies)
    w_bias_grad = jnp.zeros((8, width), F32)
    left = lax.broadcasted_iota(jnp.int32, (8, width), 1) < BAND
    for t in range(0, tokens, 2):
        two = token_grad[HEADS * t : HEADS * t + 8]
        two = jnp.where(left, two, pltpu.roll(two, 4, 0))
        stack = jnp.concatenate([band[t], band[t + 1]], axis=0)
        w_bias_grad = w_bias_grad + mm2(two, stack)
    upper = lax.broadcasted_iota(jnp.int32, (8, width), 0) < HEADS
    spread = jnp.where(upper, w_bias_grad, pltpu.roll(w_bias_grad, 4, 0))
    share = chunk // HEADS
    for j in range(share):
        pay_ref[pl.ds(j, plane * HEADS, stride=share + 1), :] = main[
            pl.ds(col * share + j, plane * HEADS, stride=chunk), :
        ]
    pay_ref[pl.ds(share, plane * HEADS, stride=share + 1), :] = jnp.concatenate(
        [spread] * (plane * HEADS // 8), axis=0
    )

    key_part = mm2(grad_k, wk_t) + mm2(grad_v, wv_t)
    query_part = mm2(grad_q, wq_t) + upstream.astype(F32)
    shift = lax.rem(width - col * head, width)
    whole = jnp.concatenate(
        [key_part[REACH : REACH + atoms] + query_part, key_part[:REACH]]
        + [key_part[REACH + atoms :], jnp.zeros((REACH, width), F32)],
        axis=0,
    )
    whole = pltpu.roll(whole, shift, 1).T[:head]
    own_out_ref[...] = whole[:, :atoms]
    rim_down = whole[:, atoms : atoms + REACH]
    rim_up = whole[:, atoms + REACH : atoms + 2 * REACH]
    rim_far = jnp.where(odd, rim_up, rim_down)
    rim_far_ref[...] = jnp.concatenate([rim_far[: head // 2], rim_far[head // 2 :]], axis=1)
    rim_near_ref[...] = jnp.where(odd, rim_down, rim_up).astype(BF16)
    wait_all(outs)


def final_kernel(
    gathered_ref,
    bias_ref,
    own_ref,
    near_ref,
    atoms_ref,
    gq_ref,
    gk_ref,
    gv_ref,
    go_ref,
    gb_ref,
    *,
    seqs,
    chunk,
):
    head, atoms = atoms_ref.shape
    seq = lax.axis_index("seq")
    odd = lax.rem(seq, 2) == 1
    rim_rows = head // 2
    rows = chunk + rim_rows
    plane = gathered_ref.shape[0] // rows
    partner = lax.rem(jnp.where(odd, seq + 1, seq - 1 + seqs), plane)
    far = gathered_ref[pl.ds(pl.multiple_of(partner * rows + chunk, 8), rim_rows), :]
    far = jnp.concatenate([far[:, :REACH], far[:, REACH:]], axis=0)
    far = jnp.where(jnp.where(odd, seq + 1, seq) % seqs == 0, 0.0, far)
    near = near_ref[...].astype(F32)
    below, above = jnp.where(odd, near, far), jnp.where(odd, far, near)
    middle = jnp.zeros((head, atoms - 2 * REACH), F32)
    atoms_ref[...] = (own_ref[...] + jnp.concatenate([below, middle, above], axis=1)).astype(BF16)
    main = jnp.concatenate(
        [gathered_ref[p * rows : p * rows + chunk, :] for p in range(plane)], axis=0
    )
    for i, ref in enumerate((gq_ref, gk_ref, gv_ref, go_ref)):
        ref[...] = main[i * head : (i + 1) * head]
    gb_ref[...] = bias_ref[...]


def vmem():
    return pl.BlockSpec(memory_space=pltpu.VMEM)


def smem():
    return pl.BlockSpec(memory_space=pltpu.SMEM)


def in_hbm():
    return pl.BlockSpec(memory_space=pltpu.MemorySpace.HBM)


def shape(dims, dtype):
    return jax.ShapeDtypeStruct(dims, dtype)


def params(mebibytes):
    return pltpu.CompilerParams(vmem_limit_bytes=mebibytes * 1024 * 1024)


def per_device(
    atom_inputs,
    atom_token,
    counts,
    window_start,
    pair_features,
    w_query,
    w_key,
    w_value,
    w_out,
    w_bias,
    atom_cotangent,
    token_cotangent,
):
    atoms, width = atom_inputs.shape
    tokens, columns, _ = pair_features.shape
    head = w_query.shape[1]
    seqs = lax.axis_size("seq")
    plane = 16 if seqs % 16 == 0 else 4
    planes = seqs // plane
    cols = lax.axis_size("col")
    seq = lax.axis_index("seq")
    odd = seq % 2 == 1
    token_row = atom_token[None, :]

    near = [(i, i ^ 1) for i in range(seqs)]
    far_groups = [
        [n * cols + c for n in (i, (i + 1) % seqs) for c in range(cols)] for i in range(1, seqs, 2)
    ]
    edge_start = jnp.where(odd, 0, atoms - REACH)
    code = lax.dynamic_slice(atom_token, (edge_start,), (REACH,)) + 1
    line = jnp.concatenate([code // 64, code % 64]).astype(BF16)[None]
    edge = lax.dynamic_slice(atom_inputs, (edge_start, 0), (REACH, width))
    near_edge = lax.ppermute(
        jnp.concatenate([edge, line, jnp.zeros((15, width), BF16)], axis=0), "seq", near
    )
    w_bias_t = w_bias.T
    pack = pl.pallas_call(
        pack_kernel,
        out_shape=shape((2 * HEADS, width, width), BF16),
        in_specs=[in_hbm()] * 6 + [vmem()] * 2,
        out_specs=vmem(),
        scratch_shapes=[
            pltpu.VMEM((tokens, BAND, width), BF16),
            pltpu.VMEM((width, width), BF16),
            pltpu.VMEM((REACH // HEADS, width), BF16),
            pltpu.VMEM((tokens * HEADS, width), F32),
            pltpu.SemaphoreType.DMA((3,)),
            pltpu.SemaphoreType.DMA((5,)),
        ],
        compiler_params=params(60),
        name="pack",
    )(
        pair_features,
        w_query.T,
        w_key.T,
        w_value.T,
        w_out,
        atom_inputs,
        w_bias_t,
        token_row,
    )
    recv = lax.all_to_all(
        pack, ("seq", "col"), 0, 0, tiled=True, axis_index_groups=far_groups
    )

    chunk = width // plane
    share = chunk // HEADS
    pay, rim_far, rim_near, own_part, grad_pair = pl.pallas_call(
        functools.partial(attention_kernel, seqs=seqs, plane=plane),
        out_shape=(
            shape((plane * HEADS * (share + 1), width), F32),
            shape((head // 2, width), F32),
            shape((head, REACH), BF16),
            shape((head, atoms), F32),
            shape(pair_features.shape, BF16),
        ),
        in_specs=[smem(), in_hbm()] + [vmem()] * 9,
        out_specs=(vmem(), vmem(), vmem(), vmem(), in_hbm()),
        scratch_shapes=[
            pltpu.VMEM((tokens, BAND, width), BF16),
            pltpu.VMEM((columns, width), BF16),
            pltpu.VMEM((HEADS * width, width), F32),
            pltpu.VMEM((tokens, 3 * SUB, width), BF16),
            pltpu.SemaphoreType.DMA((3,)),
            pltpu.SemaphoreType.DMA((tokens,)),
            pltpu.SemaphoreType.DMA((3,)),
        ],
        compiler_params=params(32),
        name="attention",
    )(
        window_start,
        pair_features,
        recv,
        near_edge,
        atom_inputs,
        token_row,
        atom_token[:, None],
        counts[None, :],
        atom_cotangent,
        token_cotangent,
        w_bias_t,
    )
    rim_near = lax.ppermute(rim_near, "seq", near)

    whole_planes = [
        [(z * plane + i) * cols + c for i in range(plane) for c in range(cols)]
        for z in range(planes)
    ]
    across = [[z * plane + i for z in range(planes)] for i in range(plane)]
    within = [
        [(z + 1) * plane % seqs] + [z * plane + i for i in range(1, plane)] for z in range(planes)
    ]
    first = lax.all_to_all(
        pay.reshape(plane * HEADS, 1, (share + 1) * width), ("seq", "col"), 0, 0, tiled=True, axis_index_groups=whole_planes
    )
    summed = first.reshape(plane, HEADS, (share + 1) * width).sum(axis=0)
    mains = summed[:, : share * width].reshape(1, chunk * width)
    tail = summed[:, share * width :].sum(axis=0, keepdims=True)
    joined = jnp.concatenate([mains, tail], axis=1)
    second = lax.all_to_all(
        jnp.broadcast_to(joined[None], (planes, 1, joined.shape[1])),
        "seq",
        0,
        0,
        tiled=True,
        axis_index_groups=across,
    ).sum(axis=0)
    partner = jnp.where(odd, seq + 1, seq - 1 + seqs) % plane
    positions = lax.broadcasted_iota(jnp.int32, (plane, 1, 1), 0)
    gathered = jnp.concatenate(
        [
            jnp.broadcast_to(second[:, : chunk * width].reshape(1, chunk, width), (plane, chunk, width)),
            jnp.where(positions == partner, rim_far[None], 0.0),
        ],
        axis=1,
    ).reshape(plane * (chunk + head // 2), width)
    third = lax.all_to_all(gathered, "seq", 0, 0, tiled=True, axis_index_groups=within)
    grad_atoms, gq, gk, gv, go, gb = pl.pallas_call(
        functools.partial(final_kernel, seqs=seqs, chunk=chunk),
        out_shape=(
            shape((head, atoms), BF16),
            shape((head, width), F32),
            shape((head, width), F32),
            shape((head, width), F32),
            shape((head, width), F32),
            shape((1, width), F32),
        ),
        in_specs=[vmem()] * 4,
        out_specs=(vmem(),) * 6,
        compiler_params=params(16),
        name="final",
    )(
        third,
        second[:, chunk * width :],
        own_part,
        rim_near,
    )
    return (grad_atoms.T, grad_pair, gq.T, gk.T, gv.T, go, gb.T)


def solution(mesh):
    placed = (
        P("seq", None),
        P("seq"),
        P("seq"),
        P("seq"),
        P("seq", "col", None),
        P(None, "col"),
        P(None, "col"),
        P(None, "col"),
        P("col", None),
        P(),
        P("seq", None),
        P("seq", None),
    )
    return jax.shard_map(
        per_device,
        mesh=mesh,
        in_specs=placed,
        out_specs=(
            P("seq", "col"),
            P("seq", "col", None),
            P(None, "col"),
            P(None, "col"),
            P(None, "col"),
            P("col", None),
            P(None, "col"),
        ),
        check_vma=False,
    )
```

```python
import functools
import math

import jax
import jax.numpy as jnp
from jax import lax
from jax.experimental import pallas as pl
from jax.experimental.pallas import tpu as pltpu
from jax.sharding import PartitionSpec as P

QUERY_BLOCK = 32
KEY_WINDOW = 128
REACH = 64
SUB = 16
BAND = 64
GROUP = 96
SPAN = GROUP + 2 * REACH
HEADS = 4
F32 = jnp.float32
BF16 = jnp.bfloat16

NN = (((1,), (0,)), ((), ()))
NT = (((1,), (1,)), ((), ()))
TN = (((0,), (0,)), ((), ()))


def mm(a, b, dims=NN):
    return lax.dot_general(a, b, dims, preferred_element_type=F32)


def halves(x):
    high = x.astype(BF16)
    return high, (x - high.astype(F32)).astype(BF16)


def mm2(a, b, dims=NN):
    high, low = halves(a)
    return mm(high, b, dims) + mm(low, b, dims)


def own_thirds(seq, col, width):
    thirds = []
    for part in range(3):
        start = (seq + part - 1) * SUB - col * width
        own = jnp.logical_and(start >= 0, start < width)
        thirds.append((own, pl.multiple_of(jnp.clip(start, 0, width - SUB), SUB)))
    return thirds


def band_copies(seq, col, pair_ref, band, sems):
    copies = []
    for part, (own, safe) in enumerate(own_thirds(seq, col, pair_ref.shape[1])):
        copy = pltpu.make_async_copy(
            pair_ref.at[:, pl.ds(safe, SUB), :],
            band.at[:, pl.ds(part * SUB, SUB), :],
            sems.at[part],
        )
        copies.append((own, safe, copy))
    return copies


def gathered_rows(recv_ref, member, first, count):
    return jnp.concatenate(
        [recv_ref[member + c, first : first + count, :] for c in range(HEADS)], axis=0
    )


def turned_weights(recv_ref, head):
    return (
        gathered_rows(recv_ref, 0, 0, head),
        gathered_rows(recv_ref, 0, head, head),
        gathered_rows(recv_ref, HEADS, 0, head),
    )


def start_band(copies, band):
    tokens = band.shape[0]
    band[:, 3 * SUB :, :] = jnp.zeros((tokens, BAND - 3 * SUB, band.shape[2]), BF16)
    for part, (own, _, copy) in enumerate(copies):

        @pl.when(own)
        def _(copy=copy):
            copy.start()

        @pl.when(jnp.logical_not(own))
        def _(part=part):
            band[:, part * SUB : (part + 1) * SUB, :] = jnp.zeros((tokens, SUB, band.shape[2]), BF16)


def wait_all(copies):
    for own, _, copy in copies:

        @pl.when(own)
        def _(copy=copy):
            copy.wait()


def pad_rows(x, rows):
    return jnp.concatenate([x, jnp.zeros((rows - x.shape[0],) + x.shape[1:], x.dtype)], axis=0)


def pick(condition, one, other):
    return jnp.where(condition, one.astype(F32), other.astype(F32))


def pack_kernel(
    pair_ref,
    wq_ref,
    wk_ref,
    wv_ref,
    wo_ref,
    atoms_ref,
    wb_ref,
    token_row_ref,
    pack_ref,
    band,
    half,
    edge,
    bias,
    band_sems,
    sems,
):
    seq, col = lax.axis_index("seq"), lax.axis_index("col")
    odd = lax.rem(seq, 2) == 1
    copies = band_copies(seq, col, pair_ref, band, band_sems)
    start_band(copies, band)
    tokens = band.shape[0]
    atoms = atoms_ref.shape[0]
    head = wq_ref.shape[0]
    share = REACH // HEADS
    first = jnp.where(odd, atoms - REACH, 0) + col * share
    others = [
        pltpu.make_async_copy(
            atoms_ref.at[pl.ds(pl.multiple_of(first, share), share), :], edge, sems.at[0]
        )
    ] + [
        pltpu.make_async_copy(ref, half.at[i * head : (i + 1) * head, :], sems.at[i + 1])
        for i, ref in enumerate((wq_ref, wk_ref, wv_ref, wo_ref))
    ]
    for copy in others:
        copy.start()
    row = token_row_ref[...]
    code = jnp.where(odd, row[:, atoms - REACH :], row[:, :REACH]) + 1
    line = jnp.concatenate([code >> 6, code & 63], axis=1).astype(F32)
    line = jnp.broadcast_to(line, (share, line.shape[1])).astype(BF16)
    rows = pad_rows(wb_ref[...].astype(F32), 8).astype(BF16)
    for copy in others:
        copy.wait()
    weights = pick(odd, half[: 2 * head, :], half[2 * head :, :]).astype(BF16)
    other = jnp.concatenate(
        [edge[...], line, jnp.zeros((REACH - 2 * share, edge.shape[1]), BF16)], axis=0
    )
    wait_all(copies)
    for t in range(0, tokens, 2):
        part = mm(rows, band[t], NT) + pltpu.roll(mm(rows, band[t + 1], NT), 4, 0)
        high = part.astype(BF16).astype(F32)
        bias[4 * t : 4 * t + 8, :] = jnp.concatenate([high, part - high], axis=1)
    low_tail = pick(odd, bias[...], other).astype(BF16)
    high_tail = pick(odd, other, bias[...]).astype(BF16)
    for c in range(HEADS):
        pack_ref[c] = jnp.concatenate([weights, low_tail], axis=0)
        pack_ref[HEADS + c] = jnp.concatenate([weights, high_tail], axis=0)


def attention_kernel(
    window_ref,
    pair_ref,
    recv_ref,
    near_ref,
    own_ref,
    token_row_ref,
    token_col_ref,
    counts_ref,
    atom_cot_ref,
    token_cot_ref,
    pay_ref,
    grad_q_ref,
    grad_k_ref,
    grad_v_ref,
    upstream_ref,
    token_grad_ref,
    band,
    main,
    band_sems,
    *,
    seqs,
    plane,
):
    seq, col = lax.axis_index("seq"), lax.axis_index("col")
    copies = band_copies(seq, col, pair_ref, band, band_sems)
    start_band(copies, band)
    tokens = band.shape[0]
    odd = lax.rem(seq, 2) == 1
    atoms = own_ref.shape[0]
    width = own_ref.shape[1]
    head = width // HEADS
    inv_root = 1.0 / math.sqrt(head)
    slot_base = seq * atoms
    token_base = seq * tokens
    same = jnp.where(odd, 0, HEADS)
    paired = HEADS - same
    share = REACH // HEADS

    wq_t, wk_t, wv_t = turned_weights(recv_ref, head)
    wo = gathered_rows(recv_ref, HEADS, head, head)
    bias = recv_ref[same, 2 * head :, :].astype(F32)
    for c in range(1, HEADS):
        bias = bias + recv_ref[same + c, 2 * head :, :].astype(F32)
    bias = bias.astype(BF16)

    own = own_ref[...]
    far_rows = jnp.concatenate(
        [recv_ref[paired + c, 2 * head : 2 * head + share, :] for c in range(HEADS)], axis=0
    )
    near_rows = near_ref[:REACH, :]
    has_below, has_above = seq > 0, seq < seqs - 1
    below = jnp.where(has_below, pick(odd, near_rows, far_rows), 0.0).astype(BF16)
    above = jnp.where(has_above, pick(odd, far_rows, near_rows), 0.0).astype(BF16)
    ext = jnp.concatenate([below, own, above], axis=0)
    queries = mm(own, wq_t, NT).astype(BF16)
    keys = mm(ext, wk_t, NT).astype(BF16)
    values = mm(ext, wv_t, NT).astype(BF16)

    token_col = token_col_ref[...]
    live_col = token_col >= 0
    local_col = token_col - token_base
    token_lanes = lax.broadcasted_iota(jnp.int32, (atoms, tokens), 1)
    onehot = (local_col == token_lanes).astype(F32)
    pooled = mm(onehot.astype(BF16), token_cot_ref[...])
    count = jnp.sum(onehot * counts_ref[...].astype(F32), axis=1, keepdims=True)
    safe_count = jnp.where(live_col, count, 1.0)
    upstream = jnp.where(live_col, atom_cot_ref[...].astype(F32) + pooled / safe_count, 0.0)
    upstream = upstream.astype(BF16)
    grad_attended = mm(upstream, wo, NT).astype(BF16)

    def decoded(line):
        row = line.astype(F32)[:1]
        return (row[:, :REACH] * 64.0 + row[:, REACH:]).astype(jnp.int32) - 1

    far_token = decoded(recv_ref[paired, 2 * head + share : 2 * head + 2 * share, :])
    near_token = decoded(near_ref[REACH : REACH + 16, :])
    below_token = jnp.where(has_below, jnp.where(odd, near_token, far_token), -1)
    above_token = jnp.where(has_above, jnp.where(odd, far_token, near_token), -1)
    own_row = token_row_ref[...]
    key_rows = (
        jnp.concatenate([below_token, own_row[:, : SPAN - REACH]], axis=1),
        jnp.concatenate([own_row[:, atoms - (SPAN - REACH) :], above_token], axis=1),
    )
    head_lanes = lax.broadcasted_iota(jnp.int32, (GROUP, width), 1) // head
    head_masks = [head_lanes == h for h in range(HEADS)]

    def stacked(x):
        return jnp.concatenate(
            [jnp.where(mask, x, jnp.zeros_like(x)) for mask in head_masks], axis=0
        )

    def folded(x):
        total = jnp.where(head_masks[0], x[:GROUP], 0.0)
        for h in range(1, HEADS):
            total = total + jnp.where(head_masks[h], x[h * GROUP : (h + 1) * GROUP], 0.0)
        return total

    attended, grad_queries, key_terms, value_terms = [], [], [], []
    token_grad = jnp.zeros((tokens * HEADS, width), F32)
    for g in range(atoms // GROUP):
        rows = slice(g * GROUP, (g + 1) * GROUP)
        span = slice(g * GROUP, g * GROUP + SPAN)
        k_g, v_g = keys[span], values[span]
        q_m = stacked(queries[rows].astype(F32)).astype(BF16)
        a_m = stacked(grad_attended[rows].astype(F32)).astype(BF16)
        key_token = key_rows[g]
        key_live = key_token >= 0
        key_band = jnp.where(key_live, key_token - (token_base - tokens), -1000)
        lane_band = lax.broadcasted_iota(jnp.int32, (width, SPAN), 0)
        key_onehot = ((lane_band & (BAND - 1)) == key_band).astype(F32).astype(BF16)
        local = local_col[rows]
        slot = lax.broadcasted_iota(jnp.int32, (GROUP, tokens * HEADS), 1)
        query_onehot = jnp.concatenate(
            [(slot == local * HEADS + h).astype(F32) for h in range(HEADS)], axis=0
        )
        query_onehot = query_onehot.astype(BF16)
        picked = mm(query_onehot, bias).astype(BF16)
        scores = mm(q_m, k_g, NT) * inv_root + mm(picked, key_onehot)
        scores = scores.reshape(HEADS, GROUP, SPAN)
        block = lax.broadcasted_iota(jnp.int32, (GROUP, 1), 0) // QUERY_BLOCK
        base = slot_base - REACH + g * GROUP
        first = g * (GROUP // QUERY_BLOCK)
        start = jnp.where(
            block == 0,
            window_ref[first] - base,
            jnp.where(block == 1, window_ref[first + 1] - base, window_ref[first + 2] - base),
        )
        position = lax.broadcasted_iota(jnp.int32, (GROUP, SPAN), 1)
        inside = (position >= start) & (position < start + KEY_WINDOW)
        dead_query = local < 0
        allowed = inside & (key_live | dead_query)
        masked = jnp.where(allowed[None], scores, -1e30)
        row_max = jnp.max(masked, axis=-1, keepdims=True)
        raw = jnp.where(allowed[None], jnp.exp(masked - row_max), 0.0)
        weights = raw / jnp.sum(raw, axis=-1, keepdims=True)
        grad_weights = mm(a_m, v_g, NT).reshape(HEADS, GROUP, SPAN)
        inner = jnp.sum(weights * grad_weights, axis=-1, keepdims=True)
        grad_scores = (weights * (grad_weights - inner)).reshape(HEADS * GROUP, SPAN)
        w_low = weights.reshape(HEADS * GROUP, SPAN).astype(BF16)
        s_high, s_low = halves(grad_scores)
        attended.append(folded(mm(w_low, v_g)))
        grad_queries.append(folded(mm(s_high, k_g)) * inv_root)
        key_terms.append(mm(s_high, q_m, TN) * inv_root)
        value_terms.append(mm(w_low, a_m, TN))
        by_token = mm(query_onehot, s_high, TN) + mm(query_onehot, s_low, TN)
        token_grad = token_grad + mm2(by_token, key_onehot, NT)

    attended = jnp.concatenate(attended, axis=0).astype(BF16)
    grad_q = jnp.concatenate(grad_queries, axis=0)

    def overlapped(terms):
        lap = SPAN - GROUP
        return jnp.concatenate(
            [terms[0][:GROUP], terms[0][GROUP:] + terms[1][:lap], terms[1][lap:]], axis=0
        )

    grad_k = overlapped(key_terms)
    grad_v = overlapped(value_terms)

    grad_q_ref[...] = grad_q
    grad_k_ref[...] = grad_k
    grad_v_ref[...] = grad_v
    upstream_ref[...] = upstream
    token_grad_ref[...] = token_grad

    chunk = width // plane
    products = (
        mm2(grad_q, own, TN),
        mm2(grad_k, ext, TN),
        mm2(grad_v, ext, TN),
        mm(attended, upstream, TN),
    )
    per_product = head // chunk
    for i, product in enumerate(products):
        for c in range(HEADS):
            for j in range(per_product):
                to = ((i * per_product + j) * HEADS + c) * chunk
                at = c * head + j * chunk
                main[to : to + chunk, :] = product[at : at + chunk]
    wait_all(copies)
    w_bias_grad = jnp.zeros((8, width), F32)
    left = lax.broadcasted_iota(jnp.int32, (8, width), 1) < BAND
    for t in range(0, tokens, 2):
        two = token_grad[HEADS * t : HEADS * t + 8]
        two = jnp.where(left, two, pltpu.roll(two, 4, 0))
        stack = jnp.concatenate([band[t], band[t + 1]], axis=0)
        w_bias_grad = w_bias_grad + mm2(two, stack)
    upper = lax.broadcasted_iota(jnp.int32, (8, width), 0) < HEADS
    spread = jnp.where(upper, w_bias_grad, pltpu.roll(w_bias_grad, 4, 0))
    share = chunk // HEADS
    for j in range(share):
        pay_ref[pl.ds(j, plane * HEADS, stride=share + 1), :] = main[
            pl.ds(col * share + j, plane * HEADS, stride=chunk), :
        ]
    pay_ref[pl.ds(share, plane * HEADS, stride=share + 1), :] = jnp.concatenate(
        [spread] * (plane * HEADS // 8), axis=0
    )


def turned_kernel(
    recv_ref,
    wb_ref,
    grad_q_ref,
    grad_k_ref,
    grad_v_ref,
    upstream_ref,
    token_grad_ref,
    rim_far_ref,
    rim_near_ref,
    own_out_ref,
    grad_pair_ref,
    zeros,
    grad_band,
    zero_sems,
    out_sems,
):
    seq, col = lax.axis_index("seq"), lax.axis_index("col")
    odd = lax.rem(seq, 2) == 1
    tokens = grad_band.shape[0]
    zeros[...] = jnp.zeros(zeros.shape, BF16)
    fills = [
        pltpu.make_async_copy(zeros, grad_pair_ref.at[t], zero_sems.at[t]) for t in range(tokens)
    ]
    for fill in fills:
        fill.start()
    atoms, width = grad_q_ref.shape
    head = width // HEADS

    rows = pad_rows(wb_ref[...].astype(F32), 8)
    turned = pad_rows(token_grad_ref[...], width).T[: 3 * SUB]
    for t in range(tokens):
        at = HEADS * t
        total = turned[:, at : at + 1] * rows[0:1]
        for h in range(1, HEADS):
            total = total + turned[:, at + h : at + h + 1] * rows[h : h + 1]
        grad_band[t] = total.astype(BF16)

    wq_t, wk_t, wv_t = turned_weights(recv_ref, head)
    key_part = mm2(grad_k_ref[...], wk_t) + mm2(grad_v_ref[...], wv_t)
    query_part = mm2(grad_q_ref[...], wq_t) + upstream_ref[...].astype(F32)
    shift = lax.rem(width - col * head, width)
    whole = jnp.concatenate(
        [key_part[REACH : REACH + atoms] + query_part, key_part[:REACH]]
        + [key_part[REACH + atoms :], jnp.zeros((REACH, width), F32)],
        axis=0,
    )
    whole = pltpu.roll(whole, shift, 1).T[:head]
    own_out_ref[...] = whole[:, :atoms]
    rim_down = whole[:, atoms : atoms + REACH]
    rim_up = whole[:, atoms + REACH : atoms + 2 * REACH]
    rim_far = jnp.where(odd, rim_up, rim_down)
    rim_far_ref[...] = jnp.concatenate([rim_far[: head // 2], rim_far[head // 2 :]], axis=1)
    rim_near_ref[...] = jnp.where(odd, rim_down, rim_up).astype(BF16)
    for fill in fills:
        fill.wait()
    outs = []
    for part, (own_part, safe) in enumerate(own_thirds(seq, col, grad_pair_ref.shape[1])):
        copy = pltpu.make_async_copy(
            grad_band.at[:, pl.ds(part * SUB, SUB), :],
            grad_pair_ref.at[:, pl.ds(safe, SUB), :],
            out_sems.at[part],
        )
        outs.append((own_part, safe, copy))

        @pl.when(own_part)
        def _(copy=copy):
            copy.start()

    wait_all(outs)


def final_kernel(
    gathered_ref,
    bias_ref,
    own_ref,
    near_ref,
    atoms_ref,
    gq_ref,
    gk_ref,
    gv_ref,
    go_ref,
    gb_ref,
    *,
    seqs,
    chunk,
):
    head, atoms = atoms_ref.shape
    seq = lax.axis_index("seq")
    odd = lax.rem(seq, 2) == 1
    rim_rows = head // 2
    rows = chunk + rim_rows
    plane = gathered_ref.shape[0] // rows
    partner = lax.rem(jnp.where(odd, seq + 1, seq - 1 + seqs), plane)
    far = gathered_ref[pl.ds(pl.multiple_of(partner * rows + chunk, 8), rim_rows), :]
    far = jnp.concatenate([far[:, :REACH], far[:, REACH:]], axis=0)
    far = jnp.where(jnp.where(odd, seq + 1, seq) % seqs == 0, 0.0, far)
    near = near_ref[...].astype(F32)
    below, above = jnp.where(odd, near, far), jnp.where(odd, far, near)
    middle = jnp.zeros((head, atoms - 2 * REACH), F32)
    atoms_ref[...] = (own_ref[...] + jnp.concatenate([below, middle, above], axis=1)).astype(BF16)
    main = jnp.concatenate(
        [gathered_ref[p * rows : p * rows + chunk, :] for p in range(plane)], axis=0
    )
    for i, ref in enumerate((gq_ref, gk_ref, gv_ref, go_ref)):
        ref[...] = main[i * head : (i + 1) * head]
    gb_ref[...] = bias_ref[...]


def vmem():
    return pl.BlockSpec(memory_space=pltpu.VMEM)


def smem():
    return pl.BlockSpec(memory_space=pltpu.SMEM)


def in_hbm():
    return pl.BlockSpec(memory_space=pltpu.MemorySpace.HBM)


def shape(dims, dtype):
    return jax.ShapeDtypeStruct(dims, dtype)


def params(mebibytes):
    return pltpu.CompilerParams(vmem_limit_bytes=mebibytes * 1024 * 1024)


def per_device(
    atom_inputs,
    atom_token,
    counts,
    window_start,
    pair_features,
    w_query,
    w_key,
    w_value,
    w_out,
    w_bias,
    atom_cotangent,
    token_cotangent,
):
    atoms, width = atom_inputs.shape
    tokens, columns, _ = pair_features.shape
    head = w_query.shape[1]
    seqs = lax.axis_size("seq")
    plane = 16 if seqs % 16 == 0 else 4
    planes = seqs // plane
    cols = lax.axis_size("col")
    seq = lax.axis_index("seq")
    odd = seq % 2 == 1
    token_row = atom_token[None, :]

    near = [(i, i ^ 1) for i in range(seqs)]
    far_groups = [
        [n * cols + c for n in (i, (i + 1) % seqs) for c in range(cols)] for i in range(1, seqs, 2)
    ]
    edge_start = jnp.where(odd, 0, atoms - REACH)
    code = lax.dynamic_slice(atom_token, (edge_start,), (REACH,)) + 1
    line = jnp.concatenate([code // 64, code % 64]).astype(BF16)[None]
    edge = lax.dynamic_slice(atom_inputs, (edge_start, 0), (REACH, width))
    near_edge = lax.ppermute(
        jnp.concatenate([edge, line, jnp.zeros((15, width), BF16)], axis=0), "seq", near
    )
    w_bias_t = w_bias.T
    pack = pl.pallas_call(
        pack_kernel,
        out_shape=shape((2 * HEADS, width, width), BF16),
        in_specs=[in_hbm()] * 6 + [vmem()] * 2,
        out_specs=vmem(),
        scratch_shapes=[
            pltpu.VMEM((tokens, BAND, width), BF16),
            pltpu.VMEM((width, width), BF16),
            pltpu.VMEM((REACH // HEADS, width), BF16),
            pltpu.VMEM((tokens * HEADS, width), F32),
            pltpu.SemaphoreType.DMA((3,)),
            pltpu.SemaphoreType.DMA((5,)),
        ],
        compiler_params=params(60),
        name="pack",
    )(
        pair_features,
        w_query.T,
        w_key.T,
        w_value.T,
        w_out,
        atom_inputs,
        w_bias_t,
        token_row,
    )
    pack, near_edge = lax.optimization_barrier((pack, near_edge))
    recv = lax.all_to_all(
        pack, ("seq", "col"), 0, 0, tiled=True, axis_index_groups=far_groups
    )

    chunk = width // plane
    share = chunk // HEADS
    pay, *parts = pl.pallas_call(
        functools.partial(attention_kernel, seqs=seqs, plane=plane),
        out_shape=(
            shape((plane * HEADS * (share + 1), width), F32),
            shape((atoms, width), F32),
            shape((atoms + 2 * REACH, width), F32),
            shape((atoms + 2 * REACH, width), F32),
            shape((atoms, width), BF16),
            shape((tokens * HEADS, width), F32),
        ),
        in_specs=[smem(), in_hbm()] + [vmem()] * 8,
        out_specs=(vmem(),) * 6,
        scratch_shapes=[
            pltpu.VMEM((tokens, BAND, width), BF16),
            pltpu.VMEM((HEADS * width, width), F32),
            pltpu.SemaphoreType.DMA((3,)),
        ],
        compiler_params=params(32),
        name="attention",
    )(
        window_start,
        pair_features,
        recv,
        near_edge,
        atom_inputs,
        token_row,
        atom_token[:, None],
        counts[None, :],
        atom_cotangent,
        token_cotangent,
    )
    rim_far, rim_near, own_part, grad_pair = pl.pallas_call(
        turned_kernel,
        out_shape=(
            shape((head // 2, width), F32),
            shape((head, REACH), BF16),
            shape((head, atoms), F32),
            shape(pair_features.shape, BF16),
        ),
        in_specs=[vmem()] * 7,
        out_specs=(vmem(), vmem(), vmem(), in_hbm()),
        scratch_shapes=[
            pltpu.VMEM((columns, width), BF16),
            pltpu.VMEM((tokens, 3 * SUB, width), BF16),
            pltpu.SemaphoreType.DMA((tokens,)),
            pltpu.SemaphoreType.DMA((3,)),
        ],
        compiler_params=params(32),
        name="turned",
    )(recv, w_bias_t, *parts)

    whole_planes = [
        [(z * plane + i) * cols + c for i in range(plane) for c in range(cols)]
        for z in range(planes)
    ]
    across = [[z * plane + i for z in range(planes)] for i in range(plane)]
    within = [
        [(z + 1) * plane % seqs] + [z * plane + i for i in range(1, plane)] for z in range(planes)
    ]
    first = lax.all_to_all(
        pay.reshape(plane * HEADS, 1, (share + 1) * width), ("seq", "col"), 0, 0, tiled=True, axis_index_groups=whole_planes
    )
    summed = first.reshape(plane, HEADS, (share + 1) * width).sum(axis=0)
    mains = summed[:, : share * width].reshape(1, chunk * width)
    tail = summed[:, share * width :].sum(axis=0, keepdims=True)
    joined = jnp.concatenate([mains, tail], axis=1)
    joined, rim_near = lax.optimization_barrier((joined, rim_near))
    rim_near = lax.ppermute(rim_near, "seq", near)
    second = lax.all_to_all(
        jnp.broadcast_to(joined[None], (planes, 1, joined.shape[1])),
        "seq",
        0,
        0,
        tiled=True,
        axis_index_groups=across,
    ).sum(axis=0)
    second, rim_near = lax.optimization_barrier((second, rim_near))
    partner = jnp.where(odd, seq + 1, seq - 1 + seqs) % plane
    positions = lax.broadcasted_iota(jnp.int32, (plane, 1, 1), 0)
    gathered = jnp.concatenate(
        [
            jnp.broadcast_to(second[:, : chunk * width].reshape(1, chunk, width), (plane, chunk, width)),
            jnp.where(positions == partner, rim_far[None], 0.0),
        ],
        axis=1,
    ).reshape(plane * (chunk + head // 2), width)
    third = lax.all_to_all(gathered, "seq", 0, 0, tiled=True, axis_index_groups=within)
    grad_atoms, gq, gk, gv, go, gb = pl.pallas_call(
        functools.partial(final_kernel, seqs=seqs, chunk=chunk),
        out_shape=(
            shape((head, atoms), BF16),
            shape((head, width), F32),
            shape((head, width), F32),
            shape((head, width), F32),
            shape((head, width), F32),
            shape((1, width), F32),
        ),
        in_specs=[vmem()] * 4,
        out_specs=(vmem(),) * 6,
        compiler_params=params(16),
        name="final",
    )(
        third,
        second[:, chunk * width :],
        own_part,
        rim_near,
    )
    return (grad_atoms.T, grad_pair, gq.T, gk.T, gv.T, go, gb.T)


def solution(mesh):
    placed = (
        P("seq", None),
        P("seq"),
        P("seq"),
        P("seq"),
        P("seq", "col", None),
        P(None, "col"),
        P(None, "col"),
        P(None, "col"),
        P("col", None),
        P(),
        P("seq", None),
        P("seq", None),
    )
    return jax.shard_map(
        per_device,
        mesh=mesh,
        in_specs=placed,
        out_specs=(
            P("seq", "col"),
            P("seq", "col", None),
            P(None, "col"),
            P(None, "col"),
            P(None, "col"),
            P("col", None),
            P(None, "col"),
        ),
        check_vma=False,
    )
```

```python
import functools
import math

import jax
import jax.numpy as jnp
from jax import lax
from jax.experimental import pallas as pl
from jax.experimental.pallas import tpu as pltpu
from jax.sharding import PartitionSpec as P

QUERY_BLOCK = 32
KEY_WINDOW = 128
REACH = 64
SUB = 16
BAND = 64
GROUP = 96
SPAN = GROUP + 2 * REACH
HEADS = 4
F32 = jnp.float32
BF16 = jnp.bfloat16

NN = (((1,), (0,)), ((), ()))
NT = (((1,), (1,)), ((), ()))
TN = (((0,), (0,)), ((), ()))


def mm(a, b, dims=NN):
    return lax.dot_general(a, b, dims, preferred_element_type=F32)


def halves(x):
    high = x.astype(BF16)
    return high, (x - high.astype(F32)).astype(BF16)


def mm2(a, b, dims=NN):
    high, low = halves(a)
    return mm(high, b, dims) + mm(low, b, dims)


def own_thirds(seq, col, width):
    thirds = []
    for part in range(3):
        start = (seq + part - 1) * SUB - col * width
        own = jnp.logical_and(start >= 0, start < width)
        thirds.append((own, pl.multiple_of(jnp.clip(start, 0, width - SUB), SUB)))
    return thirds


def band_copies(seq, col, pair_ref, band, sems):
    copies = []
    for part, (own, safe) in enumerate(own_thirds(seq, col, pair_ref.shape[1])):
        copy = pltpu.make_async_copy(
            pair_ref.at[:, pl.ds(safe, SUB), :],
            band.at[:, pl.ds(part * SUB, SUB), :],
            sems.at[part],
        )
        copies.append((own, safe, copy))
    return copies


def gathered_rows(recv_ref, member, first, count):
    return jnp.concatenate(
        [recv_ref[member + c, first : first + count, :] for c in range(HEADS)], axis=0
    )


def turned_weights(recv_ref, head):
    return (
        gathered_rows(recv_ref, 0, 0, head),
        gathered_rows(recv_ref, 0, head, head),
        gathered_rows(recv_ref, HEADS, 0, head),
    )


def start_band(copies, band):
    tokens = band.shape[0]
    band[:, 3 * SUB :, :] = jnp.zeros((tokens, BAND - 3 * SUB, band.shape[2]), BF16)
    for part, (own, _, copy) in enumerate(copies):

        @pl.when(own)
        def _(copy=copy):
            copy.start()

        @pl.when(jnp.logical_not(own))
        def _(part=part):
            band[:, part * SUB : (part + 1) * SUB, :] = jnp.zeros((tokens, SUB, band.shape[2]), BF16)


def wait_all(copies):
    for own, _, copy in copies:

        @pl.when(own)
        def _(copy=copy):
            copy.wait()


def pad_rows(x, rows):
    return jnp.concatenate([x, jnp.zeros((rows - x.shape[0],) + x.shape[1:], x.dtype)], axis=0)


def pick(condition, one, other):
    return jnp.where(condition, one.astype(F32), other.astype(F32))


def pack_kernel(
    pair_ref,
    wq_ref,
    wk_ref,
    wv_ref,
    wo_ref,
    atoms_ref,
    wb_ref,
    token_row_ref,
    pack_ref,
    band,
    half,
    edge,
    bias,
    band_sems,
    sems,
):
    seq, col = lax.axis_index("seq"), lax.axis_index("col")
    odd = lax.rem(seq, 2) == 1
    copies = band_copies(seq, col, pair_ref, band, band_sems)
    start_band(copies, band)
    tokens = band.shape[0]
    atoms = atoms_ref.shape[0]
    head = wq_ref.shape[0]
    share = REACH // HEADS
    first = jnp.where(odd, atoms - REACH, 0) + col * share
    others = [
        pltpu.make_async_copy(
            atoms_ref.at[pl.ds(pl.multiple_of(first, share), share), :], edge, sems.at[0]
        )
    ] + [
        pltpu.make_async_copy(ref, half.at[i * head : (i + 1) * head, :], sems.at[i + 1])
        for i, ref in enumerate((wq_ref, wk_ref, wv_ref, wo_ref))
    ]
    for copy in others:
        copy.start()
    row = token_row_ref[...]
    code = jnp.where(odd, row[:, atoms - REACH :], row[:, :REACH]) + 1
    line = jnp.concatenate([code >> 6, code & 63], axis=1).astype(F32)
    line = jnp.broadcast_to(line, (share, line.shape[1])).astype(BF16)
    rows = pad_rows(wb_ref[...].astype(F32), 8).astype(BF16)
    for copy in others:
        copy.wait()
    weights = pick(odd, half[: 2 * head, :], half[2 * head :, :]).astype(BF16)
    other = jnp.concatenate(
        [edge[...], line, jnp.zeros((REACH - 2 * share, edge.shape[1]), BF16)], axis=0
    )
    wait_all(copies)
    for t in range(0, tokens, 2):
        part = mm(rows, band[t], NT) + pltpu.roll(mm(rows, band[t + 1], NT), 4, 0)
        high = part.astype(BF16).astype(F32)
        bias[4 * t : 4 * t + 8, :] = jnp.concatenate([high, part - high], axis=1)
    low_tail = pick(odd, bias[...], other).astype(BF16)
    high_tail = pick(odd, other, bias[...]).astype(BF16)
    for c in range(HEADS):
        pack_ref[c] = jnp.concatenate([weights, low_tail], axis=0)
        pack_ref[HEADS + c] = jnp.concatenate([weights, high_tail], axis=0)


def attention_kernel(
    window_ref,
    pair_ref,
    recv_ref,
    near_ref,
    own_ref,
    token_row_ref,
    token_col_ref,
    counts_ref,
    atom_cot_ref,
    token_cot_ref,
    pay_ref,
    grad_q_ref,
    grad_k_ref,
    grad_v_ref,
    upstream_ref,
    token_grad_ref,
    band,
    main,
    band_sems,
    *,
    seqs,
    plane,
):
    seq, col = lax.axis_index("seq"), lax.axis_index("col")
    copies = band_copies(seq, col, pair_ref, band, band_sems)
    start_band(copies, band)
    tokens = band.shape[0]
    odd = lax.rem(seq, 2) == 1
    atoms = own_ref.shape[0]
    width = own_ref.shape[1]
    head = width // HEADS
    inv_root = 1.0 / math.sqrt(head)
    slot_base = seq * atoms
    token_base = seq * tokens
    same = jnp.where(odd, 0, HEADS)
    paired = HEADS - same
    share = REACH // HEADS

    wq_t, wk_t, wv_t = turned_weights(recv_ref, head)
    wo = gathered_rows(recv_ref, HEADS, head, head)
    bias = recv_ref[same, 2 * head :, :].astype(F32)
    for c in range(1, HEADS):
        bias = bias + recv_ref[same + c, 2 * head :, :].astype(F32)
    bias = bias.astype(BF16)

    own = own_ref[...]
    far_rows = jnp.concatenate(
        [recv_ref[paired + c, 2 * head : 2 * head + share, :] for c in range(HEADS)], axis=0
    )
    near_rows = near_ref[:REACH, :]
    has_below, has_above = seq > 0, seq < seqs - 1
    below = jnp.where(has_below, pick(odd, near_rows, far_rows), 0.0).astype(BF16)
    above = jnp.where(has_above, pick(odd, far_rows, near_rows), 0.0).astype(BF16)
    ext = jnp.concatenate([below, own, above], axis=0)
    queries = mm(own, wq_t, NT).astype(BF16)
    keys = mm(ext, wk_t, NT).astype(BF16)
    values = mm(ext, wv_t, NT).astype(BF16)

    token_col = token_col_ref[...]
    live_col = token_col >= 0
    local_col = token_col - token_base
    token_lanes = lax.broadcasted_iota(jnp.int32, (atoms, tokens), 1)
    onehot = (local_col == token_lanes).astype(F32)
    pooled = mm(onehot.astype(BF16), token_cot_ref[...])
    count = jnp.sum(onehot * counts_ref[...].astype(F32), axis=1, keepdims=True)
    safe_count = jnp.where(live_col, count, 1.0)
    upstream = jnp.where(live_col, atom_cot_ref[...].astype(F32) + pooled / safe_count, 0.0)
    upstream = upstream.astype(BF16)
    grad_attended = mm(upstream, wo, NT).astype(BF16)

    def decoded(line):
        row = line.astype(F32)[:1]
        return (row[:, :REACH] * 64.0 + row[:, REACH:]).astype(jnp.int32) - 1

    far_token = decoded(recv_ref[paired, 2 * head + share : 2 * head + 2 * share, :])
    near_token = decoded(near_ref[REACH : REACH + 16, :])
    below_token = jnp.where(has_below, jnp.where(odd, near_token, far_token), -1)
    above_token = jnp.where(has_above, jnp.where(odd, far_token, near_token), -1)
    own_row = token_row_ref[...]
    key_rows = (
        jnp.concatenate([below_token, own_row[:, : SPAN - REACH]], axis=1),
        jnp.concatenate([own_row[:, atoms - (SPAN - REACH) :], above_token], axis=1),
    )
    head_lanes = lax.broadcasted_iota(jnp.int32, (GROUP, width), 1) // head
    head_masks = [head_lanes == h for h in range(HEADS)]

    def stacked(x):
        return jnp.concatenate(
            [jnp.where(mask, x, jnp.zeros_like(x)) for mask in head_masks], axis=0
        )

    def folded(x):
        total = jnp.where(head_masks[0], x[:GROUP], 0.0)
        for h in range(1, HEADS):
            total = total + jnp.where(head_masks[h], x[h * GROUP : (h + 1) * GROUP], 0.0)
        return total

    attended, grad_queries, key_terms, value_terms = [], [], [], []
    token_grad = jnp.zeros((tokens * HEADS, width), F32)
    for g in range(atoms // GROUP):
        rows = slice(g * GROUP, (g + 1) * GROUP)
        span = slice(g * GROUP, g * GROUP + SPAN)
        k_g, v_g = keys[span], values[span]
        q_m = stacked(queries[rows].astype(F32)).astype(BF16)
        a_m = stacked(grad_attended[rows].astype(F32)).astype(BF16)
        key_token = key_rows[g]
        key_live = key_token >= 0
        key_band = jnp.where(key_live, key_token - (token_base - tokens), -1000)
        lane_band = lax.broadcasted_iota(jnp.int32, (width, SPAN), 0)
        key_onehot = ((lane_band & (BAND - 1)) == key_band).astype(F32).astype(BF16)
        local = local_col[rows]
        slot = lax.broadcasted_iota(jnp.int32, (GROUP, tokens * HEADS), 1)
        query_onehot = jnp.concatenate(
            [(slot == local * HEADS + h).astype(F32) for h in range(HEADS)], axis=0
        )
        query_onehot = query_onehot.astype(BF16)
        picked = mm(query_onehot, bias).astype(BF16)
        scores = mm(q_m, k_g, NT) * inv_root + mm(picked, key_onehot)
        scores = scores.reshape(HEADS, GROUP, SPAN)
        block = lax.broadcasted_iota(jnp.int32, (GROUP, 1), 0) // QUERY_BLOCK
        base = slot_base - REACH + g * GROUP
        first = g * (GROUP // QUERY_BLOCK)
        start = jnp.where(
            block == 0,
            window_ref[first] - base,
            jnp.where(block == 1, window_ref[first + 1] - base, window_ref[first + 2] - base),
        )
        position = lax.broadcasted_iota(jnp.int32, (GROUP, SPAN), 1)
        inside = (position >= start) & (position < start + KEY_WINDOW)
        dead_query = local < 0
        allowed = inside & (key_live | dead_query)
        masked = jnp.where(allowed[None], scores, -1e30)
        row_max = jnp.max(masked, axis=-1, keepdims=True)
        raw = jnp.where(allowed[None], jnp.exp(masked - row_max), 0.0)
        weights = raw / jnp.sum(raw, axis=-1, keepdims=True)
        grad_weights = mm(a_m, v_g, NT).reshape(HEADS, GROUP, SPAN)
        inner = jnp.sum(weights * grad_weights, axis=-1, keepdims=True)
        grad_scores = (weights * (grad_weights - inner)).reshape(HEADS * GROUP, SPAN)
        w_low = weights.reshape(HEADS * GROUP, SPAN).astype(BF16)
        s_high, s_low = halves(grad_scores)
        attended.append(folded(mm(w_low, v_g)))
        grad_queries.append(folded(mm(s_high, k_g)) * inv_root)
        key_terms.append(mm(s_high, q_m, TN) * inv_root)
        value_terms.append(mm(w_low, a_m, TN))
        by_token = mm(query_onehot, s_high, TN) + mm(query_onehot, s_low, TN)
        token_grad = token_grad + mm2(by_token, key_onehot, NT)

    attended = jnp.concatenate(attended, axis=0).astype(BF16)
    grad_q = jnp.concatenate(grad_queries, axis=0)

    def overlapped(terms):
        lap = SPAN - GROUP
        return jnp.concatenate(
            [terms[0][:GROUP], terms[0][GROUP:] + terms[1][:lap], terms[1][lap:]], axis=0
        )

    grad_k = overlapped(key_terms)
    grad_v = overlapped(value_terms)

    grad_q_ref[...] = grad_q
    grad_k_ref[...] = grad_k
    grad_v_ref[...] = grad_v
    upstream_ref[...] = upstream
    token_grad_ref[...] = token_grad

    chunk = width // plane
    products = (
        mm2(grad_q, own, TN),
        mm2(grad_k, ext, TN),
        mm2(grad_v, ext, TN),
        mm(attended, upstream, TN),
    )
    per_product = head // chunk
    for i, product in enumerate(products):
        for c in range(HEADS):
            for j in range(per_product):
                to = ((i * per_product + j) * HEADS + c) * chunk
                at = c * head + j * chunk
                main[to : to + chunk, :] = product[at : at + chunk]
    wait_all(copies)
    w_bias_grad = jnp.zeros((8, width), F32)
    left = lax.broadcasted_iota(jnp.int32, (8, width), 1) < BAND
    for t in range(0, tokens, 2):
        two = token_grad[HEADS * t : HEADS * t + 8]
        two = jnp.where(left, two, pltpu.roll(two, 4, 0))
        stack = jnp.concatenate([band[t], band[t + 1]], axis=0)
        w_bias_grad = w_bias_grad + mm2(two, stack)
    upper = lax.broadcasted_iota(jnp.int32, (8, width), 0) < HEADS
    spread = jnp.where(upper, w_bias_grad, pltpu.roll(w_bias_grad, 4, 0))
    share = chunk // HEADS
    for j in range(share):
        pay_ref[pl.ds(j, plane * HEADS, stride=share + 1), :] = main[
            pl.ds(col * share + j, plane * HEADS, stride=chunk), :
        ]
    pay_ref[pl.ds(share, plane * HEADS, stride=share + 1), :] = jnp.concatenate(
        [spread] * (plane * HEADS // 8), axis=0
    )


def turned_kernel(
    recv_ref,
    wb_ref,
    grad_q_ref,
    grad_k_ref,
    grad_v_ref,
    upstream_ref,
    token_grad_ref,
    rim_far_ref,
    rim_near_ref,
    own_out_ref,
    grad_pair_ref,
    zeros,
    grad_band,
    zero_sems,
    out_sems,
):
    seq, col = lax.axis_index("seq"), lax.axis_index("col")
    odd = lax.rem(seq, 2) == 1
    tokens = grad_band.shape[0]
    zeros[...] = jnp.zeros(zeros.shape, BF16)
    fills = [
        pltpu.make_async_copy(zeros, grad_pair_ref.at[t], zero_sems.at[t]) for t in range(tokens)
    ]
    for fill in fills:
        fill.start()
    atoms, width = grad_q_ref.shape
    head = width // HEADS

    rows = pad_rows(wb_ref[...].astype(F32), 8)
    turned = pad_rows(token_grad_ref[...], width).T[: 3 * SUB]
    for t in range(tokens):
        at = HEADS * t
        total = turned[:, at : at + 1] * rows[0:1]
        for h in range(1, HEADS):
            total = total + turned[:, at + h : at + h + 1] * rows[h : h + 1]
        grad_band[t] = total.astype(BF16)

    wq_t, wk_t, wv_t = turned_weights(recv_ref, head)
    key_part = mm2(grad_k_ref[...], wk_t) + mm2(grad_v_ref[...], wv_t)
    query_part = mm2(grad_q_ref[...], wq_t) + upstream_ref[...].astype(F32)
    shift = lax.rem(width - col * head, width)
    whole = jnp.concatenate(
        [key_part[REACH : REACH + atoms] + query_part, key_part[:REACH]]
        + [key_part[REACH + atoms :], jnp.zeros((REACH, width), F32)],
        axis=0,
    )
    whole = pltpu.roll(whole, shift, 1).T[:head]
    own_out_ref[...] = whole[:, :atoms]
    rim_down = whole[:, atoms : atoms + REACH]
    rim_up = whole[:, atoms + REACH : atoms + 2 * REACH]
    rim_far = jnp.where(odd, rim_up, rim_down)
    rim_far_ref[...] = jnp.concatenate([rim_far[: head // 2], rim_far[head // 2 :]], axis=1)
    rim_near_ref[...] = jnp.where(odd, rim_down, rim_up).astype(BF16)
    for fill in fills:
        fill.wait()
    outs = []
    for part, (own_part, safe) in enumerate(own_thirds(seq, col, grad_pair_ref.shape[1])):
        copy = pltpu.make_async_copy(
            grad_band.at[:, pl.ds(part * SUB, SUB), :],
            grad_pair_ref.at[:, pl.ds(safe, SUB), :],
            out_sems.at[part],
        )
        outs.append((own_part, safe, copy))

        @pl.when(own_part)
        def _(copy=copy):
            copy.start()

    wait_all(outs)


def final_kernel(
    gathered_ref,
    bias_ref,
    own_ref,
    near_ref,
    atoms_ref,
    gq_ref,
    gk_ref,
    gv_ref,
    go_ref,
    gb_ref,
    *,
    seqs,
    chunk,
):
    head, atoms = atoms_ref.shape
    seq = lax.axis_index("seq")
    odd = lax.rem(seq, 2) == 1
    rim_rows = head // 2
    rows = chunk + rim_rows
    plane = gathered_ref.shape[0] // rows
    partner = lax.rem(jnp.where(odd, seq + 1, seq - 1 + seqs), plane)
    far = gathered_ref[pl.ds(pl.multiple_of(partner * rows + chunk, 8), rim_rows), :]
    far = jnp.concatenate([far[:, :REACH], far[:, REACH:]], axis=0)
    far = jnp.where(jnp.where(odd, seq + 1, seq) % seqs == 0, 0.0, far)
    near = near_ref[...].astype(F32)
    below, above = jnp.where(odd, near, far), jnp.where(odd, far, near)
    middle = jnp.zeros((head, atoms - 2 * REACH), F32)
    atoms_ref[...] = (own_ref[...] + jnp.concatenate([below, middle, above], axis=1)).astype(BF16)
    main = jnp.concatenate(
        [gathered_ref[p * rows : p * rows + chunk, :] for p in range(plane)], axis=0
    )
    for i, ref in enumerate((gq_ref, gk_ref, gv_ref, go_ref)):
        ref[...] = main[i * head : (i + 1) * head]
    gb_ref[...] = bias_ref[...]


def vmem():
    return pl.BlockSpec(memory_space=pltpu.VMEM)


def smem():
    return pl.BlockSpec(memory_space=pltpu.SMEM)


def in_hbm():
    return pl.BlockSpec(memory_space=pltpu.MemorySpace.HBM)


def shape(dims, dtype):
    return jax.ShapeDtypeStruct(dims, dtype)


def params(mebibytes):
    return pltpu.CompilerParams(vmem_limit_bytes=mebibytes * 1024 * 1024)


def per_device(
    atom_inputs,
    atom_token,
    counts,
    window_start,
    pair_features,
    w_query,
    w_key,
    w_value,
    w_out,
    w_bias,
    atom_cotangent,
    token_cotangent,
):
    atoms, width = atom_inputs.shape
    tokens, columns, _ = pair_features.shape
    head = w_query.shape[1]
    seqs = lax.axis_size("seq")
    plane = 16 if seqs % 16 == 0 else 4
    planes = seqs // plane
    cols = lax.axis_size("col")
    seq = lax.axis_index("seq")
    odd = seq % 2 == 1
    token_row = atom_token[None, :]

    near = [(i, i ^ 1) for i in range(seqs)]
    far_groups = [
        [n * cols + c for n in (i, (i + 1) % seqs) for c in range(cols)] for i in range(1, seqs, 2)
    ]
    edge_start = jnp.where(odd, 0, atoms - REACH)
    code = lax.dynamic_slice(atom_token, (edge_start,), (REACH,)) + 1
    line = jnp.concatenate([code // 64, code % 64]).astype(BF16)[None]
    edge = lax.dynamic_slice(atom_inputs, (edge_start, 0), (REACH, width))
    near_edge = lax.ppermute(
        jnp.concatenate([edge, line, jnp.zeros((15, width), BF16)], axis=0), "seq", near
    )
    w_bias_t = w_bias.T
    pack = pl.pallas_call(
        pack_kernel,
        out_shape=shape((2 * HEADS, width, width), BF16),
        in_specs=[in_hbm()] * 6 + [vmem()] * 2,
        out_specs=vmem(),
        scratch_shapes=[
            pltpu.VMEM((tokens, BAND, width), BF16),
            pltpu.VMEM((width, width), BF16),
            pltpu.VMEM((REACH // HEADS, width), BF16),
            pltpu.VMEM((tokens * HEADS, width), F32),
            pltpu.SemaphoreType.DMA((3,)),
            pltpu.SemaphoreType.DMA((5,)),
        ],
        compiler_params=params(60),
        name="pack",
    )(
        pair_features,
        w_query.T,
        w_key.T,
        w_value.T,
        w_out,
        atom_inputs,
        w_bias_t,
        token_row,
    )
    recv = lax.all_to_all(
        pack, ("seq", "col"), 0, 0, tiled=True, axis_index_groups=far_groups
    )

    chunk = width // plane
    share = chunk // HEADS
    pay, *parts = pl.pallas_call(
        functools.partial(attention_kernel, seqs=seqs, plane=plane),
        out_shape=(
            shape((plane * HEADS * (share + 1), width), F32),
            shape((atoms, width), F32),
            shape((atoms + 2 * REACH, width), F32),
            shape((atoms + 2 * REACH, width), F32),
            shape((atoms, width), BF16),
            shape((tokens * HEADS, width), F32),
        ),
        in_specs=[smem(), in_hbm()] + [vmem()] * 8,
        out_specs=(vmem(),) * 6,
        scratch_shapes=[
            pltpu.VMEM((tokens, BAND, width), BF16),
            pltpu.VMEM((HEADS * width, width), F32),
            pltpu.SemaphoreType.DMA((3,)),
        ],
        compiler_params=params(32),
        name="attention",
    )(
        window_start,
        pair_features,
        recv,
        near_edge,
        atom_inputs,
        token_row,
        atom_token[:, None],
        counts[None, :],
        atom_cotangent,
        token_cotangent,
    )
    rim_far, rim_near, own_part, grad_pair = pl.pallas_call(
        turned_kernel,
        out_shape=(
            shape((head // 2, width), F32),
            shape((head, REACH), BF16),
            shape((head, atoms), F32),
            shape(pair_features.shape, BF16),
        ),
        in_specs=[vmem()] * 7,
        out_specs=(vmem(), vmem(), vmem(), in_hbm()),
        scratch_shapes=[
            pltpu.VMEM((columns, width), BF16),
            pltpu.VMEM((tokens, 3 * SUB, width), BF16),
            pltpu.SemaphoreType.DMA((tokens,)),
            pltpu.SemaphoreType.DMA((3,)),
        ],
        compiler_params=params(32),
        name="turned",
    )(recv, w_bias_t, *parts)

    whole_planes = [
        [(z * plane + i) * cols + c for i in range(plane) for c in range(cols)]
        for z in range(planes)
    ]
    across = [[z * plane + i for z in range(planes)] for i in range(plane)]
    within = [
        [(z + 1) * plane % seqs] + [z * plane + i for i in range(1, plane)] for z in range(planes)
    ]
    first = lax.all_to_all(
        pay.reshape(plane * HEADS, 1, (share + 1) * width), ("seq", "col"), 0, 0, tiled=True, axis_index_groups=whole_planes
    )
    summed = first.reshape(plane, HEADS, (share + 1) * width).sum(axis=0)
    mains = summed[:, : share * width].reshape(1, chunk * width)
    tail = summed[:, share * width :].sum(axis=0, keepdims=True)
    joined = jnp.concatenate([mains, tail], axis=1)
    joined, rim_near = lax.optimization_barrier((joined, rim_near))
    rim_near = lax.ppermute(rim_near, "seq", near)
    second = lax.all_to_all(
        jnp.broadcast_to(joined[None], (planes, 1, joined.shape[1])),
        "seq",
        0,
        0,
        tiled=True,
        axis_index_groups=across,
    ).sum(axis=0)
    partner = jnp.where(odd, seq + 1, seq - 1 + seqs) % plane
    positions = lax.broadcasted_iota(jnp.int32, (plane, 1, 1), 0)
    gathered = jnp.concatenate(
        [
            jnp.broadcast_to(second[:, : chunk * width].reshape(1, chunk, width), (plane, chunk, width)),
            jnp.where(positions == partner, rim_far[None], 0.0),
        ],
        axis=1,
    ).reshape(plane * (chunk + head // 2), width)
    third = lax.all_to_all(gathered, "seq", 0, 0, tiled=True, axis_index_groups=within)
    grad_atoms, gq, gk, gv, go, gb = pl.pallas_call(
        functools.partial(final_kernel, seqs=seqs, chunk=chunk),
        out_shape=(
            shape((head, atoms), BF16),
            shape((head, width), F32),
            shape((head, width), F32),
            shape((head, width), F32),
            shape((head, width), F32),
            shape((1, width), F32),
        ),
        in_specs=[vmem()] * 4,
        out_specs=(vmem(),) * 6,
        compiler_params=params(16),
        name="final",
    )(
        third,
        second[:, chunk * width :],
        own_part,
        rim_near,
    )
    return (grad_atoms.T, grad_pair, gq.T, gk.T, gv.T, go, gb.T)


def solution(mesh):
    placed = (
        P("seq", None),
        P("seq"),
        P("seq"),
        P("seq"),
        P("seq", "col", None),
        P(None, "col"),
        P(None, "col"),
        P(None, "col"),
        P("col", None),
        P(),
        P("seq", None),
        P("seq", None),
    )
    return jax.shard_map(
        per_device,
        mesh=mesh,
        in_specs=placed,
        out_specs=(
            P("seq", "col"),
            P("seq", "col", None),
            P(None, "col"),
            P(None, "col"),
            P(None, "col"),
            P("col", None),
            P(None, "col"),
        ),
        check_vma=False,
    )
```

```python
import functools
import math

import jax
import jax.numpy as jnp
from jax import lax
from jax.experimental import pallas as pl
from jax.experimental.pallas import tpu as pltpu
from jax.sharding import PartitionSpec as P

QUERY_BLOCK = 32
KEY_WINDOW = 128
REACH = 64
SUB = 16
BAND = 64
GROUP = 96
SPAN = GROUP + 2 * REACH
HEADS = 4
SAME_ROWS = 56
SPARE = 16
F32 = jnp.float32
BF16 = jnp.bfloat16

NN = (((1,), (0,)), ((), ()))
NT = (((1,), (1,)), ((), ()))
TN = (((0,), (0,)), ((), ()))


def mm(a, b, dims=NN):
    return lax.dot_general(a, b, dims, preferred_element_type=F32)


def halves(x):
    high = x.astype(BF16)
    return high, (x - high.astype(F32)).astype(BF16)


def mm2(a, b, dims=NN):
    high, low = halves(a)
    return mm(high, b, dims) + mm(low, b, dims)


def own_thirds(seq, col, width):
    thirds = []
    for part in range(3):
        start = (seq + part - 1) * SUB - col * width
        own = jnp.logical_and(start >= 0, start < width)
        thirds.append((own, pl.multiple_of(jnp.clip(start, 0, width - SUB), SUB)))
    return thirds


def band_copies(seq, col, pair_ref, band, sems):
    copies = []
    for part, (own, safe) in enumerate(own_thirds(seq, col, pair_ref.shape[1])):
        copy = pltpu.make_async_copy(
            pair_ref.at[:, pl.ds(safe, SUB), :],
            band.at[:, pl.ds(part * SUB, SUB), :],
            sems.at[part],
        )
        copies.append((own, safe, copy))
    return copies


def gathered_weights(recv_ref, same, paired, head):
    whole = [
        jnp.concatenate(
            [
                recv_ref[same + c].astype(F32)[:SAME_ROWS],
                recv_ref[paired + c].astype(F32)[: 4 * head - SAME_ROWS],
            ],
            axis=0,
        )
        for c in range(HEADS)
    ]
    return [
        jnp.concatenate([w[i * head : (i + 1) * head] for w in whole], axis=0).astype(BF16)
        for i in range(4)
    ]


def spare_lanes(rows):
    lane = lax.broadcasted_iota(jnp.int32, (rows, 2 * BAND), 1) & (BAND - 1)
    return lane, lane >= BAND - SPARE


def tucked(bias):
    _, spare = spare_lanes(SPARE)
    last = bias[3 * SPARE :]
    return jnp.concatenate(
        [
            jnp.where(spare, pltpu.roll(last, (3 - p) * SPARE, 1), bias[p * SPARE : (p + 1) * SPARE])
            for p in range(3)
        ],
        axis=0,
    )


def untucked(rows):
    lane, spare = spare_lanes(SPARE)
    blocks = [rows[p * SPARE : (p + 1) * SPARE] for p in range(3)]
    last = jnp.zeros_like(blocks[0])
    for p, block in enumerate(blocks):
        back = pltpu.roll(block, 2 * BAND - (3 - p) * SPARE, 1)
        last = jnp.where((lane >= p * SPARE) & (lane < (p + 1) * SPARE), back, last)
    return jnp.concatenate([jnp.where(spare, 0.0, block) for block in blocks] + [last], axis=0)


def start_band(copies, band):
    tokens = band.shape[0]
    band[:, 3 * SUB :, :] = jnp.zeros((tokens, BAND - 3 * SUB, band.shape[2]), BF16)
    for part, (own, _, copy) in enumerate(copies):

        @pl.when(own)
        def _(copy=copy):
            copy.start()

        @pl.when(jnp.logical_not(own))
        def _(part=part):
            band[:, part * SUB : (part + 1) * SUB, :] = jnp.zeros((tokens, SUB, band.shape[2]), BF16)


def wait_all(copies):
    for own, _, copy in copies:

        @pl.when(own)
        def _(copy=copy):
            copy.wait()


def pad_rows(x, rows):
    return jnp.concatenate([x, jnp.zeros((rows - x.shape[0],) + x.shape[1:], x.dtype)], axis=0)


def pick(condition, one, other):
    return jnp.where(condition, one.astype(F32), other.astype(F32))


def pack_kernel(
    pair_ref,
    wq_ref,
    wk_ref,
    wv_ref,
    wo_ref,
    atoms_ref,
    wb_ref,
    token_row_ref,
    pack_ref,
    near_ref,
    band,
    whole,
    edge,
    bias,
    band_sems,
    sems,
):
    seq, col = lax.axis_index("seq"), lax.axis_index("col")
    odd = lax.rem(seq, 2) == 1
    copies = band_copies(seq, col, pair_ref, band, band_sems)
    start_band(copies, band)
    tokens = band.shape[0]
    atoms = atoms_ref.shape[0]
    head = wq_ref.shape[0]
    share = REACH // HEADS
    first = jnp.where(odd, atoms - REACH, 0) + col * share
    near_first = jnp.where(odd, 0, atoms - REACH)
    others = [
        pltpu.make_async_copy(
            atoms_ref.at[pl.ds(pl.multiple_of(first, share), share), :], edge, sems.at[0]
        ),
        pltpu.make_async_copy(
            atoms_ref.at[pl.ds(pl.multiple_of(near_first, share), REACH), :],
            near_ref.at[:REACH, :],
            sems.at[5],
        ),
    ] + [
        pltpu.make_async_copy(ref, whole.at[i * head : (i + 1) * head, :], sems.at[i + 1])
        for i, ref in enumerate((wq_ref, wk_ref, wv_ref, wo_ref))
    ]
    for copy in others:
        copy.start()
    row = token_row_ref[...]
    lower, upper = row[:, :REACH], row[:, atoms - REACH :]

    def coded(token):
        code = token + 1
        line = jnp.concatenate([code >> 6, code & 63], axis=1).astype(F32)
        return jnp.broadcast_to(line, (16, line.shape[1]))

    line = coded(jnp.where(odd, upper, lower))
    near_ref[REACH:, :] = coded(jnp.where(odd, lower, upper)).astype(BF16)
    rows = pad_rows(wb_ref[...].astype(F32), 8).astype(BF16)
    for copy in others:
        copy.wait()
    weights = whole[...].astype(F32)
    size = pack_ref.shape[1]
    other = pad_rows(
        jnp.concatenate([weights[SAME_ROWS:], edge[...].astype(F32), line[:8]], axis=0), size
    )
    wait_all(copies)
    for t in range(0, tokens, 2):
        part = mm(rows, band[t], NT) + pltpu.roll(mm(rows, band[t + 1], NT), 4, 0)
        high = part.astype(BF16).astype(F32)
        bias[4 * t : 4 * t + 8, :] = jnp.concatenate([high, part - high], axis=1)
    same = jnp.concatenate([weights[:SAME_ROWS], tucked(bias[...])], axis=0)
    low = jnp.where(odd, same, other).astype(BF16)
    high = jnp.where(odd, other, same).astype(BF16)
    for c in range(HEADS):
        pack_ref[c] = low
        pack_ref[HEADS + c] = high


def attention_kernel(
    window_ref,
    pair_ref,
    recv_ref,
    near_ref,
    own_ref,
    token_row_ref,
    token_col_ref,
    counts_ref,
    atom_cot_ref,
    token_cot_ref,
    pay_ref,
    grad_q_ref,
    grad_k_ref,
    grad_v_ref,
    upstream_ref,
    token_grad_ref,
    band,
    main,
    band_sems,
    *,
    seqs,
    plane,
):
    seq, col = lax.axis_index("seq"), lax.axis_index("col")
    copies = band_copies(seq, col, pair_ref, band, band_sems)
    start_band(copies, band)
    tokens = band.shape[0]
    odd = lax.rem(seq, 2) == 1
    atoms = own_ref.shape[0]
    width = own_ref.shape[1]
    head = width // HEADS
    inv_root = 1.0 / math.sqrt(head)
    slot_base = seq * atoms
    token_base = seq * tokens
    same = jnp.where(odd, 0, HEADS)
    paired = HEADS - same
    share = REACH // HEADS

    wq_t, wk_t, wv_t, wo = gathered_weights(recv_ref, same, paired, head)
    bias = recv_ref[same].astype(F32)[SAME_ROWS:]
    for c in range(1, HEADS):
        bias = bias + recv_ref[same + c].astype(F32)[SAME_ROWS:]
    bias = untucked(bias).astype(BF16)

    own = own_ref[...]
    at = 4 * head - SAME_ROWS
    far_chunks = [recv_ref[paired + c].astype(F32)[at : at + share + 8] for c in range(HEADS)]
    far_rows = jnp.concatenate([x[:share] for x in far_chunks], axis=0)
    near_rows = near_ref[:REACH, :]
    has_below, has_above = seq > 0, seq < seqs - 1
    below = jnp.where(has_below, pick(odd, near_rows, far_rows), 0.0).astype(BF16)
    above = jnp.where(has_above, pick(odd, far_rows, near_rows), 0.0).astype(BF16)
    ext = jnp.concatenate([below, own, above], axis=0)
    queries = mm(own, wq_t, NT).astype(BF16)
    keys = mm(ext, wk_t, NT).astype(BF16)
    values = mm(ext, wv_t, NT).astype(BF16)

    token_col = token_col_ref[...]
    live_col = token_col >= 0
    local_col = token_col - token_base
    token_lanes = lax.broadcasted_iota(jnp.int32, (atoms, tokens), 1)
    onehot = (local_col == token_lanes).astype(F32)
    pooled = mm(onehot.astype(BF16), token_cot_ref[...])
    count = jnp.sum(onehot * counts_ref[...].astype(F32), axis=1, keepdims=True)
    safe_count = jnp.where(live_col, count, 1.0)
    upstream = jnp.where(live_col, atom_cot_ref[...].astype(F32) + pooled / safe_count, 0.0)
    upstream = upstream.astype(BF16)
    grad_attended = mm(upstream, wo, NT).astype(BF16)

    def decoded(row):
        return (row[:, :REACH] * 64.0 + row[:, REACH:]).astype(jnp.int32) - 1

    far_token = decoded(far_chunks[0][share : share + 1])
    near_token = decoded(near_ref[REACH:, :].astype(F32)[:1])
    below_token = jnp.where(has_below, jnp.where(odd, near_token, far_token), -1)
    above_token = jnp.where(has_above, jnp.where(odd, far_token, near_token), -1)
    own_row = token_row_ref[...]
    key_rows = (
        jnp.concatenate([below_token, own_row[:, : SPAN - REACH]], axis=1),
        jnp.concatenate([own_row[:, atoms - (SPAN - REACH) :], above_token], axis=1),
    )
    head_lanes = lax.broadcasted_iota(jnp.int32, (GROUP, width), 1) // head
    head_masks = [head_lanes == h for h in range(HEADS)]

    def stacked(x):
        return jnp.concatenate(
            [jnp.where(mask, x, jnp.zeros_like(x)) for mask in head_masks], axis=0
        )

    def folded(x):
        total = jnp.where(head_masks[0], x[:GROUP], 0.0)
        for h in range(1, HEADS):
            total = total + jnp.where(head_masks[h], x[h * GROUP : (h + 1) * GROUP], 0.0)
        return total

    attended, grad_queries, key_terms, value_terms = [], [], [], []
    token_grad = jnp.zeros((tokens * HEADS, width), F32)
    for g in range(atoms // GROUP):
        rows = slice(g * GROUP, (g + 1) * GROUP)
        span = slice(g * GROUP, g * GROUP + SPAN)
        k_g, v_g = keys[span], values[span]
        q_m = stacked(queries[rows].astype(F32)).astype(BF16)
        a_m = stacked(grad_attended[rows].astype(F32)).astype(BF16)
        key_token = key_rows[g]
        key_live = key_token >= 0
        key_band = jnp.where(key_live, key_token - (token_base - tokens), -1000)
        lane_band = lax.broadcasted_iota(jnp.int32, (width, SPAN), 0)
        key_onehot = ((lane_band & (BAND - 1)) == key_band).astype(F32).astype(BF16)
        local = local_col[rows]
        slot = lax.broadcasted_iota(jnp.int32, (GROUP, tokens * HEADS), 1)
        query_onehot = jnp.concatenate(
            [(slot == local * HEADS + h).astype(F32) for h in range(HEADS)], axis=0
        )
        query_onehot = query_onehot.astype(BF16)
        picked = mm(query_onehot, bias).astype(BF16)
        scores = mm(q_m, k_g, NT) * inv_root + mm(picked, key_onehot)
        scores = scores.reshape(HEADS, GROUP, SPAN)
        block = lax.broadcasted_iota(jnp.int32, (GROUP, 1), 0) // QUERY_BLOCK
        base = slot_base - REACH + g * GROUP
        first = g * (GROUP // QUERY_BLOCK)
        start = jnp.where(
            block == 0,
            window_ref[first] - base,
            jnp.where(block == 1, window_ref[first + 1] - base, window_ref[first + 2] - base),
        )
        position = lax.broadcasted_iota(jnp.int32, (GROUP, SPAN), 1)
        inside = (position >= start) & (position < start + KEY_WINDOW)
        dead_query = local < 0
        allowed = inside & (key_live | dead_query)
        masked = jnp.where(allowed[None], scores, -1e30)
        row_max = jnp.max(masked, axis=-1, keepdims=True)
        raw = jnp.where(allowed[None], jnp.exp(masked - row_max), 0.0)
        weights = raw / jnp.sum(raw, axis=-1, keepdims=True)
        grad_weights = mm(a_m, v_g, NT).reshape(HEADS, GROUP, SPAN)
        inner = jnp.sum(weights * grad_weights, axis=-1, keepdims=True)
        grad_scores = (weights * (grad_weights - inner)).reshape(HEADS * GROUP, SPAN)
        w_low = weights.reshape(HEADS * GROUP, SPAN).astype(BF16)
        s_high, s_low = halves(grad_scores)
        attended.append(folded(mm(w_low, v_g)))
        grad_queries.append(folded(mm(s_high, k_g)) * inv_root)
        key_terms.append(mm(s_high, q_m, TN) * inv_root)
        value_terms.append(mm(w_low, a_m, TN))
        by_token = mm(query_onehot, s_high, TN) + mm(query_onehot, s_low, TN)
        token_grad = token_grad + mm2(by_token, key_onehot, NT)

    attended = jnp.concatenate(attended, axis=0).astype(BF16)
    grad_q = jnp.concatenate(grad_queries, axis=0)

    def overlapped(terms):
        lap = SPAN - GROUP
        return jnp.concatenate(
            [terms[0][:GROUP], terms[0][GROUP:] + terms[1][:lap], terms[1][lap:]], axis=0
        )

    grad_k = overlapped(key_terms)
    grad_v = overlapped(value_terms)

    grad_q_ref[...] = grad_q
    grad_k_ref[...] = grad_k
    grad_v_ref[...] = grad_v
    upstream_ref[...] = upstream
    token_grad_ref[...] = token_grad

    chunk = width // plane
    products = (
        mm2(grad_q, own, TN),
        mm2(grad_k, ext, TN),
        mm2(grad_v, ext, TN),
        mm(attended, upstream, TN),
    )
    per_product = head // chunk
    for i, product in enumerate(products):
        for c in range(HEADS):
            for j in range(per_product):
                to = ((i * per_product + j) * HEADS + c) * chunk
                at = c * head + j * chunk
                main[to : to + chunk, :] = product[at : at + chunk]
    wait_all(copies)
    w_bias_grad = jnp.zeros((8, width), F32)
    left = lax.broadcasted_iota(jnp.int32, (8, width), 1) < BAND
    for t in range(0, tokens, 2):
        two = token_grad[HEADS * t : HEADS * t + 8]
        two = jnp.where(left, two, pltpu.roll(two, 4, 0))
        stack = jnp.concatenate([band[t], band[t + 1]], axis=0)
        w_bias_grad = w_bias_grad + mm2(two, stack)
    upper = lax.broadcasted_iota(jnp.int32, (8, width), 0) < HEADS
    spread = jnp.where(upper, w_bias_grad, pltpu.roll(w_bias_grad, 4, 0))
    share = chunk // HEADS
    for j in range(share):
        pay_ref[pl.ds(j, plane * HEADS, stride=share + 1), :] = main[
            pl.ds(col * share + j, plane * HEADS, stride=chunk), :
        ]
    pay_ref[pl.ds(share, plane * HEADS, stride=share + 1), :] = jnp.concatenate(
        [spread] * (plane * HEADS // 8), axis=0
    )


def turned_kernel(
    recv_ref,
    wb_ref,
    grad_q_ref,
    grad_k_ref,
    grad_v_ref,
    upstream_ref,
    token_grad_ref,
    rim_far_ref,
    rim_near_ref,
    own_out_ref,
    grad_pair_ref,
    zeros,
    grad_band,
    zero_sems,
    out_sems,
):
    seq, col = lax.axis_index("seq"), lax.axis_index("col")
    odd = lax.rem(seq, 2) == 1
    tokens = grad_band.shape[0]
    zeros[...] = jnp.zeros(zeros.shape, BF16)
    fills = [
        pltpu.make_async_copy(zeros, grad_pair_ref.at[t], zero_sems.at[t]) for t in range(tokens)
    ]
    for fill in fills:
        fill.start()
    atoms, width = grad_q_ref.shape
    head = width // HEADS

    rows = pad_rows(wb_ref[...].astype(F32), 8)
    turned = pad_rows(token_grad_ref[...], width).T[: 3 * SUB]
    for t in range(tokens):
        at = HEADS * t
        total = turned[:, at : at + 1] * rows[0:1]
        for h in range(1, HEADS):
            total = total + turned[:, at + h : at + h + 1] * rows[h : h + 1]
        grad_band[t] = total.astype(BF16)

    same = jnp.where(odd, 0, HEADS)
    wq_t, wk_t, wv_t, _ = gathered_weights(recv_ref, same, HEADS - same, head)
    key_part = mm2(grad_k_ref[...], wk_t) + mm2(grad_v_ref[...], wv_t)
    query_part = mm2(grad_q_ref[...], wq_t) + upstream_ref[...].astype(F32)
    shift = lax.rem(width - col * head, width)
    whole = jnp.concatenate(
        [key_part[REACH : REACH + atoms] + query_part, key_part[:REACH]]
        + [key_part[REACH + atoms :], jnp.zeros((REACH, width), F32)],
        axis=0,
    )
    whole = pltpu.roll(whole, shift, 1).T[:head]
    own_out_ref[...] = whole[:, :atoms]
    rim_down = whole[:, atoms : atoms + REACH]
    rim_up = whole[:, atoms + REACH : atoms + 2 * REACH]
    rim_far = jnp.where(odd, rim_up, rim_down)
    rim_far_ref[...] = jnp.concatenate([rim_far[: head // 2], rim_far[head // 2 :]], axis=1)
    rim_near_ref[...] = jnp.where(odd, rim_down, rim_up).astype(BF16)
    for fill in fills:
        fill.wait()
    outs = []
    for part, (own_part, safe) in enumerate(own_thirds(seq, col, grad_pair_ref.shape[1])):
        copy = pltpu.make_async_copy(
            grad_band.at[:, pl.ds(part * SUB, SUB), :],
            grad_pair_ref.at[:, pl.ds(safe, SUB), :],
            out_sems.at[part],
        )
        outs.append((own_part, safe, copy))

        @pl.when(own_part)
        def _(copy=copy):
            copy.start()

    wait_all(outs)


def final_kernel(
    gathered_ref,
    bias_ref,
    own_ref,
    near_ref,
    atoms_ref,
    gq_ref,
    gk_ref,
    gv_ref,
    go_ref,
    gb_ref,
    *,
    seqs,
    chunk,
):
    head, atoms = atoms_ref.shape
    seq = lax.axis_index("seq")
    odd = lax.rem(seq, 2) == 1
    rim_rows = head // 2
    rows = 2 * chunk + rim_rows
    plane = gathered_ref.shape[0] // rows
    partner = lax.rem(jnp.where(odd, seq + 1, seq - 1 + seqs), plane)
    far = gathered_ref[pl.ds(pl.multiple_of(partner * rows + 2 * chunk, 16), rim_rows), :].astype(F32)
    far = jnp.concatenate([far[:, :REACH], far[:, REACH:]], axis=0)
    far = jnp.where(jnp.where(odd, seq + 1, seq) % seqs == 0, 0.0, far)
    near = near_ref[...].astype(F32)
    below, above = jnp.where(odd, near, far), jnp.where(odd, far, near)
    middle = jnp.zeros((head, atoms - 2 * REACH), F32)
    atoms_ref[...] = (own_ref[...] + jnp.concatenate([below, middle, above], axis=1)).astype(BF16)
    terms = [gathered_ref[p * rows : p * rows + 2 * chunk, :].astype(F32) for p in range(plane)]
    main = jnp.concatenate([x[:chunk] + x[chunk:] for x in terms], axis=0)
    for i, ref in enumerate((gq_ref, gk_ref, gv_ref, go_ref)):
        ref[...] = main[i * head : (i + 1) * head]
    gb_ref[...] = bias_ref[...]


def vmem():
    return pl.BlockSpec(memory_space=pltpu.VMEM)


def smem():
    return pl.BlockSpec(memory_space=pltpu.SMEM)


def in_hbm():
    return pl.BlockSpec(memory_space=pltpu.MemorySpace.HBM)


def shape(dims, dtype):
    return jax.ShapeDtypeStruct(dims, dtype)


def params(mebibytes):
    return pltpu.CompilerParams(vmem_limit_bytes=mebibytes * 1024 * 1024)


def per_device(
    atom_inputs,
    atom_token,
    counts,
    window_start,
    pair_features,
    w_query,
    w_key,
    w_value,
    w_out,
    w_bias,
    atom_cotangent,
    token_cotangent,
):
    atoms, width = atom_inputs.shape
    tokens, columns, _ = pair_features.shape
    head = w_query.shape[1]
    seqs = lax.axis_size("seq")
    plane = 16 if seqs % 16 == 0 else 4
    planes = seqs // plane
    cols = lax.axis_size("col")
    seq = lax.axis_index("seq")
    odd = seq % 2 == 1
    token_row = atom_token[None, :]

    near = [(i, i ^ 1) for i in range(seqs)]
    far_groups = [
        [n * cols + c for n in (i, (i + 1) % seqs) for c in range(cols)] for i in range(1, seqs, 2)
    ]
    w_bias_t = w_bias.T
    pack, near_edge = pl.pallas_call(
        pack_kernel,
        out_shape=(
            shape((2 * HEADS, SAME_ROWS + 3 * SPARE, width), BF16),
            shape((REACH + 16, width), BF16),
        ),
        in_specs=[in_hbm()] * 6 + [vmem()] * 2,
        out_specs=(vmem(), vmem()),
        scratch_shapes=[
            pltpu.VMEM((tokens, BAND, width), BF16),
            pltpu.VMEM((width, width), BF16),
            pltpu.VMEM((REACH // HEADS, width), BF16),
            pltpu.VMEM((tokens * HEADS, width), F32),
            pltpu.SemaphoreType.DMA((3,)),
            pltpu.SemaphoreType.DMA((6,)),
        ],
        compiler_params=params(60),
        name="pack",
    )(
        pair_features,
        w_query.T,
        w_key.T,
        w_value.T,
        w_out,
        atom_inputs,
        w_bias_t,
        token_row,
    )
    near_edge = lax.ppermute(near_edge, "seq", near)
    recv = lax.all_to_all(
        pack, ("seq", "col"), 0, 0, tiled=True, axis_index_groups=far_groups
    )

    chunk = width // plane
    share = chunk // HEADS
    pay, *parts = pl.pallas_call(
        functools.partial(attention_kernel, seqs=seqs, plane=plane),
        out_shape=(
            shape((plane * HEADS * (share + 1), width), F32),
            shape((atoms, width), F32),
            shape((atoms + 2 * REACH, width), F32),
            shape((atoms + 2 * REACH, width), F32),
            shape((atoms, width), BF16),
            shape((tokens * HEADS, width), F32),
        ),
        in_specs=[smem(), in_hbm()] + [vmem()] * 8,
        out_specs=(vmem(),) * 6,
        scratch_shapes=[
            pltpu.VMEM((tokens, BAND, width), BF16),
            pltpu.VMEM((HEADS * width, width), F32),
            pltpu.SemaphoreType.DMA((3,)),
        ],
        compiler_params=params(32),
        name="attention",
    )(
        window_start,
        pair_features,
        recv,
        near_edge,
        atom_inputs,
        token_row,
        atom_token[:, None],
        counts[None, :],
        atom_cotangent,
        token_cotangent,
    )
    rim_far, rim_near, own_part, grad_pair = pl.pallas_call(
        turned_kernel,
        out_shape=(
            shape((head // 2, width), F32),
            shape((head, REACH), BF16),
            shape((head, atoms), F32),
            shape(pair_features.shape, BF16),
        ),
        in_specs=[vmem()] * 7,
        out_specs=(vmem(), vmem(), vmem(), in_hbm()),
        scratch_shapes=[
            pltpu.VMEM((columns, width), BF16),
            pltpu.VMEM((tokens, 3 * SUB, width), BF16),
            pltpu.SemaphoreType.DMA((tokens,)),
            pltpu.SemaphoreType.DMA((3,)),
        ],
        compiler_params=params(32),
        name="turned",
    )(recv, w_bias_t, *parts)

    whole_planes = [
        [(z * plane + i) * cols + c for i in range(plane) for c in range(cols)]
        for z in range(planes)
    ]
    across = [[z * plane + i for z in range(planes)] for i in range(plane)]
    within = [
        [(z + 1) * plane % seqs] + [z * plane + i for i in range(1, plane)] for z in range(planes)
    ]
    first = lax.all_to_all(
        pay.reshape(plane * HEADS, 1, (share + 1) * width), ("seq", "col"), 0, 0, tiled=True, axis_index_groups=whole_planes
    )
    summed = first.reshape(plane, HEADS, (share + 1) * width).sum(axis=0)
    mains = summed[:, : share * width].reshape(1, chunk * width)
    tail = summed[:, share * width :].sum(axis=0, keepdims=True)
    joined = jnp.concatenate([mains, tail], axis=1)
    joined, rim_near = lax.optimization_barrier((joined, rim_near))
    rim_near = lax.ppermute(rim_near, "seq", near)
    second = lax.all_to_all(
        jnp.broadcast_to(joined[None], (planes, 1, joined.shape[1])),
        "seq",
        0,
        0,
        tiled=True,
        axis_index_groups=across,
    ).sum(axis=0)
    partner = jnp.where(odd, seq + 1, seq - 1 + seqs) % plane
    positions = lax.broadcasted_iota(jnp.int32, (plane, 1, 1), 0)
    sums = second[:, : chunk * width].reshape(1, chunk, width)
    leading = lax.reduce_precision(sums, 8, 7)
    sums = jnp.concatenate([leading, sums - leading], axis=1)
    gathered = jnp.concatenate(
        [
            jnp.broadcast_to(sums, (plane, 2 * chunk, width)),
            jnp.where(positions == partner, rim_far[None], 0.0),
        ],
        axis=1,
    )
    gathered = gathered.astype(BF16).reshape(plane * (2 * chunk + head // 2), width)
    third = lax.all_to_all(gathered, "seq", 0, 0, tiled=True, axis_index_groups=within)
    grad_atoms, gq, gk, gv, go, gb = pl.pallas_call(
        functools.partial(final_kernel, seqs=seqs, chunk=chunk),
        out_shape=(
            shape((head, atoms), BF16),
            shape((head, width), F32),
            shape((head, width), F32),
            shape((head, width), F32),
            shape((head, width), F32),
            shape((1, width), F32),
        ),
        in_specs=[vmem()] * 4,
        out_specs=(vmem(),) * 6,
        compiler_params=params(16),
        name="final",
    )(
        third,
        second[:, chunk * width :],
        own_part,
        rim_near,
    )
    return (grad_atoms.T, grad_pair, gq.T, gk.T, gv.T, go, gb.T)


def solution(mesh):
    placed = (
        P("seq", None),
        P("seq"),
        P("seq"),
        P("seq"),
        P("seq", "col", None),
        P(None, "col"),
        P(None, "col"),
        P(None, "col"),
        P("col", None),
        P(),
        P("seq", None),
        P("seq", None),
    )
    return jax.shard_map(
        per_device,
        mesh=mesh,
        in_specs=placed,
        out_specs=(
            P("seq", "col"),
            P("seq", "col", None),
            P(None, "col"),
            P(None, "col"),
            P(None, "col"),
            P("col", None),
            P(None, "col"),
        ),
        check_vma=False,
    )
```

```python
import functools
import math

import jax
import jax.numpy as jnp
from jax import lax
from jax.experimental import pallas as pl
from jax.experimental.pallas import tpu as pltpu
from jax.sharding import PartitionSpec as P

QUERY_BLOCK = 32
KEY_WINDOW = 128
REACH = 64
SUB = 16
BAND = 64
GROUP = 96
SPAN = GROUP + 2 * REACH
HEADS = 4
SAME_ROWS = 56
SPARE = 16
F32 = jnp.float32
BF16 = jnp.bfloat16

NN = (((1,), (0,)), ((), ()))
NT = (((1,), (1,)), ((), ()))
TN = (((0,), (0,)), ((), ()))


def mm(a, b, dims=NN):
    return lax.dot_general(a, b, dims, preferred_element_type=F32)


def halves(x):
    high = x.astype(BF16)
    return high, (x - high.astype(F32)).astype(BF16)


def mm2(a, b, dims=NN):
    high, low = halves(a)
    return mm(high, b, dims) + mm(low, b, dims)


def own_thirds(seq, col, width):
    thirds = []
    for part in range(3):
        start = (seq + part - 1) * SUB - col * width
        own = jnp.logical_and(start >= 0, start < width)
        thirds.append((own, pl.multiple_of(jnp.clip(start, 0, width - SUB), SUB)))
    return thirds


def band_copies(seq, col, pair_ref, band, sems):
    copies = []
    for part, (own, safe) in enumerate(own_thirds(seq, col, pair_ref.shape[1])):
        copy = pltpu.make_async_copy(
            pair_ref.at[:, pl.ds(safe, SUB), :],
            band.at[:, pl.ds(part * SUB, SUB), :],
            sems.at[part],
        )
        copies.append((own, safe, copy))
    return copies


def gathered_weights(recv_ref, same, paired, head):
    whole = [
        jnp.concatenate(
            [
                recv_ref[same + c].astype(F32)[:SAME_ROWS],
                recv_ref[paired + c].astype(F32)[: 4 * head - SAME_ROWS],
            ],
            axis=0,
        )
        for c in range(HEADS)
    ]
    return [
        jnp.concatenate([w[i * head : (i + 1) * head] for w in whole], axis=0).astype(BF16)
        for i in range(4)
    ]


def spare_lanes(rows):
    lane = lax.broadcasted_iota(jnp.int32, (rows, 2 * BAND), 1) & (BAND - 1)
    return lane, lane >= BAND - SPARE


def tucked(bias):
    _, spare = spare_lanes(SPARE)
    last = bias[3 * SPARE :]
    return jnp.concatenate(
        [
            jnp.where(spare, pltpu.roll(last, (3 - p) * SPARE, 1), bias[p * SPARE : (p + 1) * SPARE])
            for p in range(3)
        ],
        axis=0,
    )


def untucked(rows):
    lane, spare = spare_lanes(SPARE)
    blocks = [rows[p * SPARE : (p + 1) * SPARE] for p in range(3)]
    last = jnp.zeros_like(blocks[0])
    for p, block in enumerate(blocks):
        back = pltpu.roll(block, 2 * BAND - (3 - p) * SPARE, 1)
        last = jnp.where((lane >= p * SPARE) & (lane < (p + 1) * SPARE), back, last)
    return jnp.concatenate([jnp.where(spare, 0.0, block) for block in blocks] + [last], axis=0)


def start_band(copies, band):
    tokens = band.shape[0]
    band[:, 3 * SUB :, :] = jnp.zeros((tokens, BAND - 3 * SUB, band.shape[2]), BF16)
    for part, (own, _, copy) in enumerate(copies):

        @pl.when(own)
        def _(copy=copy):
            copy.start()

        @pl.when(jnp.logical_not(own))
        def _(part=part):
            band[:, part * SUB : (part + 1) * SUB, :] = jnp.zeros((tokens, SUB, band.shape[2]), BF16)


def wait_all(copies):
    for own, _, copy in copies:

        @pl.when(own)
        def _(copy=copy):
            copy.wait()


def pad_rows(x, rows):
    return jnp.concatenate([x, jnp.zeros((rows - x.shape[0],) + x.shape[1:], x.dtype)], axis=0)


def pick(condition, one, other):
    return jnp.where(condition, one.astype(F32), other.astype(F32))


def pack_kernel(
    pair_ref,
    wq_ref,
    wk_ref,
    wv_ref,
    wo_ref,
    atoms_ref,
    wb_ref,
    token_row_ref,
    pack_ref,
    near_ref,
    band,
    whole,
    edge,
    bias,
    weight_rows,
    token_line,
    near_edge,
    low_chunk,
    high_chunk,
    band_sems,
    sems,
    out_sems,
):
    seq, col = lax.axis_index("seq"), lax.axis_index("col")
    odd = lax.rem(seq, 2) == 1
    copies = band_copies(seq, col, pair_ref, band, band_sems)
    start_band(copies, band)
    tokens = band.shape[0]
    atoms = atoms_ref.shape[0]
    head = wq_ref.shape[0]
    share = REACH // HEADS
    first = jnp.where(odd, atoms - REACH, 0) + col * share
    near_first = jnp.where(odd, 0, atoms - REACH)
    others = [
        pltpu.make_async_copy(
            atoms_ref.at[pl.ds(pl.multiple_of(first, share), share), :], edge, sems.at[0]
        ),
        pltpu.make_async_copy(
            atoms_ref.at[pl.ds(pl.multiple_of(near_first, share), REACH), :],
            near_edge.at[:REACH, :],
            sems.at[5],
        ),
        pltpu.make_async_copy(wb_ref, weight_rows, sems.at[6]),
        pltpu.make_async_copy(token_row_ref, token_line, sems.at[7]),
    ] + [
        pltpu.make_async_copy(ref, whole.at[i * head : (i + 1) * head, :], sems.at[i + 1])
        for i, ref in enumerate((wq_ref, wk_ref, wv_ref, wo_ref))
    ]
    for copy in others:
        copy.start()
    for copy in others:
        copy.wait()
    row = token_line[...]
    lower, upper = row[:, :REACH], row[:, atoms - REACH :]

    def coded(token):
        code = token + 1
        line = jnp.concatenate([code >> 6, code & 63], axis=1).astype(F32)
        return jnp.broadcast_to(line, (16, line.shape[1]))

    line = coded(jnp.where(odd, upper, lower))
    near_edge[REACH:, :] = coded(jnp.where(odd, lower, upper)).astype(BF16)
    outs = [pltpu.make_async_copy(near_edge, near_ref, out_sems.at[2 * HEADS])]
    outs[0].start()
    rows = pad_rows(weight_rows[...].astype(F32), 8).astype(BF16)
    weights = whole[...].astype(F32)
    size = pack_ref.shape[1]
    other = pad_rows(
        jnp.concatenate([weights[SAME_ROWS:], edge[...].astype(F32), line[:8]], axis=0), size
    )
    wait_all(copies)
    for t in range(0, tokens, 2):
        part = mm(rows, band[t], NT) + pltpu.roll(mm(rows, band[t + 1], NT), 4, 0)
        high = part.astype(BF16).astype(F32)
        bias[4 * t : 4 * t + 8, :] = jnp.concatenate([high, part - high], axis=1)
    same = jnp.concatenate([weights[:SAME_ROWS], tucked(bias[...])], axis=0)
    low_chunk[...] = jnp.where(odd, same, other).astype(BF16)
    high_chunk[...] = jnp.where(odd, other, same).astype(BF16)
    for c in range(HEADS):
        for chunk, to in ((low_chunk, c), (high_chunk, HEADS + c)):
            copy = pltpu.make_async_copy(chunk, pack_ref.at[to], out_sems.at[to])
            copy.start()
            outs.append(copy)
    for copy in outs:
        copy.wait()


def attention_kernel(
    window_ref,
    pair_ref,
    recv_ref,
    near_ref,
    own_ref,
    token_row_ref,
    token_col_ref,
    counts_ref,
    atom_cot_ref,
    token_cot_ref,
    pay_ref,
    grad_q_ref,
    grad_k_ref,
    grad_v_ref,
    upstream_ref,
    token_grad_ref,
    band,
    main,
    band_sems,
    *,
    seqs,
    plane,
):
    seq, col = lax.axis_index("seq"), lax.axis_index("col")
    copies = band_copies(seq, col, pair_ref, band, band_sems)
    start_band(copies, band)
    tokens = band.shape[0]
    odd = lax.rem(seq, 2) == 1
    atoms = own_ref.shape[0]
    width = own_ref.shape[1]
    head = width // HEADS
    inv_root = 1.0 / math.sqrt(head)
    slot_base = seq * atoms
    token_base = seq * tokens
    same = jnp.where(odd, 0, HEADS)
    paired = HEADS - same
    share = REACH // HEADS

    wq_t, wk_t, wv_t, wo = gathered_weights(recv_ref, same, paired, head)
    bias = recv_ref[same].astype(F32)[SAME_ROWS:]
    for c in range(1, HEADS):
        bias = bias + recv_ref[same + c].astype(F32)[SAME_ROWS:]
    bias = untucked(bias).astype(BF16)

    own = own_ref[...]
    at = 4 * head - SAME_ROWS
    far_chunks = [recv_ref[paired + c].astype(F32)[at : at + share + 8] for c in range(HEADS)]
    far_rows = jnp.concatenate([x[:share] for x in far_chunks], axis=0)
    near_rows = near_ref[:REACH, :]
    has_below, has_above = seq > 0, seq < seqs - 1
    below = jnp.where(has_below, pick(odd, near_rows, far_rows), 0.0).astype(BF16)
    above = jnp.where(has_above, pick(odd, far_rows, near_rows), 0.0).astype(BF16)
    ext = jnp.concatenate([below, own, above], axis=0)
    queries = mm(own, wq_t, NT).astype(BF16)
    keys = mm(ext, wk_t, NT).astype(BF16)
    values = mm(ext, wv_t, NT).astype(BF16)

    token_col = token_col_ref[...]
    live_col = token_col >= 0
    local_col = token_col - token_base
    token_lanes = lax.broadcasted_iota(jnp.int32, (atoms, tokens), 1)
    onehot = (local_col == token_lanes).astype(F32)
    pooled = mm(onehot.astype(BF16), token_cot_ref[...])
    count = jnp.sum(onehot * counts_ref[...].astype(F32), axis=1, keepdims=True)
    safe_count = jnp.where(live_col, count, 1.0)
    upstream = jnp.where(live_col, atom_cot_ref[...].astype(F32) + pooled / safe_count, 0.0)
    upstream = upstream.astype(BF16)
    grad_attended = mm(upstream, wo, NT).astype(BF16)

    def decoded(row):
        return (row[:, :REACH] * 64.0 + row[:, REACH:]).astype(jnp.int32) - 1

    far_token = decoded(far_chunks[0][share : share + 1])
    near_token = decoded(near_ref[REACH:, :].astype(F32)[:1])
    below_token = jnp.where(has_below, jnp.where(odd, near_token, far_token), -1)
    above_token = jnp.where(has_above, jnp.where(odd, far_token, near_token), -1)
    own_row = token_row_ref[...]
    key_rows = (
        jnp.concatenate([below_token, own_row[:, : SPAN - REACH]], axis=1),
        jnp.concatenate([own_row[:, atoms - (SPAN - REACH) :], above_token], axis=1),
    )
    head_lanes = lax.broadcasted_iota(jnp.int32, (GROUP, width), 1) // head
    head_masks = [head_lanes == h for h in range(HEADS)]

    def stacked(x):
        return jnp.concatenate(
            [jnp.where(mask, x, jnp.zeros_like(x)) for mask in head_masks], axis=0
        )

    def folded(x):
        total = jnp.where(head_masks[0], x[:GROUP], 0.0)
        for h in range(1, HEADS):
            total = total + jnp.where(head_masks[h], x[h * GROUP : (h + 1) * GROUP], 0.0)
        return total

    attended, grad_queries, key_terms, value_terms = [], [], [], []
    token_grad = jnp.zeros((tokens * HEADS, width), F32)
    for g in range(atoms // GROUP):
        rows = slice(g * GROUP, (g + 1) * GROUP)
        span = slice(g * GROUP, g * GROUP + SPAN)
        k_g, v_g = keys[span], values[span]
        q_m = stacked(queries[rows].astype(F32)).astype(BF16)
        a_m = stacked(grad_attended[rows].astype(F32)).astype(BF16)
        key_token = key_rows[g]
        key_live = key_token >= 0
        key_band = jnp.where(key_live, key_token - (token_base - tokens), -1000)
        lane_band = lax.broadcasted_iota(jnp.int32, (width, SPAN), 0)
        key_onehot = ((lane_band & (BAND - 1)) == key_band).astype(F32).astype(BF16)
        local = local_col[rows]
        slot = lax.broadcasted_iota(jnp.int32, (GROUP, tokens * HEADS), 1)
        query_onehot = jnp.concatenate(
            [(slot == local * HEADS + h).astype(F32) for h in range(HEADS)], axis=0
        )
        query_onehot = query_onehot.astype(BF16)
        picked = mm(query_onehot, bias).astype(BF16)
        scores = mm(q_m, k_g, NT) * inv_root + mm(picked, key_onehot)
        scores = scores.reshape(HEADS, GROUP, SPAN)
        block = lax.broadcasted_iota(jnp.int32, (GROUP, 1), 0) // QUERY_BLOCK
        base = slot_base - REACH + g * GROUP
        first = g * (GROUP // QUERY_BLOCK)
        start = jnp.where(
            block == 0,
            window_ref[first] - base,
            jnp.where(block == 1, window_ref[first + 1] - base, window_ref[first + 2] - base),
        )
        position = lax.broadcasted_iota(jnp.int32, (GROUP, SPAN), 1)
        inside = (position >= start) & (position < start + KEY_WINDOW)
        dead_query = local < 0
        allowed = inside & (key_live | dead_query)
        masked = jnp.where(allowed[None], scores, -1e30)
        row_max = jnp.max(masked, axis=-1, keepdims=True)
        raw = jnp.where(allowed[None], jnp.exp(masked - row_max), 0.0)
        weights = raw / jnp.sum(raw, axis=-1, keepdims=True)
        grad_weights = mm(a_m, v_g, NT).reshape(HEADS, GROUP, SPAN)
        inner = jnp.sum(weights * grad_weights, axis=-1, keepdims=True)
        grad_scores = (weights * (grad_weights - inner)).reshape(HEADS * GROUP, SPAN)
        w_low = weights.reshape(HEADS * GROUP, SPAN).astype(BF16)
        s_high, s_low = halves(grad_scores)
        attended.append(folded(mm(w_low, v_g)))
        grad_queries.append(folded(mm(s_high, k_g)) * inv_root)
        key_terms.append(mm(s_high, q_m, TN) * inv_root)
        value_terms.append(mm(w_low, a_m, TN))
        by_token = mm(query_onehot, s_high, TN) + mm(query_onehot, s_low, TN)
        token_grad = token_grad + mm2(by_token, key_onehot, NT)

    attended = jnp.concatenate(attended, axis=0).astype(BF16)
    grad_q = jnp.concatenate(grad_queries, axis=0)

    def overlapped(terms):
        lap = SPAN - GROUP
        return jnp.concatenate(
            [terms[0][:GROUP], terms[0][GROUP:] + terms[1][:lap], terms[1][lap:]], axis=0
        )

    grad_k = overlapped(key_terms)
    grad_v = overlapped(value_terms)

    grad_q_ref[...] = grad_q
    grad_k_ref[...] = grad_k
    grad_v_ref[...] = grad_v
    upstream_ref[...] = upstream
    token_grad_ref[...] = token_grad

    chunk = width // plane
    products = (
        mm2(grad_q, own, TN),
        mm2(grad_k, ext, TN),
        mm2(grad_v, ext, TN),
        mm(attended, upstream, TN),
    )
    per_product = head // chunk
    for i, product in enumerate(products):
        for c in range(HEADS):
            for j in range(per_product):
                to = ((i * per_product + j) * HEADS + c) * chunk
                at = c * head + j * chunk
                main[to : to + chunk, :] = product[at : at + chunk]
    wait_all(copies)
    w_bias_grad = jnp.zeros((8, width), F32)
    left = lax.broadcasted_iota(jnp.int32, (8, width), 1) < BAND
    for t in range(0, tokens, 2):
        two = token_grad[HEADS * t : HEADS * t + 8]
        two = jnp.where(left, two, pltpu.roll(two, 4, 0))
        stack = jnp.concatenate([band[t], band[t + 1]], axis=0)
        both = mm(jnp.concatenate(halves(two), axis=0), stack)
        w_bias_grad = w_bias_grad + both[:8] + both[8:]
    upper = lax.broadcasted_iota(jnp.int32, (8, width), 0) < HEADS
    spread = jnp.where(upper, w_bias_grad, pltpu.roll(w_bias_grad, 4, 0))
    share = chunk // HEADS
    for j in range(share):
        pay_ref[pl.ds(j, plane * HEADS, stride=share + 1), :] = main[
            pl.ds(col * share + j, plane * HEADS, stride=chunk), :
        ]
    pay_ref[pl.ds(share, plane * HEADS, stride=share + 1), :] = jnp.concatenate(
        [spread] * (plane * HEADS // 8), axis=0
    )


def turned_kernel(
    recv_ref,
    wb_ref,
    grad_q_ref,
    grad_k_ref,
    grad_v_ref,
    upstream_ref,
    token_grad_ref,
    rim_far_ref,
    rim_near_ref,
    own_out_ref,
    grad_pair_ref,
    zeros,
    grad_band,
    zero_sems,
    out_sems,
):
    seq, col = lax.axis_index("seq"), lax.axis_index("col")
    odd = lax.rem(seq, 2) == 1
    tokens = grad_band.shape[0]
    zeros[...] = jnp.zeros(zeros.shape, BF16)
    fills = [
        pltpu.make_async_copy(zeros, grad_pair_ref.at[t], zero_sems.at[t]) for t in range(tokens)
    ]
    for fill in fills:
        fill.start()
    atoms, width = grad_q_ref.shape
    head = width // HEADS

    rows = pad_rows(wb_ref[...].astype(F32), 8)
    turned = pad_rows(token_grad_ref[...], width).T[: 3 * SUB]
    for t in range(tokens):
        at = HEADS * t
        total = turned[:, at : at + 1] * rows[0:1]
        for h in range(1, HEADS):
            total = total + turned[:, at + h : at + h + 1] * rows[h : h + 1]
        grad_band[t] = total.astype(BF16)

    same = jnp.where(odd, 0, HEADS)
    wq_t, wk_t, wv_t, _ = gathered_weights(recv_ref, same, HEADS - same, head)
    key_part = mm2(grad_k_ref[...], wk_t) + mm2(grad_v_ref[...], wv_t)
    query_part = mm2(grad_q_ref[...], wq_t) + upstream_ref[...].astype(F32)
    shift = lax.rem(width - col * head, width)
    whole = jnp.concatenate(
        [key_part[REACH : REACH + atoms] + query_part, key_part[:REACH]]
        + [key_part[REACH + atoms :], jnp.zeros((REACH, width), F32)],
        axis=0,
    )
    whole = pltpu.roll(whole, shift, 1).T[:head]
    own_out_ref[...] = whole[:, :atoms]
    rim_down = whole[:, atoms : atoms + REACH]
    rim_up = whole[:, atoms + REACH : atoms + 2 * REACH]
    rim_far = jnp.where(odd, rim_up, rim_down)
    rim_far_ref[...] = jnp.concatenate([rim_far[: head // 2], rim_far[head // 2 :]], axis=1)
    rim_near_ref[...] = jnp.where(odd, rim_down, rim_up).astype(BF16)
    for fill in fills:
        fill.wait()
    outs = []
    for part, (own_part, safe) in enumerate(own_thirds(seq, col, grad_pair_ref.shape[1])):
        copy = pltpu.make_async_copy(
            grad_band.at[:, pl.ds(part * SUB, SUB), :],
            grad_pair_ref.at[:, pl.ds(safe, SUB), :],
            out_sems.at[part],
        )
        outs.append((own_part, safe, copy))

        @pl.when(own_part)
        def _(copy=copy):
            copy.start()

    wait_all(outs)


def final_kernel(
    gathered_ref,
    bias_ref,
    own_ref,
    near_ref,
    atoms_ref,
    gq_ref,
    gk_ref,
    gv_ref,
    go_ref,
    gb_ref,
    *,
    seqs,
    chunk,
):
    head, atoms = atoms_ref.shape
    seq = lax.axis_index("seq")
    odd = lax.rem(seq, 2) == 1
    rim_rows = head // 2
    rows = 2 * chunk + rim_rows
    plane = gathered_ref.shape[0] // rows
    partner = lax.rem(jnp.where(odd, seq + 1, seq - 1 + seqs), plane)
    far = gathered_ref[pl.ds(pl.multiple_of(partner * rows + 2 * chunk, 16), rim_rows), :].astype(F32)
    far = jnp.concatenate([far[:, :REACH], far[:, REACH:]], axis=0)
    far = jnp.where(jnp.where(odd, seq + 1, seq) % seqs == 0, 0.0, far)
    near = near_ref[...].astype(F32)
    below, above = jnp.where(odd, near, far), jnp.where(odd, far, near)
    middle = jnp.zeros((head, atoms - 2 * REACH), F32)
    atoms_ref[...] = (own_ref[...] + jnp.concatenate([below, middle, above], axis=1)).astype(BF16)
    terms = [gathered_ref[p * rows : p * rows + 2 * chunk, :].astype(F32) for p in range(plane)]
    main = jnp.concatenate([x[:chunk] + x[chunk:] for x in terms], axis=0)
    for i, ref in enumerate((gq_ref, gk_ref, gv_ref, go_ref)):
        ref[...] = main[i * head : (i + 1) * head]
    gb_ref[...] = bias_ref[...]


def vmem():
    return pl.BlockSpec(memory_space=pltpu.VMEM)


def smem():
    return pl.BlockSpec(memory_space=pltpu.SMEM)


def in_hbm():
    return pl.BlockSpec(memory_space=pltpu.MemorySpace.HBM)


def shape(dims, dtype):
    return jax.ShapeDtypeStruct(dims, dtype)


def params(mebibytes):
    return pltpu.CompilerParams(vmem_limit_bytes=mebibytes * 1024 * 1024)


def per_device(
    atom_inputs,
    atom_token,
    counts,
    window_start,
    pair_features,
    w_query,
    w_key,
    w_value,
    w_out,
    w_bias,
    atom_cotangent,
    token_cotangent,
):
    atoms, width = atom_inputs.shape
    tokens, columns, _ = pair_features.shape
    head = w_query.shape[1]
    seqs = lax.axis_size("seq")
    plane = 16 if seqs % 16 == 0 else 4
    planes = seqs // plane
    cols = lax.axis_size("col")
    seq = lax.axis_index("seq")
    odd = seq % 2 == 1
    token_row = atom_token[None, :]

    near = [(i, i ^ 1) for i in range(seqs)]
    far_groups = [
        [n * cols + c for n in (i, (i + 1) % seqs) for c in range(cols)] for i in range(1, seqs, 2)
    ]
    w_bias_t = w_bias.T
    pack, near_edge = pl.pallas_call(
        pack_kernel,
        out_shape=(
            shape((2 * HEADS, SAME_ROWS + 3 * SPARE, width), BF16),
            shape((REACH + 16, width), BF16),
        ),
        in_specs=[in_hbm()] * 8,
        out_specs=(in_hbm(), in_hbm()),
        scratch_shapes=[
            pltpu.VMEM((tokens, BAND, width), BF16),
            pltpu.VMEM((width, width), BF16),
            pltpu.VMEM((REACH // HEADS, width), BF16),
            pltpu.VMEM((tokens * HEADS, width), F32),
            pltpu.VMEM(w_bias_t.shape, BF16),
            pltpu.VMEM(token_row.shape, jnp.int32),
            pltpu.VMEM((REACH + 16, width), BF16),
            pltpu.VMEM((SAME_ROWS + 3 * SPARE, width), BF16),
            pltpu.VMEM((SAME_ROWS + 3 * SPARE, width), BF16),
            pltpu.SemaphoreType.DMA((3,)),
            pltpu.SemaphoreType.DMA((8,)),
            pltpu.SemaphoreType.DMA((2 * HEADS + 1,)),
        ],
        compiler_params=params(60),
        name="pack",
    )(
        pair_features,
        w_query.T,
        w_key.T,
        w_value.T,
        w_out,
        atom_inputs,
        w_bias_t,
        token_row,
    )
    near_edge = lax.ppermute(near_edge, "seq", near)
    recv = lax.all_to_all(
        pack, ("seq", "col"), 0, 0, tiled=True, axis_index_groups=far_groups
    )

    chunk = width // plane
    share = chunk // HEADS
    pay, *parts = pl.pallas_call(
        functools.partial(attention_kernel, seqs=seqs, plane=plane),
        out_shape=(
            shape((plane * HEADS * (share + 1), width), F32),
            shape((atoms, width), F32),
            shape((atoms + 2 * REACH, width), F32),
            shape((atoms + 2 * REACH, width), F32),
            shape((atoms, width), BF16),
            shape((tokens * HEADS, width), F32),
        ),
        in_specs=[smem(), in_hbm()] + [vmem()] * 8,
        out_specs=(vmem(),) * 6,
        scratch_shapes=[
            pltpu.VMEM((tokens, BAND, width), BF16),
            pltpu.VMEM((HEADS * width, width), F32),
            pltpu.SemaphoreType.DMA((3,)),
        ],
        compiler_params=params(32),
        name="attention",
    )(
        window_start,
        pair_features,
        recv,
        near_edge,
        atom_inputs,
        token_row,
        atom_token[:, None],
        counts[None, :],
        atom_cotangent,
        token_cotangent,
    )
    rim_far, rim_near, own_part, grad_pair = pl.pallas_call(
        turned_kernel,
        out_shape=(
            shape((head // 2, width), F32),
            shape((head, REACH), BF16),
            shape((head, atoms), F32),
            shape(pair_features.shape, BF16),
        ),
        in_specs=[vmem()] * 7,
        out_specs=(vmem(), vmem(), vmem(), in_hbm()),
        scratch_shapes=[
            pltpu.VMEM((columns, width), BF16),
            pltpu.VMEM((tokens, 3 * SUB, width), BF16),
            pltpu.SemaphoreType.DMA((tokens,)),
            pltpu.SemaphoreType.DMA((3,)),
        ],
        compiler_params=params(32),
        name="turned",
    )(recv, w_bias_t, *parts)

    whole_planes = [
        [(z * plane + i) * cols + c for i in range(plane) for c in range(cols)]
        for z in range(planes)
    ]
    across = [[z * plane + i for z in range(planes)] for i in range(plane)]
    within = [
        [(z + 1) * plane % seqs] + [z * plane + i for i in range(1, plane)] for z in range(planes)
    ]
    first = lax.all_to_all(
        pay.reshape(plane * HEADS, 1, (share + 1) * width), ("seq", "col"), 0, 0, tiled=True, axis_index_groups=whole_planes
    )
    summed = first.reshape(plane, HEADS, (share + 1) * width).sum(axis=0)
    mains = summed[:, : share * width].reshape(1, chunk * width)
    tail = summed[:, share * width :].sum(axis=0, keepdims=True)
    joined = jnp.concatenate([mains, tail], axis=1)
    joined, rim_near = lax.optimization_barrier((joined, rim_near))
    rim_near = lax.ppermute(rim_near, "seq", near)
    second = lax.all_to_all(
        jnp.broadcast_to(joined[None], (planes, 1, joined.shape[1])),
        "seq",
        0,
        0,
        tiled=True,
        axis_index_groups=across,
    ).sum(axis=0)
    partner = jnp.where(odd, seq + 1, seq - 1 + seqs) % plane
    positions = lax.broadcasted_iota(jnp.int32, (plane, 1, 1), 0)
    sums = second[:, : chunk * width].reshape(1, chunk, width)
    leading = lax.reduce_precision(sums, 8, 7)
    sums = jnp.concatenate([leading, sums - leading], axis=1)
    gathered = jnp.concatenate(
        [
            jnp.broadcast_to(sums, (plane, 2 * chunk, width)),
            jnp.where(positions == partner, rim_far[None], 0.0),
        ],
        axis=1,
    )
    gathered = gathered.astype(BF16).reshape(plane * (2 * chunk + head // 2), width)
    third = lax.all_to_all(gathered, "seq", 0, 0, tiled=True, axis_index_groups=within)
    grad_atoms, gq, gk, gv, go, gb = pl.pallas_call(
        functools.partial(final_kernel, seqs=seqs, chunk=chunk),
        out_shape=(
            shape((head, atoms), BF16),
            shape((head, width), F32),
            shape((head, width), F32),
            shape((head, width), F32),
            shape((head, width), F32),
            shape((1, width), F32),
        ),
        in_specs=[vmem()] * 4,
        out_specs=(vmem(),) * 6,
        compiler_params=params(16),
        name="final",
    )(
        third,
        second[:, chunk * width :],
        own_part,
        rim_near,
    )
    return (grad_atoms.T, grad_pair, gq.T, gk.T, gv.T, go, gb.T)


def solution(mesh):
    placed = (
        P("seq", None),
        P("seq"),
        P("seq"),
        P("seq"),
        P("seq", "col", None),
        P(None, "col"),
        P(None, "col"),
        P(None, "col"),
        P("col", None),
        P(),
        P("seq", None),
        P("seq", None),
    )
    return jax.shard_map(
        per_device,
        mesh=mesh,
        in_specs=placed,
        out_specs=(
            P("seq", "col"),
            P("seq", "col", None),
            P(None, "col"),
            P(None, "col"),
            P(None, "col"),
            P("col", None),
            P(None, "col"),
        ),
        check_vma=False,
    )
```

```python
import functools
import math

import jax
import jax.numpy as jnp
from jax import lax
from jax.experimental import pallas as pl
from jax.experimental.pallas import tpu as pltpu
from jax.sharding import PartitionSpec as P

QUERY_BLOCK = 32
KEY_WINDOW = 128
REACH = 64
SUB = 16
BAND = 64
GROUP = 96
SPAN = GROUP + 2 * REACH
HEADS = 4
SAME_ROWS = 40
NEAR_ROWS = 40
SPARE = 16
F32 = jnp.float32
BF16 = jnp.bfloat16

NN = (((1,), (0,)), ((), ()))
NT = (((1,), (1,)), ((), ()))
TN = (((0,), (0,)), ((), ()))


def mm(a, b, dims=NN):
    return lax.dot_general(a, b, dims, preferred_element_type=F32)


def halves(x):
    high = x.astype(BF16)
    return high, (x - high.astype(F32)).astype(BF16)


def mm2(a, b, dims=NN):
    high, low = halves(a)
    return mm(high, b, dims) + mm(low, b, dims)


def own_thirds(seq, col, width):
    thirds = []
    for part in range(3):
        start = (seq + part - 1) * SUB - col * width
        own = jnp.logical_and(start >= 0, start < width)
        thirds.append((own, pl.multiple_of(jnp.clip(start, 0, width - SUB), SUB)))
    return thirds


def band_copies(seq, col, pair_ref, band, sems):
    copies = []
    for part, (own, safe) in enumerate(own_thirds(seq, col, pair_ref.shape[1])):
        copy = pltpu.make_async_copy(
            pair_ref.at[:, pl.ds(safe, SUB), :],
            band.at[:, pl.ds(part * SUB, SUB), :],
            sems.at[part],
        )
        copies.append((own, safe, copy))
    return copies


def gathered_weights(recv_ref, near_ref, mine, same, paired, col):
    size = mine.shape[0]
    head = size // 4
    middle = size - SAME_ROWS - NEAR_ROWS
    ending = near_ref[REACH + 16 :, :].astype(F32)
    other = col + 1 - 2 * lax.rem(col, 2)
    whole = []
    for h in range(HEADS):
        first = recv_ref[same + h].astype(F32)[:SAME_ROWS]
        second = recv_ref[paired + h].astype(F32)
        across = jnp.concatenate([first, second[: size - SAME_ROWS]], axis=0)
        beside = jnp.concatenate([first, second[SAME_ROWS : SAME_ROWS + middle], ending], axis=0)
        whole.append(jnp.where(col == h, mine, jnp.where(other == h, beside, across)))
    return [
        jnp.concatenate([w[i * head : (i + 1) * head] for w in whole], axis=0).astype(BF16)
        for i in range(4)
    ]


def spare_lanes(rows):
    lane = lax.broadcasted_iota(jnp.int32, (rows, 2 * BAND), 1) & (BAND - 1)
    return lane, lane >= BAND - SPARE


def tucked(bias):
    _, spare = spare_lanes(SPARE)
    last = bias[3 * SPARE :]
    return jnp.concatenate(
        [
            jnp.where(spare, pltpu.roll(last, (3 - p) * SPARE, 1), bias[p * SPARE : (p + 1) * SPARE])
            for p in range(3)
        ],
        axis=0,
    )


def untucked(rows):
    lane, spare = spare_lanes(SPARE)
    blocks = [rows[p * SPARE : (p + 1) * SPARE] for p in range(3)]
    last = jnp.zeros_like(blocks[0])
    for p, block in enumerate(blocks):
        back = pltpu.roll(block, 2 * BAND - (3 - p) * SPARE, 1)
        last = jnp.where((lane >= p * SPARE) & (lane < (p + 1) * SPARE), back, last)
    return jnp.concatenate([jnp.where(spare, 0.0, block) for block in blocks] + [last], axis=0)


def start_band(copies, band):
    tokens = band.shape[0]
    band[:, 3 * SUB :, :] = jnp.zeros((tokens, BAND - 3 * SUB, band.shape[2]), BF16)
    for part, (own, _, copy) in enumerate(copies):

        @pl.when(own)
        def _(copy=copy):
            copy.start()

        @pl.when(jnp.logical_not(own))
        def _(part=part):
            band[:, part * SUB : (part + 1) * SUB, :] = jnp.zeros((tokens, SUB, band.shape[2]), BF16)


def wait_all(copies):
    for own, _, copy in copies:

        @pl.when(own)
        def _(copy=copy):
            copy.wait()


def pad_rows(x, rows):
    return jnp.concatenate([x, jnp.zeros((rows - x.shape[0],) + x.shape[1:], x.dtype)], axis=0)


def pick(condition, one, other):
    return jnp.where(condition, one.astype(F32), other.astype(F32))


def pack_kernel(
    pair_ref,
    wq_ref,
    wk_ref,
    wv_ref,
    wo_ref,
    atoms_ref,
    wb_ref,
    token_row_ref,
    pack_ref,
    near_ref,
    band,
    whole,
    edge,
    bias,
    weight_rows,
    token_line,
    near_edge,
    chunks,
    band_sems,
    sems,
    out_sems,
):
    seq, col = lax.axis_index("seq"), lax.axis_index("col")
    odd = lax.rem(seq, 2) == 1
    copies = band_copies(seq, col, pair_ref, band, band_sems)
    start_band(copies, band)
    tokens = band.shape[0]
    atoms = atoms_ref.shape[0]
    head = wq_ref.shape[0]
    share = REACH // 2
    first = jnp.where(odd, atoms - REACH, 0) + lax.rem(col, 2) * share
    near_first = jnp.where(odd, 0, atoms - REACH)
    others = [
        pltpu.make_async_copy(
            atoms_ref.at[pl.ds(pl.multiple_of(first, share), share), :], edge, sems.at[0]
        ),
        pltpu.make_async_copy(
            atoms_ref.at[pl.ds(pl.multiple_of(near_first, share), REACH), :],
            near_edge.at[:REACH, :],
            sems.at[5],
        ),
        pltpu.make_async_copy(wb_ref, weight_rows, sems.at[6]),
        pltpu.make_async_copy(token_row_ref, token_line, sems.at[7]),
    ] + [
        pltpu.make_async_copy(ref, whole.at[i * head : (i + 1) * head, :], sems.at[i + 1])
        for i, ref in enumerate((wq_ref, wk_ref, wv_ref, wo_ref))
    ]
    for copy in others:
        copy.start()
    for copy in others:
        copy.wait()
    row = token_line[...]
    lower, upper = row[:, :REACH], row[:, atoms - REACH :]

    def coded(token):
        code = token + 1
        line = jnp.concatenate([code >> 6, code & 63], axis=1).astype(F32)
        return jnp.broadcast_to(line, (16, line.shape[1]))

    line = coded(jnp.where(odd, upper, lower))
    near_edge[REACH : REACH + 16, :] = coded(jnp.where(odd, lower, upper)).astype(BF16)
    rows = pad_rows(weight_rows[...].astype(F32), 8).astype(BF16)
    weights = whole[...].astype(F32)
    ending = weights.shape[0] - NEAR_ROWS
    near_edge[REACH + 16 :, :] = weights[ending:].astype(BF16)
    outs = [pltpu.make_async_copy(near_edge, near_ref, out_sems.at[2 * HEADS])]
    outs[0].start()
    chunks[1] = jnp.concatenate(
        [edge[...].astype(F32), line[:8], weights[SAME_ROWS:ending]], axis=0
    ).astype(BF16)
    chunks[2] = weights[SAME_ROWS:].astype(BF16)
    wait_all(copies)
    for t in range(0, tokens, 2):
        part = mm(rows, band[t], NT) + pltpu.roll(mm(rows, band[t + 1], NT), 4, 0)
        high = part.astype(BF16).astype(F32)
        bias[4 * t : 4 * t + 8, :] = jnp.concatenate([high, part - high], axis=1)
    same = jnp.concatenate([weights[:SAME_ROWS], tucked(bias[...])], axis=0)
    chunks[0] = same.astype(BF16)
    for to in range(2 * HEADS):
        own_range = odd if to < HEADS else jnp.logical_not(odd)
        own_half = (to % HEADS) // 2 == lax.div(col, 2)
        kind = jnp.where(own_range, 0, jnp.where(own_half, 1, 2))
        copy = pltpu.make_async_copy(chunks.at[kind], pack_ref.at[to], out_sems.at[to])
        copy.start()
        outs.append(copy)
    for copy in outs:
        copy.wait()


def attention_kernel(
    window_ref,
    pair_ref,
    recv_ref,
    near_ref,
    own_ref,
    token_row_ref,
    token_col_ref,
    counts_ref,
    atom_cot_ref,
    token_cot_ref,
    wq_ref,
    wk_ref,
    wv_ref,
    wo_ref,
    pay_ref,
    grad_q_ref,
    grad_k_ref,
    grad_v_ref,
    upstream_ref,
    token_grad_ref,
    wq_out_ref,
    wk_out_ref,
    wv_out_ref,
    band,
    main,
    band_sems,
    *,
    seqs,
    plane,
):
    seq, col = lax.axis_index("seq"), lax.axis_index("col")
    copies = band_copies(seq, col, pair_ref, band, band_sems)
    start_band(copies, band)
    tokens = band.shape[0]
    odd = lax.rem(seq, 2) == 1
    atoms = own_ref.shape[0]
    width = own_ref.shape[1]
    head = width // HEADS
    inv_root = 1.0 / math.sqrt(head)
    slot_base = seq * atoms
    token_base = seq * tokens
    same = jnp.where(odd, 0, HEADS)
    paired = HEADS - same
    mine = jnp.concatenate(
        [ref[...].astype(F32) for ref in (wq_ref, wk_ref, wv_ref, wo_ref)], axis=0
    )
    wq_t, wk_t, wv_t, wo = gathered_weights(recv_ref, near_ref, mine, same, paired, col)
    wq_out_ref[...] = wq_t
    wk_out_ref[...] = wk_t
    wv_out_ref[...] = wv_t
    bias = recv_ref[same].astype(F32)[SAME_ROWS:]
    for c in range(1, HEADS):
        bias = bias + recv_ref[same + c].astype(F32)[SAME_ROWS:]
    bias = untucked(bias).astype(BF16)

    own = own_ref[...]
    share = REACH // 2
    beside = paired + lax.div(col, 2) * 2
    far_chunks = [recv_ref[beside + k].astype(F32)[: share + 8] for k in range(2)]
    far_rows = jnp.concatenate([x[:share] for x in far_chunks], axis=0)
    near_rows = near_ref[:REACH, :]
    has_below, has_above = seq > 0, seq < seqs - 1
    below = jnp.where(has_below, pick(odd, near_rows, far_rows), 0.0).astype(BF16)
    above = jnp.where(has_above, pick(odd, far_rows, near_rows), 0.0).astype(BF16)
    ext = jnp.concatenate([below, own, above], axis=0)
    queries = mm(own, wq_t, NT).astype(BF16)
    keys = mm(ext, wk_t, NT).astype(BF16)
    values = mm(ext, wv_t, NT).astype(BF16)

    token_col = token_col_ref[...]
    live_col = token_col >= 0
    local_col = token_col - token_base
    token_lanes = lax.broadcasted_iota(jnp.int32, (atoms, tokens), 1)
    onehot = (local_col == token_lanes).astype(F32)
    pooled = mm(onehot.astype(BF16), token_cot_ref[...])
    count = jnp.sum(onehot * counts_ref[...].astype(F32), axis=1, keepdims=True)
    safe_count = jnp.where(live_col, count, 1.0)
    upstream = jnp.where(live_col, atom_cot_ref[...].astype(F32) + pooled / safe_count, 0.0)
    upstream = upstream.astype(BF16)
    grad_attended = mm(upstream, wo, NT).astype(BF16)

    def decoded(row):
        return (row[:, :REACH] * 64.0 + row[:, REACH:]).astype(jnp.int32) - 1

    far_token = decoded(far_chunks[0][share : share + 1])
    near_token = decoded(near_ref[REACH : REACH + 16, :].astype(F32)[:1])
    below_token = jnp.where(has_below, jnp.where(odd, near_token, far_token), -1)
    above_token = jnp.where(has_above, jnp.where(odd, far_token, near_token), -1)
    own_row = token_row_ref[...]
    key_rows = (
        jnp.concatenate([below_token, own_row[:, : SPAN - REACH]], axis=1),
        jnp.concatenate([own_row[:, atoms - (SPAN - REACH) :], above_token], axis=1),
    )
    head_lanes = lax.broadcasted_iota(jnp.int32, (GROUP, width), 1) // head
    head_masks = [head_lanes == h for h in range(HEADS)]

    def stacked(x):
        return jnp.concatenate(
            [jnp.where(mask, x, jnp.zeros_like(x)) for mask in head_masks], axis=0
        )

    def folded(x):
        total = jnp.where(head_masks[0], x[:GROUP], 0.0)
        for h in range(1, HEADS):
            total = total + jnp.where(head_masks[h], x[h * GROUP : (h + 1) * GROUP], 0.0)
        return total

    attended, grad_queries, key_terms, value_terms = [], [], [], []
    token_grad = jnp.zeros((tokens * HEADS, width), F32)
    for g in range(atoms // GROUP):
        rows = slice(g * GROUP, (g + 1) * GROUP)
        span = slice(g * GROUP, g * GROUP + SPAN)
        k_g, v_g = keys[span], values[span]
        q_m = stacked(queries[rows].astype(F32)).astype(BF16)
        a_m = stacked(grad_attended[rows].astype(F32)).astype(BF16)
        key_token = key_rows[g]
        key_live = key_token >= 0
        key_band = jnp.where(key_live, key_token - (token_base - tokens), -1000)
        lane_band = lax.broadcasted_iota(jnp.int32, (width, SPAN), 0)
        key_onehot = ((lane_band & (BAND - 1)) == key_band).astype(F32).astype(BF16)
        local = local_col[rows]
        slot = lax.broadcasted_iota(jnp.int32, (GROUP, tokens * HEADS), 1)
        query_onehot = jnp.concatenate(
            [(slot == local * HEADS + h).astype(F32) for h in range(HEADS)], axis=0
        )
        query_onehot = query_onehot.astype(BF16)
        picked = mm(query_onehot, bias).astype(BF16)
        scores = mm(q_m, k_g, NT) * inv_root + mm(picked, key_onehot)
        scores = scores.reshape(HEADS, GROUP, SPAN)
        block = lax.broadcasted_iota(jnp.int32, (GROUP, 1), 0) // QUERY_BLOCK
        base = slot_base - REACH + g * GROUP
        first = g * (GROUP // QUERY_BLOCK)
        start = jnp.where(
            block == 0,
            window_ref[first] - base,
            jnp.where(block == 1, window_ref[first + 1] - base, window_ref[first + 2] - base),
        )
        position = lax.broadcasted_iota(jnp.int32, (GROUP, SPAN), 1)
        inside = (position >= start) & (position < start + KEY_WINDOW)
        dead_query = local < 0
        allowed = inside & (key_live | dead_query)
        masked = jnp.where(allowed[None], scores, -1e30)
        row_max = jnp.max(masked, axis=-1, keepdims=True)
        raw = jnp.where(allowed[None], jnp.exp(masked - row_max), 0.0)
        weights = raw / jnp.sum(raw, axis=-1, keepdims=True)
        grad_weights = mm(a_m, v_g, NT).reshape(HEADS, GROUP, SPAN)
        inner = jnp.sum(weights * grad_weights, axis=-1, keepdims=True)
        grad_scores = (weights * (grad_weights - inner)).reshape(HEADS * GROUP, SPAN)
        w_low = weights.reshape(HEADS * GROUP, SPAN).astype(BF16)
        s_high, s_low = halves(grad_scores)
        attended.append(folded(mm(w_low, v_g)))
        grad_queries.append(folded(mm(s_high, k_g)) * inv_root)
        key_terms.append(mm(s_high, q_m, TN) * inv_root)
        value_terms.append(mm(w_low, a_m, TN))
        by_token = mm(query_onehot, s_high, TN) + mm(query_onehot, s_low, TN)
        token_grad = token_grad + mm2(by_token, key_onehot, NT)

    attended = jnp.concatenate(attended, axis=0).astype(BF16)
    grad_q = jnp.concatenate(grad_queries, axis=0)

    def overlapped(terms):
        lap = SPAN - GROUP
        return jnp.concatenate(
            [terms[0][:GROUP], terms[0][GROUP:] + terms[1][:lap], terms[1][lap:]], axis=0
        )

    grad_k = overlapped(key_terms)
    grad_v = overlapped(value_terms)

    grad_q_ref[...] = grad_q
    grad_k_ref[...] = grad_k
    grad_v_ref[...] = grad_v
    upstream_ref[...] = upstream
    token_grad_ref[...] = token_grad

    chunk = width // plane
    products = (
        mm2(grad_q, own, TN),
        mm2(grad_k, ext, TN),
        mm2(grad_v, ext, TN),
        mm(attended, upstream, TN),
    )
    per_product = head // chunk
    for i, product in enumerate(products):
        for c in range(HEADS):
            for j in range(per_product):
                to = ((i * per_product + j) * HEADS + c) * chunk
                at = c * head + j * chunk
                main[to : to + chunk, :] = product[at : at + chunk]
    wait_all(copies)
    w_bias_grad = jnp.zeros((8, width), F32)
    left = lax.broadcasted_iota(jnp.int32, (8, width), 1) < BAND
    for t in range(0, tokens, 2):
        two = token_grad[HEADS * t : HEADS * t + 8]
        two = jnp.where(left, two, pltpu.roll(two, 4, 0))
        stack = jnp.concatenate([band[t], band[t + 1]], axis=0)
        both = mm(jnp.concatenate(halves(two), axis=0), stack)
        w_bias_grad = w_bias_grad + both[:8] + both[8:]
    upper = lax.broadcasted_iota(jnp.int32, (8, width), 0) < HEADS
    spread = jnp.where(upper, w_bias_grad, pltpu.roll(w_bias_grad, 4, 0))
    share = chunk // HEADS
    for j in range(share):
        pay_ref[pl.ds(j, plane * HEADS, stride=share + 1), :] = main[
            pl.ds(col * share + j, plane * HEADS, stride=chunk), :
        ]
    pay_ref[pl.ds(share, plane * HEADS, stride=share + 1), :] = jnp.concatenate(
        [spread] * (plane * HEADS // 8), axis=0
    )


def turned_kernel(
    wb_ref,
    grad_q_ref,
    grad_k_ref,
    grad_v_ref,
    upstream_ref,
    token_grad_ref,
    wq_ref,
    wk_ref,
    wv_ref,
    rim_far_ref,
    rim_near_ref,
    own_out_ref,
    grad_pair_ref,
    zeros,
    grad_band,
    zero_sems,
    out_sems,
):
    seq, col = lax.axis_index("seq"), lax.axis_index("col")
    odd = lax.rem(seq, 2) == 1
    tokens = grad_band.shape[0]
    zeros[...] = jnp.zeros(zeros.shape, BF16)
    fills = [
        pltpu.make_async_copy(zeros, grad_pair_ref.at[t], zero_sems.at[t]) for t in range(tokens)
    ]
    for fill in fills:
        fill.start()
    atoms, width = grad_q_ref.shape
    head = width // HEADS

    rows = pad_rows(wb_ref[...].astype(F32), 8)
    turned = pad_rows(token_grad_ref[...], width).T[: 3 * SUB]
    for t in range(tokens):
        at = HEADS * t
        total = turned[:, at : at + 1] * rows[0:1]
        for h in range(1, HEADS):
            total = total + turned[:, at + h : at + h + 1] * rows[h : h + 1]
        grad_band[t] = total.astype(BF16)

    key_part = mm2(grad_k_ref[...], wk_ref[...]) + mm2(grad_v_ref[...], wv_ref[...])
    query_part = mm2(grad_q_ref[...], wq_ref[...]) + upstream_ref[...].astype(F32)
    shift = lax.rem(width - col * head, width)
    whole = jnp.concatenate(
        [key_part[REACH : REACH + atoms] + query_part, key_part[:REACH]]
        + [key_part[REACH + atoms :], jnp.zeros((REACH, width), F32)],
        axis=0,
    )
    whole = pltpu.roll(whole, shift, 1).T[:head]
    own_out_ref[...] = whole[:, :atoms]
    rim_down = whole[:, atoms : atoms + REACH]
    rim_up = whole[:, atoms + REACH : atoms + 2 * REACH]
    rim_far = jnp.where(odd, rim_up, rim_down)
    rim_far_ref[...] = jnp.concatenate([rim_far[: head // 2], rim_far[head // 2 :]], axis=1)
    rim_near_ref[...] = jnp.where(odd, rim_down, rim_up).astype(BF16)
    for fill in fills:
        fill.wait()
    outs = []
    for part, (own_part, safe) in enumerate(own_thirds(seq, col, grad_pair_ref.shape[1])):
        copy = pltpu.make_async_copy(
            grad_band.at[:, pl.ds(part * SUB, SUB), :],
            grad_pair_ref.at[:, pl.ds(safe, SUB), :],
            out_sems.at[part],
        )
        outs.append((own_part, safe, copy))

        @pl.when(own_part)
        def _(copy=copy):
            copy.start()

    wait_all(outs)


def final_kernel(
    gathered_ref,
    bias_ref,
    own_ref,
    near_ref,
    atoms_ref,
    gq_ref,
    gk_ref,
    gv_ref,
    go_ref,
    gb_ref,
    *,
    seqs,
    chunk,
):
    head, atoms = atoms_ref.shape
    seq = lax.axis_index("seq")
    odd = lax.rem(seq, 2) == 1
    rim_rows = head // 2
    rows = 2 * chunk + rim_rows
    plane = gathered_ref.shape[0] // rows
    partner = lax.rem(jnp.where(odd, seq + 1, seq - 1 + seqs), plane)
    far = gathered_ref[pl.ds(pl.multiple_of(partner * rows + 2 * chunk, 16), rim_rows), :].astype(F32)
    far = jnp.concatenate([far[:, :REACH], far[:, REACH:]], axis=0)
    far = jnp.where(jnp.where(odd, seq + 1, seq) % seqs == 0, 0.0, far)
    near = near_ref[...].astype(F32)
    below, above = jnp.where(odd, near, far), jnp.where(odd, far, near)
    middle = jnp.zeros((head, atoms - 2 * REACH), F32)
    atoms_ref[...] = (own_ref[...] + jnp.concatenate([below, middle, above], axis=1)).astype(BF16)
    terms = [gathered_ref[p * rows : p * rows + 2 * chunk, :].astype(F32) for p in range(plane)]
    main = jnp.concatenate([x[:chunk] + x[chunk:] for x in terms], axis=0)
    for i, ref in enumerate((gq_ref, gk_ref, gv_ref, go_ref)):
        ref[...] = main[i * head : (i + 1) * head]
    gb_ref[...] = bias_ref[...]


def vmem():
    return pl.BlockSpec(memory_space=pltpu.VMEM)


def smem():
    return pl.BlockSpec(memory_space=pltpu.SMEM)


def in_hbm():
    return pl.BlockSpec(memory_space=pltpu.MemorySpace.HBM)


def shape(dims, dtype):
    return jax.ShapeDtypeStruct(dims, dtype)


def params(mebibytes):
    return pltpu.CompilerParams(vmem_limit_bytes=mebibytes * 1024 * 1024)


def per_device(
    atom_inputs,
    atom_token,
    counts,
    window_start,
    pair_features,
    w_query,
    w_key,
    w_value,
    w_out,
    w_bias,
    atom_cotangent,
    token_cotangent,
):
    atoms, width = atom_inputs.shape
    tokens, columns, _ = pair_features.shape
    head = w_query.shape[1]
    seqs = lax.axis_size("seq")
    plane = 16 if seqs % 16 == 0 else 4
    planes = seqs // plane
    cols = lax.axis_size("col")
    seq = lax.axis_index("seq")
    odd = seq % 2 == 1
    token_row = atom_token[None, :]

    near = [(i, i ^ 1) for i in range(seqs)]
    far_groups = [
        [n * cols + c for n in (i, (i + 1) % seqs) for c in range(cols)] for i in range(1, seqs, 2)
    ]
    w_bias_t = w_bias.T
    weights = (w_query.T, w_key.T, w_value.T, w_out)
    pack, near_edge = pl.pallas_call(
        pack_kernel,
        out_shape=(
            shape((2 * HEADS, SAME_ROWS + 3 * SPARE, width), BF16),
            shape((REACH + 16 + NEAR_ROWS, width), BF16),
        ),
        in_specs=[in_hbm()] * 8,
        out_specs=(in_hbm(), in_hbm()),
        scratch_shapes=[
            pltpu.VMEM((tokens, BAND, width), BF16),
            pltpu.VMEM((width, width), BF16),
            pltpu.VMEM((REACH // 2, width), BF16),
            pltpu.VMEM((tokens * HEADS, width), F32),
            pltpu.VMEM(w_bias_t.shape, BF16),
            pltpu.VMEM(token_row.shape, jnp.int32),
            pltpu.VMEM((REACH + 16 + NEAR_ROWS, width), BF16),
            pltpu.VMEM((3, SAME_ROWS + 3 * SPARE, width), BF16),
            pltpu.SemaphoreType.DMA((3,)),
            pltpu.SemaphoreType.DMA((8,)),
            pltpu.SemaphoreType.DMA((2 * HEADS + 1,)),
        ],
        compiler_params=params(60),
        name="pack",
    )(
        pair_features,
        *weights,
        atom_inputs,
        w_bias_t,
        token_row,
    )
    near_heads = [(i * cols + c, (i ^ 1) * cols + (c ^ 1)) for i in range(seqs) for c in range(cols)]
    near_edge = lax.ppermute(near_edge, ("seq", "col"), near_heads)
    recv = lax.all_to_all(
        pack, ("seq", "col"), 0, 0, tiled=True, axis_index_groups=far_groups
    )

    chunk = width // plane
    share = chunk // HEADS
    pay, *parts = pl.pallas_call(
        functools.partial(attention_kernel, seqs=seqs, plane=plane),
        out_shape=(
            shape((plane * HEADS * (share + 1), width), F32),
            shape((atoms, width), F32),
            shape((atoms + 2 * REACH, width), F32),
            shape((atoms + 2 * REACH, width), F32),
            shape((atoms, width), BF16),
            shape((tokens * HEADS, width), F32),
        )
        + (shape((width, width), BF16),) * 3,
        in_specs=[smem(), in_hbm()] + [vmem()] * 12,
        out_specs=(vmem(),) * 9,
        scratch_shapes=[
            pltpu.VMEM((tokens, BAND, width), BF16),
            pltpu.VMEM((HEADS * width, width), F32),
            pltpu.SemaphoreType.DMA((3,)),
        ],
        compiler_params=params(32),
        name="attention",
    )(
        window_start,
        pair_features,
        recv,
        near_edge,
        atom_inputs,
        token_row,
        atom_token[:, None],
        counts[None, :],
        atom_cotangent,
        token_cotangent,
        *weights,
    )
    rim_far, rim_near, own_part, grad_pair = pl.pallas_call(
        turned_kernel,
        out_shape=(
            shape((head // 2, width), F32),
            shape((head, REACH), BF16),
            shape((head, atoms), F32),
            shape(pair_features.shape, BF16),
        ),
        in_specs=[vmem()] * 9,
        out_specs=(vmem(), vmem(), vmem(), in_hbm()),
        scratch_shapes=[
            pltpu.VMEM((columns, width), BF16),
            pltpu.VMEM((tokens, 3 * SUB, width), BF16),
            pltpu.SemaphoreType.DMA((tokens,)),
            pltpu.SemaphoreType.DMA((3,)),
        ],
        compiler_params=params(32),
        name="turned",
    )(w_bias_t, *parts)

    whole_planes = [
        [(z * plane + i) * cols + c for i in range(plane) for c in range(cols)]
        for z in range(planes)
    ]
    across = [[z * plane + i for z in range(planes)] for i in range(plane)]
    within = [
        [(z + 1) * plane % seqs] + [z * plane + i for i in range(1, plane)] for z in range(planes)
    ]
    first = lax.all_to_all(
        pay.reshape(plane * HEADS, 1, (share + 1) * width), ("seq", "col"), 0, 0, tiled=True, axis_index_groups=whole_planes
    )
    summed = first.reshape(plane, HEADS, (share + 1) * width).sum(axis=0)
    mains = summed[:, : share * width].reshape(1, chunk * width)
    tail = summed[:, share * width :].sum(axis=0, keepdims=True)
    joined = jnp.concatenate([mains, tail], axis=1)
    joined, rim_near = lax.optimization_barrier((joined, rim_near))
    rim_near = lax.ppermute(rim_near, "seq", near)
    second = lax.all_to_all(
        jnp.broadcast_to(joined[None], (planes, 1, joined.shape[1])),
        "seq",
        0,
        0,
        tiled=True,
        axis_index_groups=across,
    ).sum(axis=0)
    partner = jnp.where(odd, seq + 1, seq - 1 + seqs) % plane
    positions = lax.broadcasted_iota(jnp.int32, (plane, 1, 1), 0)
    sums = second[:, : chunk * width].reshape(1, chunk, width)
    leading = lax.reduce_precision(sums, 8, 7)
    sums = jnp.concatenate([leading, sums - leading], axis=1)
    gathered = jnp.concatenate(
        [
            jnp.broadcast_to(sums, (plane, 2 * chunk, width)),
            jnp.where(positions == partner, rim_far[None], 0.0),
        ],
        axis=1,
    )
    gathered = gathered.astype(BF16).reshape(plane * (2 * chunk + head // 2), width)
    third = lax.all_to_all(gathered, "seq", 0, 0, tiled=True, axis_index_groups=within)
    grad_atoms, gq, gk, gv, go, gb = pl.pallas_call(
        functools.partial(final_kernel, seqs=seqs, chunk=chunk),
        out_shape=(
            shape((head, atoms), BF16),
            shape((head, width), F32),
            shape((head, width), F32),
            shape((head, width), F32),
            shape((head, width), F32),
            shape((1, width), F32),
        ),
        in_specs=[vmem()] * 4,
        out_specs=(vmem(),) * 6,
        compiler_params=params(16),
        name="final",
    )(
        third,
        second[:, chunk * width :],
        own_part,
        rim_near,
    )
    return (grad_atoms.T, grad_pair, gq.T, gk.T, gv.T, go, gb.T)


def solution(mesh):
    placed = (
        P("seq", None),
        P("seq"),
        P("seq"),
        P("seq"),
        P("seq", "col", None),
        P(None, "col"),
        P(None, "col"),
        P(None, "col"),
        P("col", None),
        P(),
        P("seq", None),
        P("seq", None),
    )
    return jax.shard_map(
        per_device,
        mesh=mesh,
        in_specs=placed,
        out_specs=(
            P("seq", "col"),
            P("seq", "col", None),
            P(None, "col"),
            P(None, "col"),
            P(None, "col"),
            P("col", None),
            P(None, "col"),
        ),
        check_vma=False,
    )
```

```python
import functools
import math

import jax
import jax.numpy as jnp
from jax import lax
from jax.experimental import pallas as pl
from jax.experimental.pallas import tpu as pltpu
from jax.sharding import PartitionSpec as P

QUERY_BLOCK = 32
KEY_WINDOW = 128
REACH = 64
SUB = 16
BAND = 64
GROUP = 96
SPAN = GROUP + 2 * REACH
HEADS = 4
SAME_ROWS = 40
NEAR_ROWS = 40
SPARE = 16
F32 = jnp.float32
BF16 = jnp.bfloat16

NN = (((1,), (0,)), ((), ()))
NT = (((1,), (1,)), ((), ()))
TN = (((0,), (0,)), ((), ()))


def mm(a, b, dims=NN):
    return lax.dot_general(a, b, dims, preferred_element_type=F32)


def halves(x):
    high = x.astype(BF16)
    return high, (x - high.astype(F32)).astype(BF16)


def mm2(a, b, dims=NN):
    high, low = halves(a)
    return mm(high, b, dims) + mm(low, b, dims)


def own_thirds(seq, col, width):
    thirds = []
    for part in range(3):
        start = (seq + part - 1) * SUB - col * width
        own = jnp.logical_and(start >= 0, start < width)
        thirds.append((own, pl.multiple_of(jnp.clip(start, 0, width - SUB), SUB)))
    return thirds


def band_copies(seq, col, pair_ref, band, sems):
    copies = []
    for part, (own, safe) in enumerate(own_thirds(seq, col, pair_ref.shape[1])):
        copy = pltpu.make_async_copy(
            pair_ref.at[:, pl.ds(safe, SUB), :],
            band.at[:, pl.ds(part * SUB, SUB), :],
            sems.at[part],
        )
        copies.append((own, safe, copy))
    return copies


def gathered_weights(recv_ref, near_ref, mine, same, paired, col):
    size = mine.shape[0]
    head = size // 4
    middle = size - SAME_ROWS - NEAR_ROWS
    ending = near_ref[REACH + 16 :, :].astype(F32)
    other = col + 1 - 2 * lax.rem(col, 2)
    whole = []
    for h in range(HEADS):
        first = recv_ref[same + h].astype(F32)[:SAME_ROWS]
        second = recv_ref[paired + h].astype(F32)
        across = jnp.concatenate([first, second[: size - SAME_ROWS]], axis=0)
        beside = jnp.concatenate([first, second[SAME_ROWS : SAME_ROWS + middle], ending], axis=0)
        whole.append(jnp.where(col == h, mine, jnp.where(other == h, beside, across)))
    return [
        jnp.concatenate([w[i * head : (i + 1) * head] for w in whole], axis=0).astype(BF16)
        for i in range(4)
    ]


def spare_lanes(rows):
    lane = lax.broadcasted_iota(jnp.int32, (rows, 2 * BAND), 1) & (BAND - 1)
    return lane, lane >= BAND - SPARE


def tucked(bias):
    _, spare = spare_lanes(SPARE)
    last = bias[3 * SPARE :]
    return jnp.concatenate(
        [
            jnp.where(spare, pltpu.roll(last, (3 - p) * SPARE, 1), bias[p * SPARE : (p + 1) * SPARE])
            for p in range(3)
        ],
        axis=0,
    )


def untucked(rows):
    lane, spare = spare_lanes(SPARE)
    blocks = [rows[p * SPARE : (p + 1) * SPARE] for p in range(3)]
    last = jnp.zeros_like(blocks[0])
    for p, block in enumerate(blocks):
        back = pltpu.roll(block, 2 * BAND - (3 - p) * SPARE, 1)
        last = jnp.where((lane >= p * SPARE) & (lane < (p + 1) * SPARE), back, last)
    return jnp.concatenate([jnp.where(spare, 0.0, block) for block in blocks] + [last], axis=0)


def start_band(copies, band):
    tokens = band.shape[0]
    band[:, 3 * SUB :, :] = jnp.zeros((tokens, BAND - 3 * SUB, band.shape[2]), BF16)
    for part, (own, _, copy) in enumerate(copies):

        @pl.when(own)
        def _(copy=copy):
            copy.start()

        @pl.when(jnp.logical_not(own))
        def _(part=part):
            band[:, part * SUB : (part + 1) * SUB, :] = jnp.zeros((tokens, SUB, band.shape[2]), BF16)


def wait_all(copies):
    for own, _, copy in copies:

        @pl.when(own)
        def _(copy=copy):
            copy.wait()


def pad_rows(x, rows):
    return jnp.concatenate([x, jnp.zeros((rows - x.shape[0],) + x.shape[1:], x.dtype)], axis=0)


def pick(condition, one, other):
    return jnp.where(condition, one.astype(F32), other.astype(F32))


def pack_kernel(
    pair_ref,
    wq_ref,
    wk_ref,
    wv_ref,
    wo_ref,
    atoms_ref,
    wb_ref,
    token_row_ref,
    pack_ref,
    near_ref,
    band,
    whole,
    edge,
    bias,
    weight_rows,
    token_line,
    near_edge,
    chunks,
    band_sems,
    sems,
    out_sems,
):
    seq, col = lax.axis_index("seq"), lax.axis_index("col")
    odd = lax.rem(seq, 2) == 1
    copies = band_copies(seq, col, pair_ref, band, band_sems)
    start_band(copies, band)
    tokens = band.shape[0]
    atoms = atoms_ref.shape[0]
    head = wq_ref.shape[0]
    share = REACH // 2
    first = jnp.where(odd, atoms - REACH, 0) + lax.rem(col, 2) * share
    near_first = jnp.where(odd, 0, atoms - REACH)
    others = [
        pltpu.make_async_copy(
            atoms_ref.at[pl.ds(pl.multiple_of(first, share), share), :], edge, sems.at[0]
        ),
        pltpu.make_async_copy(
            atoms_ref.at[pl.ds(pl.multiple_of(near_first, share), REACH), :],
            near_edge.at[:REACH, :],
            sems.at[5],
        ),
        pltpu.make_async_copy(wb_ref, weight_rows, sems.at[6]),
        pltpu.make_async_copy(token_row_ref, token_line, sems.at[7]),
    ] + [
        pltpu.make_async_copy(ref, whole.at[i * head : (i + 1) * head, :], sems.at[i + 1])
        for i, ref in enumerate((wq_ref, wk_ref, wv_ref, wo_ref))
    ]
    for copy in others:
        copy.start()
    for copy in others:
        copy.wait()
    row = token_line[...]
    lower, upper = row[:, :REACH], row[:, atoms - REACH :]

    def coded(token):
        code = token + 1
        line = jnp.concatenate([code >> 6, code & 63], axis=1).astype(F32)
        return jnp.broadcast_to(line, (16, line.shape[1]))

    line = coded(jnp.where(odd, upper, lower))
    near_edge[REACH : REACH + 16, :] = coded(jnp.where(odd, lower, upper)).astype(BF16)
    rows = pad_rows(weight_rows[...].astype(F32), 8).astype(BF16)
    weights = whole[...].astype(F32)
    ending = weights.shape[0] - NEAR_ROWS
    near_edge[REACH + 16 :, :] = weights[ending:].astype(BF16)
    outs = [pltpu.make_async_copy(near_edge, near_ref, out_sems.at[2 * HEADS])]
    outs[0].start()
    chunks[1] = jnp.concatenate(
        [edge[...].astype(F32), line[:8], weights[SAME_ROWS:ending]], axis=0
    ).astype(BF16)
    chunks[2] = weights[SAME_ROWS:].astype(BF16)
    wait_all(copies)
    for t in range(0, tokens, 2):
        part = mm(rows, band[t], NT) + pltpu.roll(mm(rows, band[t + 1], NT), 4, 0)
        high = part.astype(BF16).astype(F32)
        bias[4 * t : 4 * t + 8, :] = jnp.concatenate([high, part - high], axis=1)
    same = jnp.concatenate([weights[:SAME_ROWS], tucked(bias[...])], axis=0)
    chunks[0] = same.astype(BF16)
    for to in range(2 * HEADS):
        own_range = odd if to < HEADS else jnp.logical_not(odd)
        own_half = (to % HEADS) // 2 == lax.div(col, 2)
        kind = jnp.where(own_range, 0, jnp.where(own_half, 1, 2))
        copy = pltpu.make_async_copy(chunks.at[kind], pack_ref.at[to], out_sems.at[to])
        copy.start()
        outs.append(copy)
    for copy in outs:
        copy.wait()


def attention_kernel(
    window_ref,
    pair_ref,
    recv_ref,
    near_ref,
    own_ref,
    token_row_ref,
    token_col_ref,
    counts_ref,
    atom_cot_ref,
    token_cot_ref,
    wq_ref,
    wk_ref,
    wv_ref,
    wo_ref,
    pay_ref,
    grad_q_ref,
    grad_k_ref,
    grad_v_ref,
    upstream_ref,
    token_grad_ref,
    wq_out_ref,
    wk_out_ref,
    wv_out_ref,
    band,
    main,
    band_sems,
    *,
    seqs,
    plane,
):
    seq, col = lax.axis_index("seq"), lax.axis_index("col")
    copies = band_copies(seq, col, pair_ref, band, band_sems)
    start_band(copies, band)
    tokens = band.shape[0]
    odd = lax.rem(seq, 2) == 1
    atoms = own_ref.shape[0]
    width = own_ref.shape[1]
    head = width // HEADS
    inv_root = 1.0 / math.sqrt(head)
    slot_base = seq * atoms
    token_base = seq * tokens
    same = jnp.where(odd, 0, HEADS)
    paired = HEADS - same
    mine = jnp.concatenate(
        [ref[...].astype(F32) for ref in (wq_ref, wk_ref, wv_ref, wo_ref)], axis=0
    )
    wq_t, wk_t, wv_t, wo = gathered_weights(recv_ref, near_ref, mine, same, paired, col)
    wq_out_ref[...] = wq_t
    wk_out_ref[...] = wk_t
    wv_out_ref[...] = wv_t
    bias = recv_ref[same].astype(F32)[SAME_ROWS:]
    for c in range(1, HEADS):
        bias = bias + recv_ref[same + c].astype(F32)[SAME_ROWS:]
    bias = untucked(bias).astype(BF16)

    own = own_ref[...]
    share = REACH // 2
    beside = paired + lax.div(col, 2) * 2
    far_chunks = [recv_ref[beside + k].astype(F32)[: share + 8] for k in range(2)]
    far_rows = jnp.concatenate([x[:share] for x in far_chunks], axis=0)
    near_rows = near_ref[:REACH, :]
    has_below, has_above = seq > 0, seq < seqs - 1
    below = jnp.where(has_below, pick(odd, near_rows, far_rows), 0.0).astype(BF16)
    above = jnp.where(has_above, pick(odd, far_rows, near_rows), 0.0).astype(BF16)
    ext = jnp.concatenate([below, own, above], axis=0)
    queries = mm(own, wq_t, NT).astype(BF16)
    keys = mm(ext, wk_t, NT).astype(BF16)
    values = mm(ext, wv_t, NT).astype(BF16)

    token_col = token_col_ref[...]
    live_col = token_col >= 0
    local_col = token_col - token_base
    token_lanes = lax.broadcasted_iota(jnp.int32, (atoms, tokens), 1)
    onehot = (local_col == token_lanes).astype(F32)
    pooled = mm(onehot.astype(BF16), token_cot_ref[...])
    count = jnp.sum(onehot * counts_ref[...].astype(F32), axis=1, keepdims=True)
    safe_count = jnp.where(live_col, count, 1.0)
    upstream = jnp.where(live_col, atom_cot_ref[...].astype(F32) + pooled / safe_count, 0.0)
    upstream = upstream.astype(BF16)
    grad_attended = mm(upstream, wo, NT).astype(BF16)

    def decoded(row):
        return (row[:, :REACH] * 64.0 + row[:, REACH:]).astype(jnp.int32) - 1

    far_token = decoded(far_chunks[0][share : share + 1])
    near_token = decoded(near_ref[REACH : REACH + 16, :].astype(F32)[:1])
    below_token = jnp.where(has_below, jnp.where(odd, near_token, far_token), -1)
    above_token = jnp.where(has_above, jnp.where(odd, far_token, near_token), -1)
    own_row = token_row_ref[...]
    key_rows = (
        jnp.concatenate([below_token, own_row[:, : SPAN - REACH]], axis=1),
        jnp.concatenate([own_row[:, atoms - (SPAN - REACH) :], above_token], axis=1),
    )
    head_lanes = lax.broadcasted_iota(jnp.int32, (GROUP, width), 1) // head
    head_masks = [head_lanes == h for h in range(HEADS)]

    def stacked(x):
        return jnp.concatenate(
            [jnp.where(mask, x, jnp.zeros_like(x)) for mask in head_masks], axis=0
        )

    def folded(x):
        total = jnp.where(head_masks[0], x[:GROUP], 0.0)
        for h in range(1, HEADS):
            total = total + jnp.where(head_masks[h], x[h * GROUP : (h + 1) * GROUP], 0.0)
        return total

    attended, grad_queries, key_terms, value_terms = [], [], [], []
    token_grad = jnp.zeros((tokens * HEADS, width), F32)
    for g in range(atoms // GROUP):
        rows = slice(g * GROUP, (g + 1) * GROUP)
        span = slice(g * GROUP, g * GROUP + SPAN)
        k_g, v_g = keys[span], values[span]
        q_m = stacked(queries[rows].astype(F32)).astype(BF16)
        a_m = stacked(grad_attended[rows].astype(F32)).astype(BF16)
        key_token = key_rows[g]
        key_live = key_token >= 0
        key_band = jnp.where(key_live, key_token - (token_base - tokens), -1000)
        lane_band = lax.broadcasted_iota(jnp.int32, (width, SPAN), 0)
        key_onehot = ((lane_band & (BAND - 1)) == key_band).astype(F32).astype(BF16)
        local = local_col[rows]
        slot = lax.broadcasted_iota(jnp.int32, (GROUP, tokens * HEADS), 1)
        query_onehot = jnp.concatenate(
            [(slot == local * HEADS + h).astype(F32) for h in range(HEADS)], axis=0
        )
        query_onehot = query_onehot.astype(BF16)
        picked = mm(query_onehot, bias).astype(BF16)
        scores = mm(q_m, k_g, NT) * inv_root + mm(picked, key_onehot)
        scores = scores.reshape(HEADS, GROUP, SPAN)
        block = lax.broadcasted_iota(jnp.int32, (GROUP, 1), 0) // QUERY_BLOCK
        base = slot_base - REACH + g * GROUP
        first = g * (GROUP // QUERY_BLOCK)
        start = jnp.where(
            block == 0,
            window_ref[first] - base,
            jnp.where(block == 1, window_ref[first + 1] - base, window_ref[first + 2] - base),
        )
        position = lax.broadcasted_iota(jnp.int32, (GROUP, SPAN), 1)
        inside = (position >= start) & (position < start + KEY_WINDOW)
        dead_query = local < 0
        allowed = inside & (key_live | dead_query)
        masked = jnp.where(allowed[None], scores, -1e30)
        row_max = jnp.max(masked, axis=-1, keepdims=True)
        raw = jnp.where(allowed[None], jnp.exp(masked - row_max), 0.0)
        weights = raw / jnp.sum(raw, axis=-1, keepdims=True)
        grad_weights = mm(a_m, v_g, NT).reshape(HEADS, GROUP, SPAN)
        inner = jnp.sum(weights * grad_weights, axis=-1, keepdims=True)
        grad_scores = (weights * (grad_weights - inner)).reshape(HEADS * GROUP, SPAN)
        w_low = weights.reshape(HEADS * GROUP, SPAN).astype(BF16)
        s_high, s_low = halves(grad_scores)
        attended.append(folded(mm(w_low, v_g)))
        grad_queries.append(folded(mm(s_high, k_g)) * inv_root)
        key_terms.append(mm(s_high, q_m, TN) * inv_root)
        value_terms.append(mm(w_low, a_m, TN))
        by_token = mm(query_onehot, s_high, TN) + mm(query_onehot, s_low, TN)
        token_grad = token_grad + mm2(by_token, key_onehot, NT)

    attended = jnp.concatenate(attended, axis=0).astype(BF16)
    grad_q = jnp.concatenate(grad_queries, axis=0)

    def overlapped(terms):
        lap = SPAN - GROUP
        return jnp.concatenate(
            [terms[0][:GROUP], terms[0][GROUP:] + terms[1][:lap], terms[1][lap:]], axis=0
        )

    grad_k = overlapped(key_terms)
    grad_v = overlapped(value_terms)

    grad_q_ref[...] = grad_q
    grad_k_ref[...] = grad_k
    grad_v_ref[...] = grad_v
    upstream_ref[...] = upstream
    token_grad_ref[...] = token_grad

    chunk = width // plane
    products = (
        mm2(grad_q, own, TN),
        mm2(grad_k, ext, TN),
        mm2(grad_v, ext, TN),
        mm(attended, upstream, TN),
    )
    per_product = head // chunk
    for i, product in enumerate(products):
        for c in range(HEADS):
            for j in range(per_product):
                to = ((i * per_product + j) * HEADS + c) * chunk
                at = c * head + j * chunk
                main[to : to + chunk, :] = product[at : at + chunk]
    wait_all(copies)
    w_bias_grad = jnp.zeros((8, width), F32)
    left = lax.broadcasted_iota(jnp.int32, (8, width), 1) < BAND
    for t in range(0, tokens, 2):
        two = token_grad[HEADS * t : HEADS * t + 8]
        two = jnp.where(left, two, pltpu.roll(two, 4, 0))
        stack = jnp.concatenate([band[t], band[t + 1]], axis=0)
        both = mm(jnp.concatenate(halves(two), axis=0), stack)
        w_bias_grad = w_bias_grad + both[:8] + both[8:]
    upper = lax.broadcasted_iota(jnp.int32, (8, width), 0) < HEADS
    spread = jnp.where(upper, w_bias_grad, pltpu.roll(w_bias_grad, 4, 0))
    share = chunk // HEADS
    for j in range(share):
        pay_ref[pl.ds(j, plane * HEADS, stride=share + 1), :] = main[
            pl.ds(col * share + j, plane * HEADS, stride=chunk), :
        ]
    pay_ref[pl.ds(share, plane * HEADS, stride=share + 1), :] = jnp.concatenate(
        [spread] * (plane * HEADS // 8), axis=0
    )


def turned_kernel(
    wb_ref,
    grad_q_ref,
    grad_k_ref,
    grad_v_ref,
    upstream_ref,
    token_grad_ref,
    wq_ref,
    wk_ref,
    wv_ref,
    rim_far_ref,
    rim_near_ref,
    own_out_ref,
    grad_pair_ref,
    zeros,
    grad_band,
    zero_sems,
    out_sems,
):
    seq, col = lax.axis_index("seq"), lax.axis_index("col")
    odd = lax.rem(seq, 2) == 1
    tokens = grad_band.shape[0]
    zeros[...] = jnp.zeros(zeros.shape, BF16)
    fills = [
        pltpu.make_async_copy(zeros, grad_pair_ref.at[t], zero_sems.at[t]) for t in range(tokens)
    ]
    for fill in fills:
        fill.start()
    atoms, width = grad_q_ref.shape
    head = width // HEADS

    rows = pad_rows(wb_ref[...].astype(F32), 8)
    turned = pad_rows(token_grad_ref[...], width).T[: 3 * SUB]
    for t in range(tokens):
        at = HEADS * t
        total = turned[:, at : at + 1] * rows[0:1]
        for h in range(1, HEADS):
            total = total + turned[:, at + h : at + h + 1] * rows[h : h + 1]
        grad_band[t] = total.astype(BF16)

    key_part = mm2(grad_k_ref[...], wk_ref[...]) + mm2(grad_v_ref[...], wv_ref[...])
    query_part = mm2(grad_q_ref[...], wq_ref[...]) + upstream_ref[...].astype(F32)
    shift = lax.rem(width - col * head, width)
    whole = jnp.concatenate(
        [key_part[REACH : REACH + atoms] + query_part, key_part[:REACH]]
        + [key_part[REACH + atoms :], jnp.zeros((REACH, width), F32)],
        axis=0,
    )
    whole = pltpu.roll(whole, shift, 1).T[:head]
    own_out_ref[...] = whole[:, :atoms]
    rim_down = whole[:, atoms : atoms + REACH]
    rim_up = whole[:, atoms + REACH : atoms + 2 * REACH]
    rim_far = jnp.where(odd, rim_up, rim_down)
    rim_far_ref[...] = jnp.concatenate([rim_far[: head // 2], rim_far[head // 2 :]], axis=1)
    rim_near_ref[...] = jnp.where(odd, rim_down, rim_up).astype(BF16)
    for fill in fills:
        fill.wait()
    outs = []
    for part, (own_part, safe) in enumerate(own_thirds(seq, col, grad_pair_ref.shape[1])):
        copy = pltpu.make_async_copy(
            grad_band.at[:, pl.ds(part * SUB, SUB), :],
            grad_pair_ref.at[:, pl.ds(safe, SUB), :],
            out_sems.at[part],
        )
        outs.append((own_part, safe, copy))

        @pl.when(own_part)
        def _(copy=copy):
            copy.start()

    wait_all(outs)


def merge_kernel(first_ref, out_ref, *, plane, planes):
    step = first_ref.shape[0] // plane
    each = step // HEADS
    total = first_ref[:step, :]
    for i in range(1, plane):
        total = total + first_ref[i * step : (i + 1) * step, :]
    pieces = [total[c * each : (c + 1) * each - 1] for c in range(HEADS)]
    tail = total[each - 1 : each]
    for c in range(1, HEADS):
        tail = tail + total[(c + 1) * each - 1 : (c + 1) * each]
    joined = jnp.concatenate(pieces + [tail], axis=0)
    size = joined.shape[0]
    for z in range(planes):
        out_ref[z * size : (z + 1) * size, :] = joined


def final_kernel(
    gathered_ref,
    bias_ref,
    own_ref,
    near_ref,
    atoms_ref,
    gq_ref,
    gk_ref,
    gv_ref,
    go_ref,
    gb_ref,
    *,
    seqs,
    chunk,
):
    head, atoms = atoms_ref.shape
    seq = lax.axis_index("seq")
    odd = lax.rem(seq, 2) == 1
    rim_rows = head // 2
    rows = 2 * chunk + rim_rows
    plane = gathered_ref.shape[0] // rows
    partner = lax.rem(jnp.where(odd, seq + 1, seq - 1 + seqs), plane)
    far = gathered_ref[pl.ds(pl.multiple_of(partner * rows + 2 * chunk, 16), rim_rows), :].astype(F32)
    far = jnp.concatenate([far[:, :REACH], far[:, REACH:]], axis=0)
    far = jnp.where(jnp.where(odd, seq + 1, seq) % seqs == 0, 0.0, far)
    near = near_ref[...].astype(F32)
    below, above = jnp.where(odd, near, far), jnp.where(odd, far, near)
    middle = jnp.zeros((head, atoms - 2 * REACH), F32)
    atoms_ref[...] = (own_ref[...] + jnp.concatenate([below, middle, above], axis=1)).astype(BF16)
    terms = [gathered_ref[p * rows : p * rows + 2 * chunk, :].astype(F32) for p in range(plane)]
    main = jnp.concatenate([x[:chunk] + x[chunk:] for x in terms], axis=0)
    for i, ref in enumerate((gq_ref, gk_ref, gv_ref, go_ref)):
        ref[...] = main[i * head : (i + 1) * head]
    gb_ref[...] = bias_ref[...]


def vmem():
    return pl.BlockSpec(memory_space=pltpu.VMEM)


def smem():
    return pl.BlockSpec(memory_space=pltpu.SMEM)


def in_hbm():
    return pl.BlockSpec(memory_space=pltpu.MemorySpace.HBM)


def shape(dims, dtype):
    return jax.ShapeDtypeStruct(dims, dtype)


def params(mebibytes):
    return pltpu.CompilerParams(vmem_limit_bytes=mebibytes * 1024 * 1024)


def per_device(
    atom_inputs,
    atom_token,
    counts,
    window_start,
    pair_features,
    w_query,
    w_key,
    w_value,
    w_out,
    w_bias,
    atom_cotangent,
    token_cotangent,
):
    atoms, width = atom_inputs.shape
    tokens, columns, _ = pair_features.shape
    head = w_query.shape[1]
    seqs = lax.axis_size("seq")
    plane = 16 if seqs % 16 == 0 else 4
    planes = seqs // plane
    cols = lax.axis_size("col")
    seq = lax.axis_index("seq")
    odd = seq % 2 == 1
    token_row = atom_token[None, :]

    near = [(i, i ^ 1) for i in range(seqs)]
    far_groups = [
        [n * cols + c for n in (i, (i + 1) % seqs) for c in range(cols)] for i in range(1, seqs, 2)
    ]
    w_bias_t = w_bias.T
    weights = (w_query.T, w_key.T, w_value.T, w_out)
    pack, near_edge = pl.pallas_call(
        pack_kernel,
        out_shape=(
            shape((2 * HEADS, SAME_ROWS + 3 * SPARE, width), BF16),
            shape((REACH + 16 + NEAR_ROWS, width), BF16),
        ),
        in_specs=[in_hbm()] * 8,
        out_specs=(in_hbm(), in_hbm()),
        scratch_shapes=[
            pltpu.VMEM((tokens, BAND, width), BF16),
            pltpu.VMEM((width, width), BF16),
            pltpu.VMEM((REACH // 2, width), BF16),
            pltpu.VMEM((tokens * HEADS, width), F32),
            pltpu.VMEM(w_bias_t.shape, BF16),
            pltpu.VMEM(token_row.shape, jnp.int32),
            pltpu.VMEM((REACH + 16 + NEAR_ROWS, width), BF16),
            pltpu.VMEM((3, SAME_ROWS + 3 * SPARE, width), BF16),
            pltpu.SemaphoreType.DMA((3,)),
            pltpu.SemaphoreType.DMA((8,)),
            pltpu.SemaphoreType.DMA((2 * HEADS + 1,)),
        ],
        compiler_params=params(60),
        name="pack",
    )(
        pair_features,
        *weights,
        atom_inputs,
        w_bias_t,
        token_row,
    )
    near_heads = [(i * cols + c, (i ^ 1) * cols + (c ^ 1)) for i in range(seqs) for c in range(cols)]
    near_edge = lax.ppermute(near_edge, ("seq", "col"), near_heads)
    recv = lax.all_to_all(
        pack, ("seq", "col"), 0, 0, tiled=True, axis_index_groups=far_groups
    )

    chunk = width // plane
    share = chunk // HEADS
    pay, *parts = pl.pallas_call(
        functools.partial(attention_kernel, seqs=seqs, plane=plane),
        out_shape=(
            shape((plane * HEADS * (share + 1), width), F32),
            shape((atoms, width), F32),
            shape((atoms + 2 * REACH, width), F32),
            shape((atoms + 2 * REACH, width), F32),
            shape((atoms, width), BF16),
            shape((tokens * HEADS, width), F32),
        )
        + (shape((width, width), BF16),) * 3,
        in_specs=[smem(), in_hbm()] + [vmem()] * 12,
        out_specs=(vmem(),) * 9,
        scratch_shapes=[
            pltpu.VMEM((tokens, BAND, width), BF16),
            pltpu.VMEM((HEADS * width, width), F32),
            pltpu.SemaphoreType.DMA((3,)),
        ],
        compiler_params=params(32),
        name="attention",
    )(
        window_start,
        pair_features,
        recv,
        near_edge,
        atom_inputs,
        token_row,
        atom_token[:, None],
        counts[None, :],
        atom_cotangent,
        token_cotangent,
        *weights,
    )
    rim_far, rim_near, own_part, grad_pair = pl.pallas_call(
        turned_kernel,
        out_shape=(
            shape((head // 2, width), F32),
            shape((head, REACH), BF16),
            shape((head, atoms), F32),
            shape(pair_features.shape, BF16),
        ),
        in_specs=[vmem()] * 9,
        out_specs=(vmem(), vmem(), vmem(), in_hbm()),
        scratch_shapes=[
            pltpu.VMEM((columns, width), BF16),
            pltpu.VMEM((tokens, 3 * SUB, width), BF16),
            pltpu.SemaphoreType.DMA((tokens,)),
            pltpu.SemaphoreType.DMA((3,)),
        ],
        compiler_params=params(32),
        name="turned",
    )(w_bias_t, *parts)

    whole_planes = [
        [(z * plane + i) * cols + c for i in range(plane) for c in range(cols)]
        for z in range(planes)
    ]
    across = [[z * plane + i for z in range(planes)] for i in range(plane)]
    within = [
        [(z + 1) * plane % seqs] + [z * plane + i for i in range(1, plane)] for z in range(planes)
    ]
    first = lax.all_to_all(
        pay.reshape(plane * HEADS, 1, (share + 1) * width), ("seq", "col"), 0, 0, tiled=True, axis_index_groups=whole_planes
    )
    size = chunk + 1
    joined = pl.pallas_call(
        functools.partial(merge_kernel, plane=plane, planes=planes),
        out_shape=shape((planes * size, width), F32),
        in_specs=[vmem()],
        out_specs=vmem(),
        compiler_params=params(16),
        name="merge",
    )(first.reshape(plane * HEADS * (share + 1), width))
    joined, rim_near = lax.optimization_barrier((joined, rim_near))
    rim_near = lax.ppermute(rim_near, "seq", near)
    second = lax.all_to_all(
        joined.reshape(planes, 1, size * width),
        "seq",
        0,
        0,
        tiled=True,
        axis_index_groups=across,
    ).sum(axis=0)
    partner = jnp.where(odd, seq + 1, seq - 1 + seqs) % plane
    positions = lax.broadcasted_iota(jnp.int32, (plane, 1, 1), 0)
    sums = second[:, : chunk * width].reshape(1, chunk, width)
    leading = lax.reduce_precision(sums, 8, 7)
    sums = jnp.concatenate([leading, sums - leading], axis=1)
    gathered = jnp.concatenate(
        [
            jnp.broadcast_to(sums, (plane, 2 * chunk, width)),
            jnp.where(positions == partner, rim_far[None], 0.0),
        ],
        axis=1,
    )
    gathered = gathered.astype(BF16).reshape(plane * (2 * chunk + head // 2), width)
    third = lax.all_to_all(gathered, "seq", 0, 0, tiled=True, axis_index_groups=within)
    grad_atoms, gq, gk, gv, go, gb = pl.pallas_call(
        functools.partial(final_kernel, seqs=seqs, chunk=chunk),
        out_shape=(
            shape((head, atoms), BF16),
            shape((head, width), F32),
            shape((head, width), F32),
            shape((head, width), F32),
            shape((head, width), F32),
            shape((1, width), F32),
        ),
        in_specs=[vmem()] * 4,
        out_specs=(vmem(),) * 6,
        compiler_params=params(16),
        name="final",
    )(
        third,
        second[:, chunk * width :],
        own_part,
        rim_near,
    )
    return (grad_atoms.T, grad_pair, gq.T, gk.T, gv.T, go, gb.T)


def solution(mesh):
    placed = (
        P("seq", None),
        P("seq"),
        P("seq"),
        P("seq"),
        P("seq", "col", None),
        P(None, "col"),
        P(None, "col"),
        P(None, "col"),
        P("col", None),
        P(),
        P("seq", None),
        P("seq", None),
    )
    return jax.shard_map(
        per_device,
        mesh=mesh,
        in_specs=placed,
        out_specs=(
            P("seq", "col"),
            P("seq", "col", None),
            P(None, "col"),
            P(None, "col"),
            P(None, "col"),
            P("col", None),
            P(None, "col"),
        ),
        check_vma=False,
    )
```
